32 devices in a mesh: req: 2 (over y), ctx: 16 (over z, x, core).
Axes of the slice: x: 2, y: 2, z: 4, core: 2. Of those that a mesh axis runs over, the one named last changes fastest.
Arguments:
- query_source: bfloat16 [2304, 256], P(('req', 'ctx')), parts along dimension 0, may hold values from -32 to 32
- key_source: bfloat16 [2304, 256], P(('req', 'ctx')), parts along dimension 0, may hold values from -4 to 4
- query_edit: bfloat16 [2304, 256], P(('req', 'ctx')), parts along dimension 0, may hold values from -32 to 32
- key_edit: bfloat16 [2304, 256], P(('req', 'ctx')), parts along dimension 0, may hold values from -4 to 4
- text_count: int32 [2], P('req'), parts along dimension 0, may hold values from 72 to 288, as said below
Outputs:
- query_grad: float32 [2304, 256], P(('req', 'ctx')), parts along dimension 0
- key_grad: float32 [2304, 256], P(('req', 'ctx')), parts along dimension 0
The draws below stay inside these ranges and needn't reach their ends.
There are 2 independent parts, one for each index of `req`. The reference program is written for one: setup_inputs(seed, part) draws one part's arguments, and reference() takes and returns one part's arrays. A program takes and returns all parts, laid end to end along the dimension named above; each array names one. Nothing has to cross between parts.
Inputs may be any that keep to these rules, and one draw needn't show every extreme that they name: The first 288 positions are text slots; those at or past text_count are padding.
All inputs are finite; a program needn't handle non-finite values.
Results may differ from the reference program's by a relative error of at most 0.0095.
Values may be sent and summed in bfloat16 or wider, within the bound.
A program may use at most 64 MiB of HBM per device.

```python
import math
import jax
import jax.numpy as jnp
from jax import lax

HEADS = 2
HEAD_DIM = 128
TOKENS = 1152
TEXT = 288


def draw_pair(key, offset_salt):
    base_key = jax.random.fold_in(key, offset_salt)
    first_key, second_key = jax.random.split(base_key)
    full_shape = (TOKENS, HEADS, HEAD_DIM)
    keys_all = jnp.clip(jax.random.normal(first_key, full_shape, jnp.float32), -4.0, 4.0)
    queries = jnp.clip(jax.random.normal(second_key, full_shape, jnp.float32), -4.0, 4.0)
    return (queries.reshape(TOKENS, HEADS * HEAD_DIM), keys_all.reshape(TOKENS, HEADS * HEAD_DIM))


def draw_query_source(key, part):
    return draw_pair(key, 101)[0].astype(jnp.bfloat16)


def draw_key_source(key, part):
    return draw_pair(key, 101)[1].astype(jnp.bfloat16)


def draw_query_edit(key, part):
    return draw_pair(key, 202)[0].astype(jnp.bfloat16)


def draw_key_edit(key, part):
    return draw_pair(key, 202)[1].astype(jnp.bfloat16)


def draw_text_count(key, part):
    lowest = TEXT // 4
    picked = jax.random.randint(jax.random.fold_in(key, 303), (1,), lowest, TEXT, jnp.int32)
    parity = jnp.asarray(part, jnp.int32) % 2
    return jnp.where(parity == 1, jnp.full((1,), TEXT, jnp.int32), picked).astype(jnp.int32)


def setup_inputs(seed: int = 0, part: int = 0) -> dict:
    splits = jax.random.split(jax.random.key(seed), 6)
    part_keys = jax.random.split(jax.random.fold_in(splits[5], part), 6)
    return {
        "query_source": draw_query_source(jax.random.fold_in(jax.random.fold_in(splits[5], part), 71), part),
        "key_source": draw_key_source(jax.random.fold_in(jax.random.fold_in(splits[5], part), 71), part),
        "query_edit": draw_query_edit(jax.random.fold_in(jax.random.fold_in(splits[5], part), 71), part),
        "key_edit": draw_key_edit(jax.random.fold_in(jax.random.fold_in(splits[5], part), 71), part),
        "text_count": draw_text_count(jax.random.fold_in(jax.random.fold_in(splits[5], part), 71), part),
    }


def masked_probs(scores, key_valid):
    masked = jnp.where(key_valid, scores, -jnp.inf)
    highest = lax.optimization_barrier(jnp.max(masked, axis=-1, keepdims=True))
    powers = jnp.where(key_valid, jnp.exp(scores - highest), 0.0)
    return powers / lax.optimization_barrier(jnp.sum(powers, axis=-1, keepdims=True))

def reference(query_source, key_source, query_edit, key_edit, text_count):
    score_scale = 1.0 / math.sqrt(HEAD_DIM)
    weight = 4.0 * TOKENS * math.sqrt(TOKENS)
    places = jnp.arange(TOKENS)
    token_valid = (places >= TEXT) | (places < text_count[0])
    row_weight = token_valid.astype(jnp.float32)
    block_rows = TOKENS // 8

    def split_heads(matrix):
        return matrix.reshape(TOKENS, HEADS, HEAD_DIM).transpose(1, 0, 2)

    def per_head(inputs):
        head_qs, head_ks, head_qe, head_ke = inputs
        blocks_qs = head_qs.reshape(8, block_rows, HEAD_DIM)
        blocks_qe = head_qe.reshape(8, block_rows, HEAD_DIM)
        blocks_weight = row_weight.reshape(8, block_rows, 1)

        def per_block(carry, block):
            block_qs, block_qe, block_weight = block
            scores_source = jnp.dot(block_qs, head_ks.T, preferred_element_type=jnp.float32) * score_scale
            scores_edit = jnp.dot(block_qe, head_ke.T, preferred_element_type=jnp.float32) * score_scale
            probs_source = masked_probs(scores_source, token_valid[None, :])
            probs_edit = masked_probs(scores_edit, token_valid[None, :])
            map_grad = 2.0 * weight * (probs_edit - probs_source) * block_weight
            row_delta = lax.optimization_barrier(jnp.sum(map_grad * probs_edit, axis=1, keepdims=True))
            score_grad = (probs_edit * (map_grad - row_delta)).astype(jnp.bfloat16)
            block_qgrad = jnp.dot(score_grad, head_ke, preferred_element_type=jnp.float32) * score_scale
            block_kgrad = jnp.dot(score_grad.T, block_qe, preferred_element_type=jnp.float32) * score_scale
            return (carry + block_kgrad, block_qgrad)
        start_grad = jnp.zeros((TOKENS, HEAD_DIM), jnp.float32)
        head_kgrad, head_qgrad = lax.scan(per_block, start_grad, (blocks_qs, blocks_qe, blocks_weight))
        return (head_qgrad.reshape(TOKENS, HEAD_DIM), head_kgrad)
    query_grads, key_grads = lax.map(per_head, (split_heads(query_source), split_heads(key_source), split_heads(query_edit), split_heads(key_edit)))
    query_grad = query_grads.transpose(1, 0, 2).reshape(TOKENS, HEADS * HEAD_DIM)
    key_grad = key_grads.transpose(1, 0, 2).reshape(TOKENS, HEADS * HEAD_DIM)
    return (query_grad, key_grad)
```

```python
import functools
import math

import jax
import jax.numpy as jnp
from jax import lax
from jax.experimental import pallas as pl
from jax.experimental.pallas import tpu as pltpu
from jax.sharding import PartitionSpec as P

HEAD_DIM = 128
MASKED = -1e30
F32 = jnp.float32
BF16 = jnp.bfloat16


def kernel(
    chips,
    count_hbm, qs_hbm, ks_hbm, qe_hbm, ke_hbm,
    qg_ref, kg_ref,
    count_ref, krecv, kother, qrecv, qother, qcat, kturn, e_buf, s_buf, stats_ref, st_send, st_recv,
    kg_send, kg_recv, qg_send, qg_recv, qg_own, kg_own,
    load_sem, ksend_sem, near_sem, krecv_sem, qrecv_sem, st_sems,
    kgsend_sem, gnear_sem, kgrecv_sem, qgrecv_sem,
):
    members = chips // 2
    rows = krecv.shape[3]
    pair_rows = 2 * rows
    width = 2 * pair_rows
    head = pair_rows // 128 * 128
    tail = pair_rows - head
    groups = pair_rows // 8
    all_rows = rows * chips * 2
    text_slots = min(512, all_rows // 4)
    scale = 1.0 / math.sqrt(HEAD_DIM)
    power_scale = scale * math.log2(math.e)
    weight = 4.0 * all_rows * math.sqrt(all_rows)
    me = lax.axis_index("ctx")
    chip, core = me // 2, me % 2
    other = 1 - core
    group, member = chip // members, chip % members

    def chip_of(g, m):
        return g * members + m

    def dev(g, m, c):
        return {"ctx": chip_of(g, m) * 2 + c}

    def shifted(d):
        if members % 2:
            return (member + d) % members
        return (member // 2 + d // 2) % (members // 2) * 2 + (member + d) % 2

    def sender(d):
        if members % 2:
            return (member + members - d) % members
        return (member // 2 + members - d // 2) % (members // 2) * 2 + (member + d) % 2

    def each(n, body, init):
        if n <= 8:
            for i in range(n):
                init = body(i, init)
            return init
        return lax.fori_loop(0, n, body, init)

    def wait(ref, sem):
        pltpu.make_async_copy(ref, ref, sem).wait()

    own_cols = pl.ds(pl.multiple_of(core * HEAD_DIM, HEAD_DIM), HEAD_DIM)
    other_cols = pl.ds(pl.multiple_of(other * HEAD_DIM, HEAD_DIM), HEAD_DIM)
    loads = []
    for i, (src, dst_own, dst_other) in enumerate((
        (qs_hbm, qrecv.at[0, core, 0], qother.at[0]),
        (qe_hbm, qrecv.at[0, core, 1], qother.at[1]),
        (ks_hbm, krecv.at[member, core, 0], kother.at[0]),
        (ke_hbm, krecv.at[member, core, 1], kother.at[1]),
    )):
        loads.append(pltpu.make_async_copy(src.at[:, own_cols], dst_own, load_sem.at[0]))
        loads.append(pltpu.make_async_copy(src.at[:, other_cols], dst_other, load_sem.at[0]))
    count_load = pltpu.make_async_copy(count_hbm, count_ref, load_sem.at[1])
    for load in loads:
        load.start()
    count_load.start()

    barrier = pltpu.get_barrier_semaphore()

    def greet(d, carry):
        for c in (0, 1):
            pl.semaphore_signal(barrier, inc=1, device_id=dev(group, shifted(d + 1), c))
        return carry

    for c in (0, 1):
        pl.semaphore_signal(barrier, inc=1, device_id=dev(1 - group, member, c))
    pl.semaphore_signal(barrier, inc=1, device_id=dev(group, member, other))
    each(members - 1, greet, 0)
    pl.semaphore_wait(barrier, 2 * members + 1)
    wait(krecv.at[0:2], load_sem.at[0])
    count_load.wait()

    def key_copy(m, c, same, sem):
        return pltpu.make_async_remote_copy(
            src_ref=krecv.at[member, core] if same else kother,
            dst_ref=krecv.at[member, core],
            send_sem=sem,
            recv_sem=krecv_sem.at[member],
            device_id=dev(group, m, c),
        )

    def query_copy(r, c, same):
        return pltpu.make_async_remote_copy(
            src_ref=qrecv.at[0, core] if same else qother,
            dst_ref=qrecv.at[r, core],
            send_sem=near_sem.at[0],
            recv_sem=qrecv_sem.at[r],
            device_id=dev(1 - group if r else group, member, c),
        )

    query_copy(1, core, True).start()
    query_copy(1, other, False).start()

    def send_keys(d, carry):
        m = shifted(members - 1 - d)
        key_copy(m, core, True, ksend_sem.at[0]).start()
        key_copy(m, other, False, ksend_sem.at[0]).start()
        return carry

    send_keys(0, 0)
    query_copy(0, other, False).start()
    key_copy(member, other, False, near_sem.at[0]).start()
    if members > 2:
        each(members - 2, lambda d, carry: send_keys(d + 1, carry), 0)

    count = count_ref[0]

    def valid(positions):
        return (positions >= text_slots) | (positions < count)

    lane = lax.broadcasted_iota(jnp.int32, (1, width), 1)
    in_tail = lane >= 2 * head
    spot = jnp.where(in_tail, lane - 2 * head, lane)
    half = jnp.where(in_tail, tail, head)
    far = spot >= half
    spot = jnp.where(far, spot - half, spot) + jnp.where(in_tail, head, 0)
    row_place = jnp.where(far, chip_of(1 - group, member), chip) * pair_rows + spot
    row_weight = jnp.where(valid(row_place), 2.0 * weight, 0.0)

    def place_queries(r):
        for which in (0, 1):
            joined = jnp.concatenate([qrecv[r, c, which].astype(F32) for c in (0, 1)], axis=0)
            joined = joined.astype(BF16)
            qcat[which, r * head:(r + 1) * head] = joined[:head]
            if tail:
                at = 2 * head + r * tail
                qcat[which, at:at + tail] = joined[head:]

    def powers(m, which, lanes, key_valid, buf):
        span = lanes.stop - lanes.start
        q = qcat[which, lanes]
        scores = jnp.concatenate([
            lax.dot_general(
                krecv[m, c, which], q, (((1,), (1,)), ((), ())), preferred_element_type=F32
            ) for c in (0, 1)
        ], axis=0)
        scores = jnp.where(key_valid, scores, MASKED).reshape(groups, 8, span)
        top = jnp.max(scores, axis=0)
        power = jnp.exp2((scores - top[None]) * power_scale)
        return top, power

    def score_chunk(d, m, lanes):
        place = chip_of(group, m) * pair_rows + lax.broadcasted_iota(jnp.int32, (pair_rows, 1), 0)
        key_valid = valid(place)
        m_s, s_pow = powers(m, 0, lanes, key_valid, s_buf)
        m_e, e_pow = powers(m, 1, lanes, key_valid, e_buf)
        s_buf[d, :, :, lanes] = s_pow
        e_buf[d, :, :, lanes] = e_pow
        for i, value in enumerate((
            m_e, jnp.sum(e_pow, axis=0), m_s, jnp.sum(s_pow, axis=0),
            jnp.sum(e_pow * e_pow, axis=0), jnp.sum(e_pow * s_pow, axis=0),
        )):
            stats_ref[i, d, :, lanes] = value

    early, late, full = slice(0, head), slice(head, width), slice(0, width)
    wait(qrecv.at[0, 0], qrecv_sem.at[0])
    wait(krecv.at[member, 0], krecv_sem.at[member])
    place_queries(0)
    ahead = 2 if members == 4 else 1
    for d in range(ahead):
        m = shifted(d) if d else member
        if d:
            wait(krecv.at[m], krecv_sem.at[m])
        if head:
            score_chunk(d, m, early)
    wait(qrecv.at[1], qrecv_sem.at[1])
    place_queries(1)
    for d in range(ahead):
        score_chunk(d, shifted(d) if d else member, late)

    def far_scores(d, carry):
        d = members - 1 - d
        m = sender(d)
        wait(krecv.at[m], krecv_sem.at[m])
        score_chunk(d, m, full)
        return carry

    each(members - ahead, far_scores, 0)

    def fold(op, value):
        return op(op(value, axis=0), axis=0, keepdims=True)

    tops_e, tops_s = stats_ref[0], stats_ref[2]
    m_e, m_s = fold(jnp.max, tops_e), fold(jnp.max, tops_s)
    f_e = jnp.exp2((tops_e - m_e) * power_scale)
    f_s = jnp.exp2((tops_s - m_s) * power_scale)
    stats = (
        m_e, fold(jnp.sum, stats_ref[1] * f_e),
        m_s, fold(jnp.sum, stats_ref[3] * f_s),
        fold(jnp.sum, stats_ref[4] * (f_e * f_e)),
        fold(jnp.sum, stats_ref[5] * (f_e * f_s)),
    )
    packed = jnp.concatenate(stats + (jnp.zeros((2, width), F32),), axis=0)
    st_send[:, :head] = packed[:, head:2 * head]
    st_send[:, head:2 * head] = packed[:, :head]
    if tail:
        st_send[:, 2 * head:] = jnp.concatenate(
            [packed[:, 2 * head + tail:], packed[:, 2 * head:2 * head + tail]], axis=1
        )
    stat_copy = pltpu.make_async_remote_copy(
        src_ref=st_send, dst_ref=st_recv, send_sem=st_sems.at[0], recv_sem=st_sems.at[1],
        device_id=dev(1 - group, member, core),
    )
    stat_copy.start()

    def turn_keys(d, carry):
        m = sender(d)
        joined = jnp.concatenate([krecv[m, c, 1].astype(F32) for c in (0, 1)], axis=0)
        kturn[d] = joined.T.astype(BF16)
        return carry

    each(members, turn_keys, 0)

    stat_copy.wait_recv()
    m_e1, l_e1, m_s1, l_s1, sq1, cr1 = stats
    m_e2, l_e2, m_s2, l_s2, sq2, cr2 = (st_recv[i:i + 1] for i in range(6))
    m_e, m_s = jnp.maximum(m_e1, m_e2), jnp.maximum(m_s1, m_s2)
    fe1, fe2 = jnp.exp2((m_e1 - m_e) * power_scale), jnp.exp2((m_e2 - m_e) * power_scale)
    fs1, fs2 = jnp.exp2((m_s1 - m_s) * power_scale), jnp.exp2((m_s2 - m_s) * power_scale)
    inv_e = 1.0 / (l_e1 * fe1 + l_e2 * fe2)
    inv_s = 1.0 / (l_s1 * fs1 + l_s2 * fs2)
    sq = sq1 * fe1 * fe1 + sq2 * fe2 * fe2
    cr = cr1 * fe1 * fs1 + cr2 * fe2 * fs2
    stats_ref[1] = f_e * (fe1 * inv_e)
    stats_ref[3] = f_s * (fs1 * inv_s)
    delta = row_weight * (sq * inv_e * inv_e - cr * inv_e * inv_s)

    def kg_copy(m, c, sem):
        return pltpu.make_async_remote_copy(
            src_ref=kg_send.at[m, c], dst_ref=kg_recv.at[member, core],
            send_sem=sem, recv_sem=kgrecv_sem.at[member],
            device_id=dev(group, m, c),
        )

    def qg_copy(r, c):
        return pltpu.make_async_remote_copy(
            src_ref=qg_send.at[r, c], dst_ref=qg_recv.at[r, core],
            send_sem=gnear_sem.at[0], recv_sem=qgrecv_sem.at[r],
            device_id=dev(1 - group if r else group, member, c),
        )

    q_edit = qcat[1]

    def grad_chunk(d, q_total):
        prob_e = e_buf[d] * stats_ref[1, d][None]
        prob_s = s_buf[d] * stats_ref[3, d][None]
        grad = prob_e * (row_weight[None] * (prob_e - prob_s) - delta[None])
        grad = grad.reshape(pair_rows, width).astype(BF16)
        k_part = jnp.dot(grad, q_edit, preferred_element_type=F32) * scale
        q_part = jnp.dot(kturn[d], grad, preferred_element_type=F32)
        return k_part, q_total + q_part

    def far_grad(d, q_total):
        d = members - 1 - d
        m = sender(d)
        k_part, q_total = grad_chunk(d, q_total)
        for c in (0, 1):
            kg_send[m, c] = k_part[c * rows:(c + 1) * rows].astype(BF16)
        for c in (core, other):
            kg_copy(m, c, kgsend_sem.at[0]).start()
        return q_total

    q_total = each(members - 1, far_grad, jnp.zeros((HEAD_DIM, width), F32))
    k_part, q_total = grad_chunk(0, q_total)
    for c in (0, 1):
        kg_own[c] = k_part[c * rows:(c + 1) * rows]
        kg_send[member, c] = k_part[c * rows:(c + 1) * rows].astype(BF16)

    q_rows = q_total.T * scale
    for r in (1, 0):
        joined = [q_rows[r * head:(r + 1) * head]]
        if tail:
            at = 2 * head + r * tail
            joined.append(q_rows[at:at + tail])
        joined = jnp.concatenate(joined, axis=0)
        for c in (0, 1):
            part = joined[c * rows:(c + 1) * rows]
            if not r:
                qg_own[c] = part
            qg_send[r, c] = part.astype(BF16)
        if r:
            qg_copy(1, core).start()
            qg_copy(1, other).start()
    qg_copy(0, other).start()
    kg_copy(member, other, gnear_sem.at[0]).start()

    def put(ref, mine, theirs):
        ref[:, own_cols] = mine
        ref[:, other_cols] = theirs

    wait(kg_recv.at[member, 0], kgrecv_sem.at[member])

    def add_far(d, sums):
        mine, theirs = sums
        m = shifted(d + 1)
        wait(kg_recv.at[m], kgrecv_sem.at[m])
        return mine + kg_recv[m, core].astype(F32), theirs + kg_recv[m, other].astype(F32)

    sums = each(members - 1, add_far, (kg_own[core], kg_recv[member, other].astype(F32)))
    put(kg_ref, *sums)

    wait(qg_recv.at[0, 0], qgrecv_sem.at[0])
    wait(qg_recv.at[1], qgrecv_sem.at[1])
    put(
        qg_ref,
        qg_own[core] + qg_recv[1, core].astype(F32),
        qg_recv[0, other].astype(F32) + qg_recv[1, other].astype(F32),
    )

    wait(krecv.at[0:members - 1], ksend_sem.at[0])
    wait(qrecv, near_sem.at[0])
    stat_copy.wait_send()
    wait(kg_send.at[0:members - 1], kgsend_sem.at[0])
    wait(qg_send, gnear_sem.at[0])


def put_out(qg_vmem, kg_vmem, qg_hbm, kg_hbm, sems):
    copies = (
        pltpu.make_async_copy(qg_vmem, qg_hbm, sems.at[0]),
        pltpu.make_async_copy(kg_vmem, kg_hbm, sems.at[1]),
    )
    for copy in copies:
        copy.start()
    for copy in copies:
        copy.wait()


def solution(mesh):
    chips = mesh.shape["ctx"] // 2
    members = chips // 2

    def local(query_source, key_source, query_edit, key_edit, text_count):
        rows, full = query_source.shape
        width = 4 * rows
        groups = 2 * rows // 8
        dma = pltpu.SemaphoreType.DMA
        vmem = pltpu.VMEM
        grads = pl.pallas_call(
            functools.partial(kernel, chips),
            out_shape=(
                pltpu.VMEM((rows, full), F32),
                pltpu.VMEM((rows, full), F32),
            ),
            in_specs=[pl.BlockSpec(memory_space=pltpu.HBM)] * 5,
            out_specs=(pl.BlockSpec(memory_space=pltpu.VMEM),) * 2,
            scratch_shapes=[
                pltpu.SMEM((1,), jnp.int32),
                vmem((members, 2, 2, rows, HEAD_DIM), BF16),
                vmem((2, rows, HEAD_DIM), BF16),
                vmem((2, 2, 2, rows, HEAD_DIM), BF16),
                vmem((2, rows, HEAD_DIM), BF16),
                vmem((2, width, HEAD_DIM), BF16),
                vmem((members, HEAD_DIM, 2 * rows), BF16),
                vmem((members, groups, 8, width), F32),
                vmem((members, groups, 8, width), F32),
                vmem((6, members, 8, width), F32),
                vmem((8, width), F32),
                vmem((8, width), F32),
                vmem((members, 2, rows, HEAD_DIM), BF16),
                vmem((members, 2, rows, HEAD_DIM), BF16),
                vmem((2, 2, rows, HEAD_DIM), BF16),
                vmem((2, 2, rows, HEAD_DIM), BF16),
                vmem((2, rows, HEAD_DIM), F32),
                vmem((2, rows, HEAD_DIM), F32),
                dma((2,)),
                dma((1,)),
                dma((1,)),
                dma((members,)),
                dma((2,)),
                dma((2,)),
                dma((1,)),
                dma((1,)),
                dma((members,)),
                dma((2,)),
            ],
            compiler_params=pltpu.CompilerParams(collective_id=0, has_side_effects=True),
        )(text_count, query_source, key_source, query_edit, key_edit)
        return pl.pallas_call(
            put_out,
            out_shape=(pltpu.HBM((rows, full), F32),) * 2,
            in_specs=[pl.BlockSpec(memory_space=pltpu.VMEM)] * 2,
            out_specs=(pl.BlockSpec(memory_space=pltpu.HBM),) * 2,
            scratch_shapes=[dma((2,))],
        )(*(pltpu.with_memory_space_constraint(g, pltpu.VMEM) for g in grads))

    spec = P(("req", "ctx"), None)
    return jax.shard_map(
        local, mesh=mesh, in_specs=(spec,) * 4 + (P("req"),), out_specs=(spec, spec), check_vma=False
    )
```

```python
import functools
import math

import jax
import jax.numpy as jnp
from jax import lax
from jax.experimental import pallas as pl
from jax.experimental.pallas import tpu as pltpu
from jax.sharding import PartitionSpec as P

HEAD_DIM = 128
MASKED = -1e30
F32 = jnp.float32
BF16 = jnp.bfloat16


def split(positions):
    members = 1
    while members * members * 4 <= positions:
        members *= 2
    while positions % members:
        members //= 2
    return members, positions // members


def kernel(
    positions,
    count_hbm, qs_hbm, ks_hbm, qe_hbm, ke_hbm,
    qg_ref, kg_ref,
    count_ref, krecv, kother, qrecv, qother, qcat, kturn, e_buf, s_buf, stats_ref, st_send, st_recv,
    kn_send, kn_recv, kg_part, kg_send, kg_recv, qg_send, qg_recv, qg_own,
    load_sem, far_sem, near_sem, kfar_sem, knear_sem, qrecv_sem, st_sems,
    kn_sem, knrecv_sem, kg_sems, qg_sems,
):
    q_span, k_span = split(positions)
    rows = krecv.shape[3]
    pair_rows = 2 * rows
    width = 2 * q_span * rows
    head = q_span * rows // 128 * 128
    groups = pair_rows // 8
    all_rows = rows * positions * 4
    text_slots = min(512, all_rows // 4)
    scale = 1.0 / math.sqrt(HEAD_DIM)
    power_scale = scale * math.log2(math.e)
    weight = 4.0 * all_rows * math.sqrt(all_rows)
    me = lax.axis_index("ctx")
    core, x, p = me % 2, me // 2 % 2, me // 4
    a, b = p % q_span, p // q_span

    def chip_of(b, a, x):
        return (b * q_span + a) * 2 + x

    def dev(b, a, x, c):
        return {"ctx": chip_of(b, a, x) * 2 + c}

    def flip(r):
        return 1 - x if isinstance(r, int) and r else x if isinstance(r, int) else (x + r) % 2

    def each(n, body, init):
        if n <= 8:
            for i in range(n):
                init = body(i, init)
            return init
        return lax.fori_loop(0, n, body, init)

    def far_first(span, i):
        return 1 - i % 2, span - 1 - i // 2

    def near_first(span, i):
        if span == 2:
            return ((0, 1), (1, 0), (1, 1))[i]
        return far_first(span, i)

    def wait(ref, sem):
        pltpu.make_async_copy(ref, ref, sem).wait()

    own_cols = pl.ds(pl.multiple_of(x * HEAD_DIM, HEAD_DIM), HEAD_DIM)
    other_cols = pl.ds(pl.multiple_of((1 - x) * HEAD_DIM, HEAD_DIM), HEAD_DIM)
    loads = []
    for src, dst_own, dst_other in (
        (ks_hbm, krecv.at[b, core, 0], kother.at[0]),
        (ke_hbm, krecv.at[b, core, 1], kother.at[1]),
        (qs_hbm, qrecv.at[a, 0], qother.at[0]),
        (qe_hbm, qrecv.at[a, 1], qother.at[1]),
    ):
        loads.append(pltpu.make_async_copy(src.at[:, own_cols], dst_own, load_sem.at[0]))
        loads.append(pltpu.make_async_copy(src.at[:, other_cols], dst_other, load_sem.at[0]))
    count_load = pltpu.make_async_copy(count_hbm, count_ref, load_sem.at[1])
    for load in loads:
        load.start()
    count_load.start()

    barrier = pltpu.get_barrier_semaphore()

    def greet_q(i, carry):
        r, d = far_first(q_span, i)
        pl.semaphore_signal(barrier, inc=1, device_id=dev(b, (a + d) % q_span, flip(r), core))
        return carry

    def greet_k(i, carry):
        r, d = far_first(k_span, i)
        pl.semaphore_signal(barrier, inc=1, device_id=dev((b + d) % k_span, a, flip(r), core))
        return carry

    each(2 * k_span - 2, greet_k, 0)
    each(2 * q_span - 1, greet_q, 0)
    pl.semaphore_signal(barrier, inc=1, device_id=dev(b, a, x, 1 - core))
    pl.semaphore_wait(barrier, 2 * k_span + 2 * q_span - 2)
    wait(krecv.at[0:2], load_sem.at[0])
    count_load.wait()

    def key_copy(r, d):
        return pltpu.make_async_remote_copy(
            src_ref=kother if isinstance(r, int) and r else krecv.at[b, core],
            dst_ref=krecv.at[r * k_span + b, core],
            send_sem=far_sem.at[0],
            recv_sem=kfar_sem.at[r * k_span + b],
            device_id=dev((b + d) % k_span, a, flip(r), core),
        )

    def query_copy(r, d):
        return pltpu.make_async_remote_copy(
            src_ref=qother if isinstance(r, int) and r else qrecv.at[a],
            dst_ref=qrecv.at[r * q_span + a],
            send_sem=far_sem.at[0],
            recv_sem=qrecv_sem.at[r],
            device_id=dev(b, (a + d) % q_span, flip(r), core),
        )

    def near_copy(s):
        return pltpu.make_async_remote_copy(
            src_ref=krecv.at[s, core],
            dst_ref=krecv.at[s, core],
            send_sem=near_sem.at[0],
            recv_sem=knear_sem.at[s],
            device_id=dev(b, a, x, 1 - core),
        )

    def fan_out(span, copy):
        def pair(i, carry):
            copy(1, span - 1 - i).start()
            copy(0, span - 1 - i).start()
            return carry

        each(span - 1, pair, 0)
        copy(1, 0).start()

    near_copy(b).start()
    fan_out(k_span, key_copy)
    fan_out(q_span, query_copy)

    count = count_ref[0]

    def valid(positions):
        return (positions >= text_slots) | (positions < count)

    lane = lax.broadcasted_iota(jnp.int32, (1, width), 1)
    lane_piece, lane_row = lane // rows, lane % rows
    lane_chip = chip_of(b, lane_piece % q_span, jnp.where(lane_piece < q_span, x, 1 - x))
    row_weight = jnp.where(valid((lane_chip * 2 + core) * rows + lane_row), 2.0 * weight, 0.0)

    def place_queries(r):
        at = r * q_span * rows
        for which in (0, 1):
            pieces = [qrecv[r * q_span + i, which].astype(F32) for i in range(q_span)]
            if r:
                pieces = ([qcat_tail[which]] if at > head else []) + pieces
            joined = jnp.concatenate(pieces, axis=0)
            start = head if r else 0
            stop = width if r else head
            if not r:
                qcat_tail.append(joined[head:])
            qcat[which, start:stop] = joined[:stop - start].astype(BF16)

    qcat_tail = []

    def powers(s, which, lanes, key_valid):
        q = qcat[which, lanes]
        scores = jnp.concatenate([
            lax.dot_general(
                krecv[s, c, which], q, (((1,), (1,)), ((), ())), preferred_element_type=F32
            ) for c in (0, 1)
        ], axis=0)
        scores = jnp.where(key_valid, scores, MASKED).reshape(groups, 8, lanes.stop - lanes.start)
        top = jnp.max(scores, axis=0)
        return top, jnp.exp2((scores - top[None]) * power_scale)

    def slot(r, d):
        return r * k_span + (b + d) % k_span

    def score_chunk(r, d, lanes):
        s = slot(r, d)
        place = chip_of((b + d) % k_span, a, flip(r)) * pair_rows
        key_valid = valid(place + lax.broadcasted_iota(jnp.int32, (pair_rows, 1), 0))
        m_s, s_pow = powers(s, 0, lanes, key_valid)
        m_e, e_pow = powers(s, 1, lanes, key_valid)
        s_buf[s, :, :, lanes] = s_pow
        e_buf[s, :, :, lanes] = e_pow
        for i, value in enumerate((
            m_e, jnp.sum(e_pow, axis=0), m_s, jnp.sum(s_pow, axis=0),
            jnp.sum(e_pow * e_pow, axis=0), jnp.sum(e_pow * s_pow, axis=0),
        )):
            stats_ref[i, s, :, lanes] = value

    early, late = slice(0, head), slice(head, width)

    def pass_on(i, carry):
        s = slot(*near_first(k_span, i))
        wait(krecv.at[s, core], kfar_sem.at[s])
        near_copy(s).start()
        return carry

    wait(krecv.at[b, 1 - core], knear_sem.at[b])
    each(2 * k_span - 1, pass_on, 0)
    wait(qrecv.at[0:q_span - 1], qrecv_sem.at[0])
    place_queries(0)
    if head:
        score_chunk(0, 0, early)

    def near_scores(i, carry):
        r, d = near_first(k_span, i)
        s = slot(r, d)
        wait(krecv.at[s, 1 - core], knear_sem.at[s])
        if head:
            score_chunk(r, d, early)
        return carry

    each(2 * k_span - 1, near_scores, 0)
    wait(qrecv.at[q_span:2 * q_span], qrecv_sem.at[1])
    place_queries(1)

    def late_scores(i, carry):
        score_chunk(*far_first(k_span, i), late)
        return carry

    each(2 * k_span - 1, late_scores, 0)
    score_chunk(0, 0, late)

    def fold(op, value):
        return op(op(value, axis=0), axis=0, keepdims=True)

    tops_e, tops_s = stats_ref[0], stats_ref[2]
    m_e, m_s = fold(jnp.max, tops_e), fold(jnp.max, tops_s)
    f_e = jnp.exp2((tops_e - m_e) * power_scale)
    f_s = jnp.exp2((tops_s - m_s) * power_scale)
    stats = (
        m_e, fold(jnp.sum, stats_ref[1] * f_e),
        m_s, fold(jnp.sum, stats_ref[3] * f_s),
        fold(jnp.sum, stats_ref[4] * (f_e * f_e)),
        fold(jnp.sum, stats_ref[5] * (f_e * f_s)),
    )
    for i, value in enumerate(stats):
        st_send[i:i + 1] = value
    for i in (6, 7):
        st_send[i:i + 1] = jnp.zeros((1, width), F32)

    def stat_copy(d):
        return pltpu.make_async_remote_copy(
            src_ref=st_send, dst_ref=st_recv.at[d - 1], send_sem=st_sems.at[0], recv_sem=st_sems.at[1],
            device_id=dev(b, (a + d) % q_span, x, core),
        )

    for d in range(1, q_span):
        stat_copy(d).start()
    stats_ref[1] = f_e
    stats_ref[3] = f_s

    def turn_keys(i, carry):
        joined = jnp.concatenate([krecv[i, c, 1].astype(F32) for c in (0, 1)], axis=0)
        kturn[i] = joined.T.astype(BF16)
        return carry

    each(2 * k_span, turn_keys, 0)

    wait(st_recv, st_sems.at[1])
    total = stats
    for d in range(q_span - 1):
        m_e1, l_e1, m_s1, l_s1, sq1, cr1 = total
        m_e2, l_e2, m_s2, l_s2, sq2, cr2 = (st_recv[d, i:i + 1] for i in range(6))
        m_e, m_s = jnp.maximum(m_e1, m_e2), jnp.maximum(m_s1, m_s2)
        fe1, fe2 = jnp.exp2((m_e1 - m_e) * power_scale), jnp.exp2((m_e2 - m_e) * power_scale)
        fs1, fs2 = jnp.exp2((m_s1 - m_s) * power_scale), jnp.exp2((m_s2 - m_s) * power_scale)
        total = (
            m_e, l_e1 * fe1 + l_e2 * fe2, m_s, l_s1 * fs1 + l_s2 * fs2,
            sq1 * fe1 * fe1 + sq2 * fe2 * fe2, cr1 * fe1 * fs1 + cr2 * fe2 * fs2,
        )
    m_e, l_e, m_s, l_s, sq, cr = total
    inv_e, inv_s = 1.0 / l_e, 1.0 / l_s
    to_e = jnp.exp2((stats[0] - m_e) * power_scale) * inv_e
    to_s = jnp.exp2((stats[2] - m_s) * power_scale) * inv_s
    delta = row_weight * (sq * inv_e * inv_e - cr * inv_e * inv_s)

    q_edit = qcat[1]

    def grad_chunk(s, q_total):
        prob_e = e_buf[s] * (stats_ref[1, s] * to_e)[None]
        prob_s = s_buf[s] * (stats_ref[3, s] * to_s)[None]
        grad = prob_e * (row_weight[None] * (prob_e - prob_s) - delta[None])
        grad = grad.reshape(pair_rows, width).astype(BF16)
        k_part = jnp.dot(grad, q_edit, preferred_element_type=F32) * scale
        q_part = jnp.dot(kturn[s], grad, preferred_element_type=F32)
        for c in (0, 1):
            part = k_part[c * rows:(c + 1) * rows]
            kg_part[s, c] = part
            kn_send[s, c] = part.astype(BF16)
        pltpu.make_async_remote_copy(
            src_ref=kn_send.at[s, 1 - core], dst_ref=kn_recv.at[s],
            send_sem=kn_sem.at[0], recv_sem=knrecv_sem.at[s],
            device_id=dev(b, a, x, 1 - core),
        ).start()
        return q_total + q_part

    q_total = each(
        2 * k_span - 1, lambda i, q: grad_chunk(slot(*far_first(k_span, i)), q),
        jnp.zeros((HEAD_DIM, width), F32),
    )
    q_total = grad_chunk(b, q_total)

    def kg_copy(r, d):
        return pltpu.make_async_remote_copy(
            src_ref=kg_send.at[slot(r, d)], dst_ref=kg_recv.at[r * k_span + b],
            send_sem=kg_sems.at[0], recv_sem=kg_sems.at[1],
            device_id=dev((b + d) % k_span, a, flip(r), core),
        )

    def qg_copy(r, d):
        return pltpu.make_async_remote_copy(
            src_ref=qg_send.at[r * q_span + (a + d) % q_span], dst_ref=qg_recv.at[r * q_span + a],
            send_sem=qg_sems.at[0], recv_sem=qg_sems.at[1],
            device_id=dev(b, (a + d) % q_span, flip(r), core),
        )

    q_rows = q_total.T * scale
    for i in range(2 * q_span):
        part = q_rows[i * rows:(i + 1) * rows]
        qg_send[i] = part.astype(BF16)
        if i < q_span:
            qg_own[i] = part
    fan_out(q_span, qg_copy)

    def joined_kg(s):
        wait(kn_recv.at[s], knrecv_sem.at[s])
        return kg_part[s, core] + kn_recv[s].astype(F32)

    def send_kg(i, carry):
        r, d = far_first(k_span, i)
        s = slot(r, d)
        kg_send[s] = joined_kg(s).astype(BF16)
        kg_copy(r, d).start()
        return carry

    each(2 * k_span - 1, send_kg, 0)
    kg_mine = joined_kg(b)

    def put(ref, mine, recv, span, at):
        others = [recv[(at + d) % span].astype(F32) for d in range(1, span)]
        theirs = [recv[span + i].astype(F32) for i in range(span)]
        ref[:, own_cols] = sum(others, mine)
        ref[:, other_cols] = sum(theirs[1:], theirs[0])

    wait(qg_recv.at[0:2 * q_span - 1], qg_sems.at[1])
    put(qg_ref, qg_own[a], qg_recv, q_span, a)
    wait(kg_recv.at[0:2 * k_span - 1], kg_sems.at[1])
    put(kg_ref, kg_mine, kg_recv, k_span, b)

    wait(krecv.at[0:q_span + k_span - 1], far_sem.at[0])
    wait(krecv.at[0:k_span], near_sem.at[0])
    wait(st_recv, st_sems.at[0])
    wait(kn_recv, kn_sem.at[0])
    wait(kg_send.at[0:2 * k_span - 1], kg_sems.at[0])
    wait(qg_send.at[0:2 * q_span - 1], qg_sems.at[0])


def put_out(qg_vmem, kg_vmem, qg_hbm, kg_hbm, sems):
    copies = (
        pltpu.make_async_copy(qg_vmem, qg_hbm, sems.at[0]),
        pltpu.make_async_copy(kg_vmem, kg_hbm, sems.at[1]),
    )
    for copy in copies:
        copy.start()
    for copy in copies:
        copy.wait()


def solution(mesh):
    positions = mesh.shape["ctx"] // 4
    q_span, k_span = split(positions)

    def local(query_source, key_source, query_edit, key_edit, text_count):
        rows, full = query_source.shape
        width = 2 * q_span * rows
        groups = 2 * rows // 8
        dma = pltpu.SemaphoreType.DMA
        vmem = pltpu.VMEM
        grads = pl.pallas_call(
            functools.partial(kernel, positions),
            out_shape=(
                pltpu.VMEM((rows, full), F32),
                pltpu.VMEM((rows, full), F32),
            ),
            in_specs=[pl.BlockSpec(memory_space=pltpu.HBM)] * 5,
            out_specs=(pl.BlockSpec(memory_space=pltpu.VMEM),) * 2,
            scratch_shapes=[
                pltpu.SMEM((1,), jnp.int32),
                vmem((2 * k_span, 2, 2, rows, HEAD_DIM), BF16),
                vmem((2, rows, HEAD_DIM), BF16),
                vmem((2 * q_span, 2, rows, HEAD_DIM), BF16),
                vmem((2, rows, HEAD_DIM), BF16),
                vmem((2, width, HEAD_DIM), BF16),
                vmem((2 * k_span, HEAD_DIM, 2 * rows), BF16),
                vmem((2 * k_span, groups, 8, width), F32),
                vmem((2 * k_span, groups, 8, width), F32),
                vmem((6, 2 * k_span, 8, width), F32),
                vmem((8, width), F32),
                vmem((q_span - 1, 8, width), F32),
                vmem((2 * k_span, 2, rows, HEAD_DIM), BF16),
                vmem((2 * k_span, rows, HEAD_DIM), BF16),
                vmem((2 * k_span, 2, rows, HEAD_DIM), F32),
                vmem((2 * k_span, rows, HEAD_DIM), BF16),
                vmem((2 * k_span, rows, HEAD_DIM), BF16),
                vmem((2 * q_span, rows, HEAD_DIM), BF16),
                vmem((2 * q_span, rows, HEAD_DIM), BF16),
                vmem((q_span, rows, HEAD_DIM), F32),
                dma((2,)),
                dma((1,)),
                dma((1,)),
                dma((2 * k_span,)),
                dma((2 * k_span,)),
                dma((2,)),
                dma((2,)),
                dma((1,)),
                dma((2 * k_span,)),
                dma((2,)),
                dma((2,)),
            ],
            compiler_params=pltpu.CompilerParams(collective_id=0, has_side_effects=True),
        )(text_count, query_source, key_source, query_edit, key_edit)
        return pl.pallas_call(
            put_out,
            out_shape=(pltpu.HBM((rows, full), F32),) * 2,
            in_specs=[pl.BlockSpec(memory_space=pltpu.VMEM)] * 2,
            out_specs=(pl.BlockSpec(memory_space=pltpu.HBM),) * 2,
            scratch_shapes=[dma((2,))],
        )(*(pltpu.with_memory_space_constraint(g, pltpu.VMEM) for g in grads))

    spec = P(("req", "ctx"), None)
    return jax.shard_map(
        local, mesh=mesh, in_specs=(spec,) * 4 + (P("req"),), out_specs=(spec, spec), check_vma=False
    )
```

```python
import functools
import math

import jax
import jax.numpy as jnp
from jax import lax
from jax.experimental import pallas as pl
from jax.experimental.pallas import tpu as pltpu
from jax.sharding import PartitionSpec as P

HEAD_DIM = 128
MASKED = -1e30
F32 = jnp.float32
BF16 = jnp.bfloat16


def kernel(
    chips,
    count_hbm, qs_hbm, ks_hbm, qe_hbm, ke_hbm,
    qg_ref, kg_ref,
    count_ref, krecv, kother, qrecv, qother, qcat, kturn, bias_ref, grad_buf, e_buf, s_buf, stats_ref,
    st_send, st_recv,
    kg_send, kg_recv, qg_send, qg_recv, qg_own, kg_own,
    load_sem, ksend_sem, near_sem, krecv_sem, qrecv_sem, st_sems,
    kgsend_sem, gnear_sem, kgrecv_sem, qgrecv_sem,
):
    members = chips // 2
    rows = kother.shape[1]
    pair_rows = 2 * rows
    width = 2 * pair_rows
    head = pair_rows // 128 * 128
    tail = pair_rows - head
    groups = pair_rows // 8
    all_rows = rows * chips * 2
    text_slots = min(512, all_rows // 4)
    scale = 1.0 / math.sqrt(HEAD_DIM)
    power_scale = scale * math.log2(math.e)
    weight = 4.0 * all_rows * math.sqrt(all_rows)
    me = lax.axis_index("ctx")
    chip, core = me // 2, me % 2
    other = 1 - core
    group, member = chip // members, chip % members

    def chip_of(g, m):
        return g * members + m

    def dev(g, m, c):
        return {"ctx": chip_of(g, m) * 2 + c}

    def shifted(d):
        if members % 2:
            return (member + d) % members
        return (member // 2 + d // 2) % (members // 2) * 2 + (member + d) % 2

    def sender(d):
        if members % 2:
            return (member + members - d) % members
        return (member // 2 + members - d // 2) % (members // 2) * 2 + (member + d) % 2

    def each(n, body, init):
        if n <= 8:
            for i in range(n):
                init = body(i, init)
            return init
        return lax.fori_loop(0, n, body, init)

    def wait(ref, sem):
        pltpu.make_async_copy(ref, ref, sem).wait()

    def keys(m, c):
        return krecv.at[m, :, pl.ds(pl.multiple_of(c * rows, 8), rows)]

    def chips_keys(m):
        return krecv.at[m, :, 0:pair_rows]

    own_cols = pl.ds(pl.multiple_of(core * HEAD_DIM, HEAD_DIM), HEAD_DIM)
    other_cols = pl.ds(pl.multiple_of(other * HEAD_DIM, HEAD_DIM), HEAD_DIM)
    loads = []
    for i, (src, dst_own, dst_other) in enumerate((
        (qs_hbm, qrecv.at[0, core, 0], qother.at[0]),
        (qe_hbm, qrecv.at[0, core, 1], qother.at[1]),
        (ks_hbm, keys(member, core).at[0], kother.at[0]),
        (ke_hbm, keys(member, core).at[1], kother.at[1]),
    )):
        loads.append(pltpu.make_async_copy(src.at[:, own_cols], dst_own, load_sem.at[0]))
        loads.append(pltpu.make_async_copy(src.at[:, other_cols], dst_other, load_sem.at[0]))
    count_load = pltpu.make_async_copy(count_hbm, count_ref, load_sem.at[1])
    for load in loads:
        load.start()
    count_load.start()

    barrier = pltpu.get_barrier_semaphore()

    def greet(d, carry):
        for c in (0, 1):
            pl.semaphore_signal(barrier, inc=1, device_id=dev(group, shifted(d + 1), c))
        return carry

    for c in (0, 1):
        pl.semaphore_signal(barrier, inc=1, device_id=dev(1 - group, member, c))
    pl.semaphore_signal(barrier, inc=1, device_id=dev(group, member, other))
    each(members - 1, greet, 0)
    pl.semaphore_wait(barrier, 2 * members + 1)
    wait(chips_keys(slice(0, 2)), load_sem.at[0])
    count_load.wait()

    def key_copy(m, c, same, sem):
        return pltpu.make_async_remote_copy(
            src_ref=keys(member, core) if same else kother,
            dst_ref=keys(member, core),
            send_sem=sem,
            recv_sem=krecv_sem.at[member],
            device_id=dev(group, m, c),
        )

    def query_copy(r, c, same):
        return pltpu.make_async_remote_copy(
            src_ref=qrecv.at[0, core] if same else qother,
            dst_ref=qrecv.at[r, core],
            send_sem=near_sem.at[0],
            recv_sem=qrecv_sem.at[r],
            device_id=dev(1 - group if r else group, member, c),
        )

    query_copy(1, core, True).start()
    query_copy(1, other, False).start()

    def send_keys(d, carry):
        m = shifted(members - 1 - d)
        key_copy(m, core, True, ksend_sem.at[0]).start()
        key_copy(m, other, False, ksend_sem.at[0]).start()
        return carry

    send_keys(0, 0)
    query_copy(0, other, False).start()
    key_copy(member, other, False, near_sem.at[0]).start()
    if members > 2:
        each(members - 2, lambda d, carry: send_keys(d + 1, carry), 0)

    count = count_ref[0]

    def valid(positions):
        return (positions >= text_slots) | (positions < count)

    lane = lax.broadcasted_iota(jnp.int32, (1, width), 1)
    in_tail = lane >= 2 * head
    spot = jnp.where(in_tail, lane - 2 * head, lane)
    half = jnp.where(in_tail, tail, head)
    far = spot >= half
    spot = jnp.where(far, spot - half, spot) + jnp.where(in_tail, head, 0)
    row_place = jnp.where(far, chip_of(1 - group, member), chip) * pair_rows + spot
    row_weight = jnp.where(valid(row_place), 2.0 * weight, 0.0)

    def place_queries(r):
        for which in (0, 1):
            joined = jnp.concatenate([qrecv[r, c, which].astype(F32) for c in (0, 1)], axis=0)
            joined = joined.astype(BF16)
            qcat[which, r * head:(r + 1) * head] = joined[:head]
            if tail:
                at = 2 * head + r * tail
                qcat[which, at:at + tail] = joined[head:]

    def fill_bias(d, carry):
        place = chip_of(group, sender(d)) * pair_rows
        place += lax.broadcasted_iota(jnp.int32, (pair_rows, 128), 0)
        bias_ref[d] = jnp.where(valid(place), 0.0, MASKED).reshape(groups, 8, 128)
        return carry

    each(members, fill_bias, 0)

    def powers(d, m, which, lanes):
        span = lanes.stop - lanes.start
        scores = lax.dot_general(
            krecv[m, which, 0:pair_rows], qcat[which, lanes], (((1,), (1,)), ((), ())),
            preferred_element_type=F32,
        ).reshape(groups, 8, span)
        bias = bias_ref[d]
        scores = jnp.concatenate([
            scores[:, :, i:min(i + 128, span)] + bias[:, :, :min(128, span - i)]
            for i in range(0, span, 128)
        ], axis=2)
        top = jnp.max(scores, axis=0)
        return top, jnp.exp2((scores - top[None]) * power_scale)

    def score_chunk(d, m, lanes):
        m_s, s_pow = powers(d, m, 0, lanes)
        m_e, e_pow = powers(d, m, 1, lanes)
        s_buf[d, :, :, lanes] = s_pow
        e_buf[d, :, :, lanes] = e_pow
        for i, value in enumerate((
            m_e, jnp.sum(e_pow, axis=0), m_s, jnp.sum(s_pow, axis=0),
            jnp.sum(e_pow * e_pow, axis=0), jnp.sum(e_pow * s_pow, axis=0),
        )):
            stats_ref[i, d, :, lanes] = value

    early, late, full = slice(0, head), slice(head, width), slice(0, width)
    wait(qrecv.at[0, 0], qrecv_sem.at[0])
    wait(kother, krecv_sem.at[member])
    place_queries(0)
    ahead = 2 if members == 4 else 1
    for d in range(ahead):
        m = shifted(d) if d else member
        if d:
            wait(chips_keys(m), krecv_sem.at[m])
        if head:
            score_chunk(d, m, early)
    wait(qrecv.at[1], qrecv_sem.at[1])
    place_queries(1)
    for d in range(ahead):
        score_chunk(d, shifted(d) if d else member, late)

    def far_scores(d, carry):
        d = members - 1 - d
        m = sender(d)
        wait(chips_keys(m), krecv_sem.at[m])
        score_chunk(d, m, full)
        return carry

    each(members - ahead, far_scores, 0)

    def fold(op, value):
        return op(op(value, axis=0), axis=0, keepdims=True)

    tops_e, tops_s = stats_ref[0], stats_ref[2]
    m_e, m_s = fold(jnp.max, tops_e), fold(jnp.max, tops_s)
    f_e = jnp.exp2((tops_e - m_e) * power_scale)
    f_s = jnp.exp2((tops_s - m_s) * power_scale)
    stats = (
        m_e, fold(jnp.sum, stats_ref[1] * f_e),
        m_s, fold(jnp.sum, stats_ref[3] * f_s),
        fold(jnp.sum, stats_ref[4] * (f_e * f_e)),
        fold(jnp.sum, stats_ref[5] * (f_e * f_s)),
    )
    packed = jnp.concatenate(stats + (jnp.zeros((2, width), F32),), axis=0)
    st_send[:, :head] = packed[:, head:2 * head]
    st_send[:, head:2 * head] = packed[:, :head]
    if tail:
        st_send[:, 2 * head:] = jnp.concatenate(
            [packed[:, 2 * head + tail:], packed[:, 2 * head:2 * head + tail]], axis=1
        )
    stat_copy = pltpu.make_async_remote_copy(
        src_ref=st_send, dst_ref=st_recv, send_sem=st_sems.at[0], recv_sem=st_sems.at[1],
        device_id=dev(1 - group, member, core),
    )
    stat_copy.start()

    def turn_keys(d, carry):
        m = sender(d)
        kturn[d] = krecv[m, 1, 0:pair_rows].astype(F32).T.astype(BF16)
        return carry

    each(members, turn_keys, 0)

    stat_copy.wait_recv()
    m_e1, l_e1, m_s1, l_s1, sq1, cr1 = stats
    m_e2, l_e2, m_s2, l_s2, sq2, cr2 = (st_recv[i:i + 1] for i in range(6))
    m_e, m_s = jnp.maximum(m_e1, m_e2), jnp.maximum(m_s1, m_s2)
    fe1, fe2 = jnp.exp2((m_e1 - m_e) * power_scale), jnp.exp2((m_e2 - m_e) * power_scale)
    fs1, fs2 = jnp.exp2((m_s1 - m_s) * power_scale), jnp.exp2((m_s2 - m_s) * power_scale)
    inv_e = 1.0 / (l_e1 * fe1 + l_e2 * fe2)
    inv_s = 1.0 / (l_s1 * fs1 + l_s2 * fs2)
    sq = sq1 * fe1 * fe1 + sq2 * fe2 * fe2
    cr = cr1 * fe1 * fs1 + cr2 * fe2 * fs2
    stats_ref[1] = f_e * (fe1 * inv_e)
    stats_ref[3] = f_s * (fs1 * inv_s)
    delta = row_weight * (sq * inv_e * inv_e - cr * inv_e * inv_s)

    def kg_copy(m, c, sem):
        return pltpu.make_async_remote_copy(
            src_ref=kg_send.at[m, c], dst_ref=kg_recv.at[member, core],
            send_sem=sem, recv_sem=kgrecv_sem.at[member],
            device_id=dev(group, m, c),
        )

    def qg_copy(r, c):
        return pltpu.make_async_remote_copy(
            src_ref=qg_send.at[r, c], dst_ref=qg_recv.at[r, core],
            send_sem=gnear_sem.at[0], recv_sem=qgrecv_sem.at[r],
            device_id=dev(1 - group if r else group, member, c),
        )

    q_edit = qcat[1]

    def grad_chunk(d):
        prob_e = e_buf[d] * stats_ref[1, d][None]
        prob_s = s_buf[d] * stats_ref[3, d][None]
        grad = prob_e * (row_weight[None] * (prob_e - prob_s) - delta[None])
        grad = grad.reshape(pair_rows, width).astype(BF16)
        grad_buf[d] = grad
        return jnp.dot(grad, q_edit, preferred_element_type=F32) * scale

    def far_grad(i, carry):
        d = (2, 3, 1)[i] if members == 4 else members - 1 - i
        m = sender(d)
        k_part = grad_chunk(d)
        for c in (0, 1):
            kg_send[m, c] = k_part[c * rows:(c + 1) * rows].astype(BF16)
        for c in (core, other):
            kg_copy(m, c, kgsend_sem.at[0]).start()
        return carry

    each(members - 1, far_grad, 0)
    k_part = grad_chunk(0)
    for c in (0, 1):
        kg_own[c] = k_part[c * rows:(c + 1) * rows]
        kg_send[member, c] = k_part[c * rows:(c + 1) * rows].astype(BF16)

    q_total = each(
        members,
        lambda d, q: q + jnp.dot(kturn[d], grad_buf[d], preferred_element_type=F32),
        jnp.zeros((HEAD_DIM, width), F32),
    )
    q_rows = q_total.T * scale
    for r in (1, 0):
        joined = [q_rows[r * head:(r + 1) * head]]
        if tail:
            at = 2 * head + r * tail
            joined.append(q_rows[at:at + tail])
        joined = jnp.concatenate(joined, axis=0)
        for c in (0, 1):
            part = joined[c * rows:(c + 1) * rows]
            if not r:
                qg_own[c] = part
            qg_send[r, c] = part.astype(BF16)
        if r:
            qg_copy(1, core).start()
            qg_copy(1, other).start()
    qg_copy(0, other).start()
    kg_copy(member, other, gnear_sem.at[0]).start()

    def put(ref, mine, theirs):
        ref[:, own_cols] = mine
        ref[:, other_cols] = theirs

    wait(kg_recv.at[member, 0], kgrecv_sem.at[member])

    def add_far(d, sums):
        mine, theirs = sums
        m = shifted(d + 1)
        wait(kg_recv.at[m], kgrecv_sem.at[m])
        return mine + kg_recv[m, core].astype(F32), theirs + kg_recv[m, other].astype(F32)

    sums = each(members - 1, add_far, (kg_own[core], kg_recv[member, other].astype(F32)))
    put(kg_ref, *sums)

    wait(qg_recv.at[0, 0], qgrecv_sem.at[0])
    wait(qg_recv.at[1], qgrecv_sem.at[1])
    put(
        qg_ref,
        qg_own[core] + qg_recv[1, core].astype(F32),
        qg_recv[0, other].astype(F32) + qg_recv[1, other].astype(F32),
    )

    wait(chips_keys(slice(0, members - 1)), ksend_sem.at[0])
    wait(qrecv, near_sem.at[0])
    stat_copy.wait_send()
    wait(kg_send.at[0:members - 1], kgsend_sem.at[0])
    wait(qg_send, gnear_sem.at[0])


def put_out(qg_vmem, kg_vmem, qg_hbm, kg_hbm, sems):
    copies = (
        pltpu.make_async_copy(qg_vmem, qg_hbm, sems.at[0]),
        pltpu.make_async_copy(kg_vmem, kg_hbm, sems.at[1]),
    )
    for copy in copies:
        copy.start()
    for copy in copies:
        copy.wait()


def solution(mesh):
    chips = mesh.shape["ctx"] // 2
    members = chips // 2

    def local(query_source, key_source, query_edit, key_edit, text_count):
        rows, full = query_source.shape
        width = 4 * rows
        groups = 2 * rows // 8
        dma = pltpu.SemaphoreType.DMA
        vmem = pltpu.VMEM
        grads = pl.pallas_call(
            functools.partial(kernel, chips),
            out_shape=(
                pltpu.VMEM((rows, full), F32),
                pltpu.VMEM((rows, full), F32),
            ),
            in_specs=[pl.BlockSpec(memory_space=pltpu.HBM)] * 5,
            out_specs=(pl.BlockSpec(memory_space=pltpu.VMEM),) * 2,
            scratch_shapes=[
                pltpu.SMEM((1,), jnp.int32),
                vmem((members, 2, 2 * rows + 8, HEAD_DIM), BF16),
                vmem((2, rows, HEAD_DIM), BF16),
                vmem((2, 2, 2, rows, HEAD_DIM), BF16),
                vmem((2, rows, HEAD_DIM), BF16),
                vmem((2, width, HEAD_DIM), BF16),
                vmem((members, HEAD_DIM, 2 * rows), BF16),
                vmem((members, groups, 8, 128), F32),
                vmem((members, 2 * rows, width), BF16),
                vmem((members, groups, 8, width), F32),
                vmem((members, groups, 8, width), F32),
                vmem((6, members, 8, width), F32),
                vmem((8, width), F32),
                vmem((8, width), F32),
                vmem((members, 2, rows, HEAD_DIM), BF16),
                vmem((members, 2, rows, HEAD_DIM), BF16),
                vmem((2, 2, rows, HEAD_DIM), BF16),
                vmem((2, 2, rows, HEAD_DIM), BF16),
                vmem((2, rows, HEAD_DIM), F32),
                vmem((2, rows, HEAD_DIM), F32),
                dma((2,)),
                dma((1,)),
                dma((1,)),
                dma((members,)),
                dma((2,)),
                dma((2,)),
                dma((1,)),
                dma((1,)),
                dma((members,)),
                dma((2,)),
            ],
            compiler_params=pltpu.CompilerParams(collective_id=0, has_side_effects=True),
        )(text_count, query_source, key_source, query_edit, key_edit)
        return pl.pallas_call(
            put_out,
            out_shape=(pltpu.HBM((rows, full), F32),) * 2,
            in_specs=[pl.BlockSpec(memory_space=pltpu.VMEM)] * 2,
            out_specs=(pl.BlockSpec(memory_space=pltpu.HBM),) * 2,
            scratch_shapes=[dma((2,))],
        )(*(pltpu.with_memory_space_constraint(g, pltpu.VMEM) for g in grads))

    spec = P(("req", "ctx"), None)
    return jax.shard_map(
        local, mesh=mesh, in_specs=(spec,) * 4 + (P("req"),), out_specs=(spec, spec), check_vma=False
    )
```

```python
import functools
import math

import jax
import jax.numpy as jnp
from jax import lax
from jax.experimental import pallas as pl
from jax.experimental.pallas import tpu as pltpu
from jax.sharding import PartitionSpec as P

HEAD_DIM = 128
MASKED = -1e30
F32 = jnp.float32
BF16 = jnp.bfloat16


def kernel(
    chips,
    count_hbm, qs_hbm, ks_hbm, qe_hbm, ke_hbm,
    qg_ref, kg_ref,
    count_ref, krecv, kother, qrecv, qother, qcat, kturn, bias_ref, grad_buf, e_buf, s_buf, stats_ref,
    st_send, st_recv,
    kg_send, kg_recv, qg_send, qg_recv, qg_own, kg_own,
    load_sem, ksend_sem, near_sem, krecv_sem, qrecv_sem, st_sems,
    kgsend_sem, gnear_sem, kgrecv_sem, qgrecv_sem,
):
    members = chips // 2
    rows = kother.shape[1]
    pair_rows = 2 * rows
    width = 2 * pair_rows
    head = pair_rows // 128 * 128
    tail = pair_rows - head
    groups = pair_rows // 8
    all_rows = rows * chips * 2
    text_slots = min(512, all_rows // 4)
    scale = 1.0 / math.sqrt(HEAD_DIM)
    power_scale = scale * math.log2(math.e)
    weight = 4.0 * all_rows * math.sqrt(all_rows)
    me = lax.axis_index("ctx")
    chip, core = me // 2, me % 2
    other = 1 - core
    group, member = chip // members, chip % members

    def chip_of(g, m):
        return g * members + m

    def dev(g, m, c):
        return {"ctx": chip_of(g, m) * 2 + c}

    def shifted(d):
        if members % 2:
            return (member + d) % members
        return (member // 2 + d // 2) % (members // 2) * 2 + (member + d) % 2

    def sender(d):
        if members % 2:
            return (member + members - d) % members
        return (member // 2 + members - d // 2) % (members // 2) * 2 + (member + d) % 2

    def each(n, body, init):
        if n <= 8:
            for i in range(n):
                init = body(i, init)
            return init
        return lax.fori_loop(0, n, body, init)

    def wait(ref, sem):
        pltpu.make_async_copy(ref, ref, sem).wait()

    def keys(m, c):
        return krecv.at[m, :, pl.ds(pl.multiple_of(c * rows, 8), rows)]

    def chips_keys(m):
        return krecv.at[m, :, 0:pair_rows]

    own_cols = pl.ds(pl.multiple_of(core * HEAD_DIM, HEAD_DIM), HEAD_DIM)
    other_cols = pl.ds(pl.multiple_of(other * HEAD_DIM, HEAD_DIM), HEAD_DIM)
    loads = []
    for i, (src, dst_own, dst_other) in enumerate((
        (qs_hbm, qrecv.at[0, core, 0], qother.at[0]),
        (qe_hbm, qrecv.at[0, core, 1], qother.at[1]),
        (ks_hbm, keys(member, core).at[0], kother.at[0]),
        (ke_hbm, keys(member, core).at[1], kother.at[1]),
    )):
        loads.append(pltpu.make_async_copy(src.at[:, own_cols], dst_own, load_sem.at[0]))
        loads.append(pltpu.make_async_copy(src.at[:, other_cols], dst_other, load_sem.at[0]))
    count_load = pltpu.make_async_copy(count_hbm, count_ref, load_sem.at[1])
    for load in loads:
        load.start()
    count_load.start()

    barrier = pltpu.get_barrier_semaphore()

    def greet(d, carry):
        for c in (0, 1):
            pl.semaphore_signal(barrier, inc=1, device_id=dev(group, shifted(d + 1), c))
        return carry

    for c in (0, 1):
        pl.semaphore_signal(barrier, inc=1, device_id=dev(1 - group, member, c))
    pl.semaphore_signal(barrier, inc=1, device_id=dev(group, member, other))
    each(members - 1, greet, 0)
    pl.semaphore_wait(barrier, 2 * members + 1)
    wait(chips_keys(slice(0, 2)), load_sem.at[0])
    count_load.wait()

    def key_copy(m, c, same, sem):
        return pltpu.make_async_remote_copy(
            src_ref=keys(member, core) if same else kother,
            dst_ref=keys(member, core),
            send_sem=sem,
            recv_sem=krecv_sem.at[member],
            device_id=dev(group, m, c),
        )

    def query_copy(r, c, same):
        return pltpu.make_async_remote_copy(
            src_ref=qrecv.at[0, core] if same else qother,
            dst_ref=qrecv.at[r, core],
            send_sem=near_sem.at[0],
            recv_sem=qrecv_sem.at[r],
            device_id=dev(1 - group if r else group, member, c),
        )

    query_copy(1, core, True).start()
    query_copy(1, other, False).start()

    def send_keys(d, carry):
        m = shifted(members - 1 - d)
        key_copy(m, core, True, ksend_sem.at[0]).start()
        key_copy(m, other, False, ksend_sem.at[0]).start()
        return carry

    send_keys(0, 0)
    query_copy(0, other, False).start()
    key_copy(member, other, False, near_sem.at[0]).start()
    if members > 2:
        each(members - 2, lambda d, carry: send_keys(d + 1, carry), 0)

    count = count_ref[0]

    def valid(positions):
        return (positions >= text_slots) | (positions < count)

    lane = lax.broadcasted_iota(jnp.int32, (1, width), 1)
    in_tail = lane >= 2 * head
    spot = jnp.where(in_tail, lane - 2 * head, lane)
    half = jnp.where(in_tail, tail, head)
    far = spot >= half
    spot = jnp.where(far, spot - half, spot) + jnp.where(in_tail, head, 0)
    row_place = jnp.where(far, chip_of(1 - group, member), chip) * pair_rows + spot
    row_weight = jnp.where(valid(row_place), 2.0 * weight, 0.0)

    def place_queries(r):
        for which in (0, 1):
            joined = jnp.concatenate([qrecv[r, c, which].astype(F32) for c in (0, 1)], axis=0)
            joined = joined.astype(BF16)
            qcat[which, r * head:(r + 1) * head] = joined[:head]
            if tail:
                at = 2 * head + r * tail
                qcat[which, at:at + tail] = joined[head:]

    def fill_bias(d, carry):
        place = chip_of(group, sender(d)) * pair_rows
        place += lax.broadcasted_iota(jnp.int32, (pair_rows, 128), 0)
        bias_ref[d] = jnp.where(valid(place), 0.0, MASKED).reshape(groups, 8, 128)
        return carry

    each(members, fill_bias, 0)

    def powers(d, m, which, lanes):
        span = lanes.stop - lanes.start
        scores = lax.dot_general(
            krecv[m, which, 0:pair_rows], qcat[which, lanes], (((1,), (1,)), ((), ())),
            preferred_element_type=F32,
        ).reshape(groups, 8, span)
        bias = bias_ref[d]
        scores = jnp.concatenate([
            scores[:, :, i:min(i + 128, span)] + bias[:, :, :min(128, span - i)]
            for i in range(0, span, 128)
        ], axis=2)
        top = jnp.max(scores, axis=0)
        return top, jnp.exp2((scores - top[None]) * power_scale)

    def score_chunk(d, m, lanes):
        m_s, s_pow = powers(d, m, 0, lanes)
        m_e, e_pow = powers(d, m, 1, lanes)
        s_buf[d, :, :, lanes] = s_pow
        e_buf[d, :, :, lanes] = e_pow
        for i, value in enumerate((
            m_e, jnp.sum(e_pow, axis=0), m_s, jnp.sum(s_pow, axis=0),
            jnp.sum(e_pow * e_pow, axis=0), jnp.sum(e_pow * s_pow, axis=0),
        )):
            stats_ref[i, d, :, lanes] = value

    early, late, full = slice(0, head), slice(head, width), slice(0, width)
    wait(qrecv.at[0, 0], qrecv_sem.at[0])
    wait(kother, krecv_sem.at[member])
    place_queries(0)
    ahead = 2 if members == 4 else 1
    for d in range(ahead):
        m = shifted(d) if d else member
        if d:
            wait(chips_keys(m), krecv_sem.at[m])
        if head:
            score_chunk(d, m, early)
    wait(qrecv.at[1], qrecv_sem.at[1])
    place_queries(1)
    for d in range(ahead):
        score_chunk(d, shifted(d) if d else member, late)

    def far_scores(d, carry):
        d = members - 1 - d
        m = sender(d)
        wait(chips_keys(m), krecv_sem.at[m])
        score_chunk(d, m, full)
        return carry

    each(members - ahead, far_scores, 0)

    def fold(op, value):
        return op(op(value, axis=0), axis=0, keepdims=True)

    tops_e, tops_s = stats_ref[0], stats_ref[2]
    m_e, m_s = fold(jnp.max, tops_e), fold(jnp.max, tops_s)
    f_e = jnp.exp2((tops_e - m_e) * power_scale)
    f_s = jnp.exp2((tops_s - m_s) * power_scale)
    stats = (
        m_e, fold(jnp.sum, stats_ref[1] * f_e),
        m_s, fold(jnp.sum, stats_ref[3] * f_s),
        fold(jnp.sum, stats_ref[4] * (f_e * f_e)),
        fold(jnp.sum, stats_ref[5] * (f_e * f_s)),
    )
    packed = jnp.concatenate(stats + (jnp.zeros((2, width), F32),), axis=0)
    st_send[:, :head] = packed[:, head:2 * head]
    st_send[:, head:2 * head] = packed[:, :head]
    if tail:
        st_send[:, 2 * head:] = jnp.concatenate(
            [packed[:, 2 * head + tail:], packed[:, 2 * head:2 * head + tail]], axis=1
        )
    stat_copy = pltpu.make_async_remote_copy(
        src_ref=st_send, dst_ref=st_recv, send_sem=st_sems.at[0], recv_sem=st_sems.at[1],
        device_id=dev(1 - group, member, core),
    )
    stat_copy.start()

    def turn_keys(d, carry):
        m = sender(d)
        kturn[d] = krecv[m, 1, 0:pair_rows].astype(F32).T.astype(BF16)
        return carry

    each(members, turn_keys, 0)

    stat_copy.wait_recv()
    m_e1, l_e1, m_s1, l_s1, sq1, cr1 = stats
    m_e2, l_e2, m_s2, l_s2, sq2, cr2 = (st_recv[i:i + 1] for i in range(6))
    m_e, m_s = jnp.maximum(m_e1, m_e2), jnp.maximum(m_s1, m_s2)
    fe1, fe2 = jnp.exp2((m_e1 - m_e) * power_scale), jnp.exp2((m_e2 - m_e) * power_scale)
    fs1, fs2 = jnp.exp2((m_s1 - m_s) * power_scale), jnp.exp2((m_s2 - m_s) * power_scale)
    inv_e = 1.0 / (l_e1 * fe1 + l_e2 * fe2)
    inv_s = 1.0 / (l_s1 * fs1 + l_s2 * fs2)
    sq = sq1 * fe1 * fe1 + sq2 * fe2 * fe2
    cr = cr1 * fe1 * fs1 + cr2 * fe2 * fs2
    stats_ref[1] = f_e * (fe1 * inv_e)
    stats_ref[3] = f_s * (fs1 * inv_s)
    delta = row_weight * (sq * inv_e * inv_e - cr * inv_e * inv_s)

    def kg_copy(m, c, sem):
        return pltpu.make_async_remote_copy(
            src_ref=kg_send.at[m, c], dst_ref=kg_recv.at[member, core],
            send_sem=sem, recv_sem=kgrecv_sem.at[member],
            device_id=dev(group, m, c),
        )

    def qg_copy(r, c):
        return pltpu.make_async_remote_copy(
            src_ref=qg_send.at[r, c], dst_ref=qg_recv.at[r, core],
            send_sem=gnear_sem.at[0], recv_sem=qgrecv_sem.at[r],
            device_id=dev(1 - group if r else group, member, c),
        )

    q_edit = qcat[1]

    def grad_chunk(d):
        prob_e = e_buf[d] * stats_ref[1, d][None]
        prob_s = s_buf[d] * stats_ref[3, d][None]
        grad = prob_e * (row_weight[None] * (prob_e - prob_s) - delta[None])
        grad = grad.reshape(pair_rows, width).astype(BF16)
        grad_buf[d] = grad
        return jnp.dot(grad, q_edit, preferred_element_type=F32) * scale

    def far_grad(i, carry):
        d = (2, 3, 1)[i] if members == 4 else members - 1 - i
        m = sender(d)
        k_part = grad_chunk(d)
        for c in (0, 1):
            kg_send[m, c] = k_part[c * rows:(c + 1) * rows].astype(BF16)
        for c in (core, other):
            kg_copy(m, c, kgsend_sem.at[0]).start()
        return carry

    each(members - 1, far_grad, 0)
    k_part = grad_chunk(0)
    for c in (0, 1):
        kg_own[c] = k_part[c * rows:(c + 1) * rows]
        kg_send[member, c] = k_part[c * rows:(c + 1) * rows].astype(BF16)

    q_total = each(
        members,
        lambda d, q: q + jnp.dot(kturn[d], grad_buf[d], preferred_element_type=F32),
        jnp.zeros((HEAD_DIM, width), F32),
    )
    q_rows = q_total.T * scale
    for r in (1, 0):
        joined = [q_rows[r * head:(r + 1) * head]]
        if tail:
            at = 2 * head + r * tail
            joined.append(q_rows[at:at + tail])
        joined = jnp.concatenate(joined, axis=0)
        for c in (0, 1):
            part = joined[c * rows:(c + 1) * rows]
            if not r:
                qg_own[c] = part
            qg_send[r, c] = part.astype(BF16)
        if r:
            qg_copy(1, core).start()
            qg_copy(1, other).start()
    qg_copy(0, other).start()
    kg_copy(member, other, gnear_sem.at[0]).start()

    def put(ref, mine, theirs):
        ref[:, own_cols] = mine
        ref[:, other_cols] = theirs

    wait(kg_recv.at[member, 0], kgrecv_sem.at[member])

    def add_far(d, sums):
        mine, theirs = sums
        m = shifted(d + 1)
        wait(kg_recv.at[m], kgrecv_sem.at[m])
        return mine + kg_recv[m, core].astype(F32), theirs + kg_recv[m, other].astype(F32)

    sums = each(members - 1, add_far, (kg_own[core], kg_recv[member, other].astype(F32)))
    put(kg_ref, *sums)

    wait(qg_recv.at[0, 0], qgrecv_sem.at[0])
    wait(qg_recv.at[1], qgrecv_sem.at[1])
    put(
        qg_ref,
        qg_own[core] + qg_recv[1, core].astype(F32),
        qg_recv[0, other].astype(F32) + qg_recv[1, other].astype(F32),
    )

    wait(chips_keys(slice(0, members - 1)), ksend_sem.at[0])
    wait(qrecv, near_sem.at[0])
    stat_copy.wait_send()
    wait(kg_send.at[0:members - 1], kgsend_sem.at[0])
    wait(qg_send, gnear_sem.at[0])


def line_kernel(
    chips,
    count_hbm, qs_hbm, ks_hbm, qe_hbm, ke_hbm,
    qg_ref, kg_ref,
    count_ref, krecv, kother, qrecv, qother, qcat, kturn, bias_ref, grad_buf, e_buf, s_buf, stats_ref,
    st_send, st_recv,
    st_side, st_turn, kg_send, kg_recv, qg_send, qg_recv, qg_own, kg_own,
    load_sem, ksend_sem, near_sem, krecv_sem, qrecv_sem, st_sems, side_sems,
    kgsend_sem, gnear_sem, gfar_sem, kgrecv_sem, qgrecv_sem,
):
    members = chips // 2
    rows = kother.shape[1]
    pair_rows = 2 * rows
    head = pair_rows // 128 * 128
    tail = pair_rows - head
    width = qcat.shape[1]
    blocks = {0: 0, 1: width - head, 2: width - 2 * head}
    groups = pair_rows // 8
    all_rows = rows * chips * 2
    text_slots = min(512, all_rows // 4)
    scale = 1.0 / math.sqrt(HEAD_DIM)
    power_scale = scale * math.log2(math.e)
    weight = 4.0 * all_rows * math.sqrt(all_rows)
    me = lax.axis_index("ctx")
    chip, core = me // 2, me % 2
    other = 1 - core
    group, member = chip // members, chip % members
    inner = (group + member // 2) % 2 == 1
    outer = (group + member // 2) % 2 == 0
    target = (2 - group) * 2 + chip % 2

    def chip_of(g, m):
        return g * members + m

    def dev(g, m, c):
        return {"ctx": chip_of(g, m) * 2 + c}

    def shifted(d):
        if members % 2:
            return (member + d) % members
        return (member // 2 + d // 2) % (members // 2) * 2 + (member + d) % 2

    def sender(d):
        if members % 2:
            return (member + members - d) % members
        return (member // 2 + members - d // 2) % (members // 2) * 2 + (member + d) % 2

    def each(n, body, init):
        if n <= 8:
            for i in range(n):
                init = body(i, init)
            return init
        return lax.fori_loop(0, n, body, init)

    def wait(ref, sem):
        pltpu.make_async_copy(ref, ref, sem).wait()

    def keys(m, c):
        return krecv.at[m, :, pl.ds(pl.multiple_of(c * rows, 8), rows)]

    def chips_keys(m):
        return krecv.at[m, :, 0:pair_rows]

    own_cols = pl.ds(pl.multiple_of(core * HEAD_DIM, HEAD_DIM), HEAD_DIM)
    other_cols = pl.ds(pl.multiple_of(other * HEAD_DIM, HEAD_DIM), HEAD_DIM)
    loads = []
    for i, (src, dst_own, dst_other) in enumerate((
        (qs_hbm, qrecv.at[0, core, 0], qother.at[0]),
        (qe_hbm, qrecv.at[0, core, 1], qother.at[1]),
        (ks_hbm, keys(member, core).at[0], kother.at[0]),
        (ke_hbm, keys(member, core).at[1], kother.at[1]),
    )):
        loads.append(pltpu.make_async_copy(src.at[:, own_cols], dst_own, load_sem.at[0]))
        loads.append(pltpu.make_async_copy(src.at[:, other_cols], dst_other, load_sem.at[0]))
    count_load = pltpu.make_async_copy(count_hbm, count_ref, load_sem.at[1])
    for load in loads:
        load.start()
    count_load.start()

    barrier = pltpu.get_barrier_semaphore()

    for c in (0, 1):
        pl.semaphore_signal(barrier, inc=1, device_id=dev(1 - group, member, c))

    @pl.when(inner)
    def _():
        for c in (0, 1):
            pl.semaphore_signal(barrier, inc=1, device_id={"ctx": target * 2 + c})

    for d in (3, 2, 1):
        for c in (0, 1):
            pl.semaphore_signal(barrier, inc=1, device_id=dev(group, shifted(d), c))
    pl.semaphore_signal(barrier, inc=1, device_id=dev(group, member, other))
    qcat[...] = jnp.zeros_like(qcat)
    pl.semaphore_wait(barrier, jnp.where(inner, 2 * members + 3, 2 * members + 1))
    wait(chips_keys(slice(0, 2)), load_sem.at[0])
    count_load.wait()

    def key_copy(m, c, same, sem):
        return pltpu.make_async_remote_copy(
            src_ref=keys(member, core) if same else kother,
            dst_ref=keys(member, core),
            send_sem=sem,
            recv_sem=krecv_sem.at[member],
            device_id=dev(group, m, c),
        )

    far_slot = jnp.where(inner, 1, 2)

    def query_copy(far, c, same):
        slot = far_slot if far else 0
        return pltpu.make_async_remote_copy(
            src_ref=qrecv.at[0, core] if same else qother,
            dst_ref=qrecv.at[slot, core],
            send_sem=near_sem.at[0],
            recv_sem=qrecv_sem.at[slot],
            device_id={"ctx": target * 2 + c} if far else dev(group, member, c),
        )

    def send_keys(d):
        key_copy(shifted(d), core, True, ksend_sem.at[0]).start()
        key_copy(shifted(d), other, False, ksend_sem.at[0]).start()

    query_copy(1, core, True).start()
    query_copy(1, other, False).start()
    query_copy(0, other, False).start()
    key_copy(member, other, False, near_sem.at[0]).start()
    send_keys(3)
    send_keys(2)
    send_keys(1)

    count = count_ref[0]

    def valid(positions):
        return (positions >= text_slots) | (positions < count)

    lane = lax.broadcasted_iota(jnp.int32, (1, width), 1)
    own_lane = lane < head
    row_place = chip * pair_rows + lane
    live = own_lane
    for slot, owner in ((0, chip), (1, target), (2, chip_of(1 - group, member))):
        there = lane >= head + slot * tail
        there = there & (lane < head + (slot + 1) * tail)
        row_place = jnp.where(there, owner * pair_rows + lane - slot * tail, row_place)
        if slot:
            at = blocks[slot]
            ahead = (lane >= at) & (lane < at + head)
            row_place = jnp.where(ahead, owner * pair_rows + lane - at, row_place)
            there = (there | ahead) & inner
        live = live | there
    row_weight = jnp.where(live & valid(row_place), 2.0 * weight, 0.0)

    @pl.when(outer)
    def _():
        for buf in (e_buf, s_buf):
            buf[:, :, :, width - 2 * head:] = jnp.zeros((members, groups, 8, 2 * head), F32)

    def place_queries(slot):
        for which in (0, 1):
            joined = jnp.concatenate([qrecv[slot, c, which].astype(F32) for c in (0, 1)], axis=0)
            joined = joined.astype(BF16)
            qcat[which, blocks[slot]:blocks[slot] + head] = joined[:head]
            if tail:
                at = head + slot * tail
                qcat[which, at:at + tail] = joined[head:]

    def fill_bias(d, carry):
        place = chip_of(group, sender(d)) * pair_rows
        place += lax.broadcasted_iota(jnp.int32, (pair_rows, 128), 0)
        bias_ref[d] = jnp.where(valid(place), 0.0, MASKED).reshape(groups, 8, 128)
        return carry

    each(members, fill_bias, 0)

    def powers(d, m, which, lanes):
        span = lanes.stop - lanes.start
        scores = lax.dot_general(
            krecv[m, which, 0:pair_rows], qcat[which, lanes], (((1,), (1,)), ((), ())),
            preferred_element_type=F32,
        ).reshape(groups, 8, span)
        bias = bias_ref[d]
        scores = jnp.concatenate([
            scores[:, :, i:min(i + 128, span)] + bias[:, :, :min(128, span - i)]
            for i in range(0, span, 128)
        ], axis=2)
        top = jnp.max(scores, axis=0)
        return top, jnp.exp2((scores - top[None]) * power_scale)

    def score_chunk(d, m, lanes):
        m_s, s_pow = powers(d, m, 0, lanes)
        m_e, e_pow = powers(d, m, 1, lanes)
        s_buf[d, :, :, lanes] = s_pow
        e_buf[d, :, :, lanes] = e_pow
        for i, value in enumerate((
            m_e, jnp.sum(e_pow, axis=0), m_s, jnp.sum(s_pow, axis=0),
            jnp.sum(e_pow * e_pow, axis=0), jnp.sum(e_pow * s_pow, axis=0),
        )):
            stats_ref[i, d, :, lanes] = value

    own, late = slice(0, head), slice(head, width - head)
    side, full, both = slice(width - head, width), slice(0, width), slice(0, width - 2 * head)

    def keys_from(d):
        m = sender(d)
        wait(chips_keys(m), krecv_sem.at[m])
        return m

    wait(qrecv.at[0, 0], qrecv_sem.at[0])
    wait(kother, krecv_sem.at[member])
    place_queries(0)

    @pl.when(outer)
    def _():
        score_chunk(0, member, both)
        for d in (1, 3, 2):
            score_chunk(d, keys_from(d), both)

    @pl.when(inner)
    def _():
        score_chunk(0, member, own)
        score_chunk(1, keys_from(1), own)
        wait(qrecv.at[1], qrecv_sem.at[1])
        place_queries(1)
        score_chunk(0, member, side)
        score_chunk(1, sender(1), side)
        for d in (3, 2):
            m = keys_from(d)
            score_chunk(d, m, own)
            score_chunk(d, m, side)
        wait(qrecv.at[2], qrecv_sem.at[2])
        place_queries(2)
        for d in range(4):
            score_chunk(d, sender(d) if d else member, late)

    def fold(op, value):
        return op(op(value, axis=0), axis=0, keepdims=True)

    tops_e, tops_s = stats_ref[0], stats_ref[2]
    m_e, m_s = fold(jnp.max, tops_e), fold(jnp.max, tops_s)
    f_e = jnp.exp2((tops_e - m_e) * power_scale)
    f_s = jnp.exp2((tops_s - m_s) * power_scale)
    stats = (
        m_e, fold(jnp.sum, stats_ref[1] * f_e),
        m_s, fold(jnp.sum, stats_ref[3] * f_s),
        fold(jnp.sum, stats_ref[4] * (f_e * f_e)),
        fold(jnp.sum, stats_ref[5] * (f_e * f_s)),
    )
    packed = jnp.concatenate(stats + (jnp.zeros((2, width), F32),), axis=0)
    span = width - 3 * head
    tails = packed[:, head:head + span]
    st_send[:, :head] = jnp.where(inner, packed[:, blocks[2]:blocks[2] + head], packed[:, :head])
    st_send[:, head:] = jnp.where(
        inner, pltpu.roll(tails, span - 2 * tail, 1), pltpu.roll(tails, 2 * tail, 1)
    )
    stat_copy = pltpu.make_async_remote_copy(
        src_ref=st_send, dst_ref=st_recv, send_sem=st_sems.at[0], recv_sem=st_sems.at[1],
        device_id=dev(1 - group, member, core),
    )
    stat_copy.start()
    side_copy = pltpu.make_async_remote_copy(
        src_ref=st_side, dst_ref=st_turn, send_sem=side_sems.at[0], recv_sem=side_sems.at[1],
        device_id={"ctx": target * 2 + core},
    )

    @pl.when(inner)
    def _():
        st_side[:, :head] = packed[:, blocks[1]:]
        st_side[:, head:2 * head] = packed[:, :head]
        tail_lane = lax.broadcasted_iota(jnp.int32, (8, span), 1)
        st_side[:, 2 * head:] = jnp.where(
            tail_lane < tail, pltpu.roll(tails, span - tail, 1), pltpu.roll(tails, tail, 1)
        )
        side_copy.start()

    def turn_keys(d, carry):
        m = sender(d)
        kturn[d] = krecv[m, 1, 0:pair_rows].astype(F32).T.astype(BF16)
        return carry

    each(members, turn_keys, 0)

    @pl.when(inner)
    def _():
        side_copy.wait_recv()

    stat_copy.wait_recv()
    there, turned = st_recv[...], st_turn[...]
    tail_lane = lax.broadcasted_iota(jnp.int32, (8, span), 1)
    second = jnp.concatenate([
        jnp.where(inner, turned[:, :head], there[:, :head]),
        jnp.where(inner & (tail_lane < 2 * tail), turned[:, 2 * head:], there[:, head:]),
        there[:, :head],
        turned[:, head:2 * head],
    ], axis=1)
    m_e1, l_e1, m_s1, l_s1, sq1, cr1 = stats
    m_e2, l_e2, m_s2, l_s2, sq2, cr2 = (second[i:i + 1] for i in range(6))
    m_e, m_s = jnp.maximum(m_e1, m_e2), jnp.maximum(m_s1, m_s2)
    fe1, fe2 = jnp.exp2((m_e1 - m_e) * power_scale), jnp.exp2((m_e2 - m_e) * power_scale)
    fs1, fs2 = jnp.exp2((m_s1 - m_s) * power_scale), jnp.exp2((m_s2 - m_s) * power_scale)
    inv_e = 1.0 / (l_e1 * fe1 + l_e2 * fe2)
    inv_s = 1.0 / (l_s1 * fs1 + l_s2 * fs2)
    sq = sq1 * fe1 * fe1 + sq2 * fe2 * fe2
    cr = cr1 * fe1 * fs1 + cr2 * fe2 * fs2
    stats_ref[1] = jnp.where(live, f_e * (fe1 * inv_e), 0.0)
    stats_ref[3] = jnp.where(live, f_s * (fs1 * inv_s), 0.0)
    delta = jnp.where(live, row_weight * (sq * inv_e * inv_e - cr * inv_e * inv_s), 0.0)

    def kg_copy(m, c, sem):
        return pltpu.make_async_remote_copy(
            src_ref=kg_send.at[m, c], dst_ref=kg_recv.at[member, core],
            send_sem=sem, recv_sem=kgrecv_sem.at[member],
            device_id=dev(group, m, c),
        )

    def qg_copy(slot, c):
        return pltpu.make_async_remote_copy(
            src_ref=qg_send.at[slot, c], dst_ref=qg_recv.at[1 if slot else 0, core],
            send_sem=gfar_sem.at[0] if slot else gnear_sem.at[0],
            recv_sem=qgrecv_sem.at[1 if slot else 0],
            device_id=(dev(group, member, c), {"ctx": target * 2 + c}, dev(1 - group, member, c))[slot],
        )

    q_edit = qcat[1]

    def grad_chunk(d):
        prob_e = e_buf[d] * stats_ref[1, d][None]
        prob_s = s_buf[d] * stats_ref[3, d][None]
        grad = prob_e * (row_weight[None] * (prob_e - prob_s) - delta[None])
        grad = grad.reshape(pair_rows, width).astype(BF16)
        grad_buf[d] = grad
        return jnp.dot(grad, q_edit, preferred_element_type=F32) * scale

    def far_grad(i, carry):
        d = (2, 3, 1)[i] if members == 4 else members - 1 - i
        m = sender(d)
        k_part = grad_chunk(d)
        for c in (0, 1):
            kg_send[m, c] = k_part[c * rows:(c + 1) * rows].astype(BF16)
        for c in (core, other):
            kg_copy(m, c, kgsend_sem.at[0]).start()
        return carry

    each(members - 1, far_grad, 0)
    k_part = grad_chunk(0)
    for c in (0, 1):
        kg_own[c] = k_part[c * rows:(c + 1) * rows]
        kg_send[member, c] = k_part[c * rows:(c + 1) * rows].astype(BF16)

    q_total = each(
        members,
        lambda d, q: q + jnp.dot(kturn[d], grad_buf[d], preferred_element_type=F32),
        jnp.zeros((HEAD_DIM, width), F32),
    )
    q_rows = q_total.T * scale
    for slot in (2, 1, 0):
        joined = [q_rows[blocks[slot]:blocks[slot] + head]]
        if tail:
            at = head + slot * tail
            joined.append(q_rows[at:at + tail])
        joined = jnp.concatenate(joined, axis=0)
        for c in (0, 1):
            part = joined[c * rows:(c + 1) * rows]
            if not slot:
                qg_own[c] = part
            qg_send[slot, c] = part.astype(BF16)

    @pl.when(inner)
    def _():
        for slot in (2, 1):
            qg_copy(slot, core).start()
            qg_copy(slot, other).start()

    qg_copy(0, other).start()
    kg_copy(member, other, gnear_sem.at[0]).start()

    def put(ref, mine, theirs):
        ref[:, own_cols] = mine
        ref[:, other_cols] = theirs

    wait(kg_recv.at[member, 0], kgrecv_sem.at[member])

    def add_far(d, sums):
        mine, theirs = sums
        m = shifted(d + 1)
        wait(kg_recv.at[m], kgrecv_sem.at[m])
        return mine + kg_recv[m, core].astype(F32), theirs + kg_recv[m, other].astype(F32)

    sums = each(members - 1, add_far, (kg_own[core], kg_recv[member, other].astype(F32)))
    put(kg_ref, *sums)

    wait(qg_recv.at[0, 0], qgrecv_sem.at[0])
    wait(qg_recv.at[1], qgrecv_sem.at[1])
    put(
        qg_ref,
        qg_own[core] + qg_recv[1, core].astype(F32),
        qg_recv[0, other].astype(F32) + qg_recv[1, other].astype(F32),
    )

    wait(chips_keys(slice(0, members - 1)), ksend_sem.at[0])
    wait(qrecv.at[0:2], near_sem.at[0])
    stat_copy.wait_send()
    wait(kg_send.at[0:members - 1], kgsend_sem.at[0])
    wait(qg_send.at[0], gnear_sem.at[0])

    @pl.when(inner)
    def _():
        wait(qg_send.at[1:3], gfar_sem.at[0])
        side_copy.wait_send()


def put_out(qg_vmem, kg_vmem, qg_hbm, kg_hbm, sems):
    copies = (
        pltpu.make_async_copy(qg_vmem, qg_hbm, sems.at[0]),
        pltpu.make_async_copy(kg_vmem, kg_hbm, sems.at[1]),
    )
    for copy in copies:
        copy.start()
    for copy in copies:
        copy.wait()


def solution(mesh):
    chips = mesh.shape["ctx"] // 2
    members = chips // 2

    def local(query_source, key_source, query_edit, key_edit, text_count):
        rows, full = query_source.shape
        width = 4 * rows
        groups = 2 * rows // 8
        dma = pltpu.SemaphoreType.DMA
        vmem = pltpu.VMEM
        in_line = chips == 8
        if in_line:
            pair = 2 * rows
            head = pair // 128 * 128
            width = 3 * head + -(-3 * (pair - head) // 128) * 128
        slots = 3 if in_line else 2
        stat = vmem((8, width - 2 * head if in_line else width), F32)
        side = [vmem((8, width - head), F32)] * 2 if in_line else []
        grads = pl.pallas_call(
            functools.partial(line_kernel if in_line else kernel, chips),
            out_shape=(
                pltpu.VMEM((rows, full), F32),
                pltpu.VMEM((rows, full), F32),
            ),
            in_specs=[pl.BlockSpec(memory_space=pltpu.HBM)] * 5,
            out_specs=(pl.BlockSpec(memory_space=pltpu.VMEM),) * 2,
            scratch_shapes=[
                pltpu.SMEM((1,), jnp.int32),
                vmem((members, 2, 2 * rows + 8, HEAD_DIM), BF16),
                vmem((2, rows, HEAD_DIM), BF16),
                vmem((slots, 2, 2, rows, HEAD_DIM), BF16),
                vmem((2, rows, HEAD_DIM), BF16),
                vmem((2, width, HEAD_DIM), BF16),
                vmem((members, HEAD_DIM, 2 * rows), BF16),
                vmem((members, groups, 8, 128), F32),
                vmem((members, 2 * rows, width), BF16),
                vmem((members, groups, 8, width), F32),
                vmem((members, groups, 8, width), F32),
                vmem((6, members, 8, width), F32),
                stat,
                stat,
                *side,
                vmem((members, 2, rows, HEAD_DIM), BF16),
                vmem((members, 2, rows, HEAD_DIM), BF16),
                vmem((slots, 2, rows, HEAD_DIM), BF16),
                vmem((2, 2, rows, HEAD_DIM), BF16),
                vmem((2, rows, HEAD_DIM), F32),
                vmem((2, rows, HEAD_DIM), F32),
                dma((2,)),
                dma((1,)),
                dma((1,)),
                dma((members,)),
                dma((slots,)),
                dma((2,)),
                *([dma((2,))] if in_line else []),
                dma((1,)),
                dma((1,)),
                *([dma((1,))] if in_line else []),
                dma((members,)),
                dma((2,)),
            ],
            compiler_params=pltpu.CompilerParams(collective_id=0, has_side_effects=True),
        )(text_count, query_source, key_source, query_edit, key_edit)
        return pl.pallas_call(
            put_out,
            out_shape=(pltpu.HBM((rows, full), F32),) * 2,
            in_specs=[pl.BlockSpec(memory_space=pltpu.VMEM)] * 2,
            out_specs=(pl.BlockSpec(memory_space=pltpu.HBM),) * 2,
            scratch_shapes=[dma((2,))],
        )(*(pltpu.with_memory_space_constraint(g, pltpu.VMEM) for g in grads))

    spec = P(("req", "ctx"), None)
    return jax.shard_map(
        local, mesh=mesh, in_specs=(spec,) * 4 + (P("req"),), out_specs=(spec, spec), check_vma=False
    )
```

```python
import functools
import math

import jax
import jax.numpy as jnp
from jax import lax
from jax.experimental import pallas as pl
from jax.experimental.pallas import tpu as pltpu
from jax.sharding import PartitionSpec as P

HEAD_DIM = 128
MASKED = -1e30
F32 = jnp.float32
BF16 = jnp.bfloat16


def kernel(
    chips,
    count_hbm, qs_hbm, ks_hbm, qe_hbm, ke_hbm,
    qg_ref, kg_ref,
    count_ref, krecv, kother, qrecv, qother, qcat, kturn, bias_ref, grad_buf, e_buf, s_buf, stats_ref,
    st_send, st_recv,
    kg_send, kg_recv, qg_send, qg_recv, qg_own, kg_own,
    load_sem, ksend_sem, near_sem, krecv_sem, qrecv_sem, st_sems,
    kgsend_sem, gnear_sem, kgrecv_sem, qgrecv_sem,
):
    members = chips // 2
    rows = kother.shape[1]
    pair_rows = 2 * rows
    width = 2 * pair_rows
    head = pair_rows // 128 * 128
    tail = pair_rows - head
    groups = pair_rows // 8
    all_rows = rows * chips * 2
    text_slots = min(512, all_rows // 4)
    scale = 1.0 / math.sqrt(HEAD_DIM)
    power_scale = scale * math.log2(math.e)
    weight = 4.0 * all_rows * math.sqrt(all_rows)
    me = lax.axis_index("ctx")
    chip, core = me // 2, me % 2
    other = 1 - core
    group, member = chip // members, chip % members

    def chip_of(g, m):
        return g * members + m

    def dev(g, m, c):
        return {"ctx": chip_of(g, m) * 2 + c}

    def shifted(d):
        if members % 2:
            return (member + d) % members
        return (member // 2 + d // 2) % (members // 2) * 2 + (member + d) % 2

    def sender(d):
        if members % 2:
            return (member + members - d) % members
        return (member // 2 + members - d // 2) % (members // 2) * 2 + (member + d) % 2

    def each(n, body, init):
        if n <= 8:
            for i in range(n):
                init = body(i, init)
            return init
        return lax.fori_loop(0, n, body, init)

    def wait(ref, sem):
        pltpu.make_async_copy(ref, ref, sem).wait()

    def keys(m, c):
        return krecv.at[m, :, pl.ds(pl.multiple_of(c * rows, 8), rows)]

    def chips_keys(m):
        return krecv.at[m, :, 0:pair_rows]

    own_cols = pl.ds(pl.multiple_of(core * HEAD_DIM, HEAD_DIM), HEAD_DIM)
    other_cols = pl.ds(pl.multiple_of(other * HEAD_DIM, HEAD_DIM), HEAD_DIM)
    loads = []
    for i, (src, dst_own, dst_other) in enumerate((
        (qs_hbm, qrecv.at[0, core, 0], qother.at[0]),
        (qe_hbm, qrecv.at[0, core, 1], qother.at[1]),
        (ks_hbm, keys(member, core).at[0], kother.at[0]),
        (ke_hbm, keys(member, core).at[1], kother.at[1]),
    )):
        loads.append(pltpu.make_async_copy(src.at[:, own_cols], dst_own, load_sem.at[0]))
        loads.append(pltpu.make_async_copy(src.at[:, other_cols], dst_other, load_sem.at[0]))
    count_load = pltpu.make_async_copy(count_hbm, count_ref, load_sem.at[1])
    for load in loads:
        load.start()
    count_load.start()

    barrier = pltpu.get_barrier_semaphore()

    def greet(d, carry):
        for c in (0, 1):
            pl.semaphore_signal(barrier, inc=1, device_id=dev(group, shifted(d + 1), c))
        return carry

    for c in (0, 1):
        pl.semaphore_signal(barrier, inc=1, device_id=dev(1 - group, member, c))
    pl.semaphore_signal(barrier, inc=1, device_id=dev(group, member, other))
    each(members - 1, greet, 0)
    pl.semaphore_wait(barrier, 2 * members + 1)
    wait(chips_keys(slice(0, 2)), load_sem.at[0])
    count_load.wait()

    def key_copy(m, c, same, sem):
        return pltpu.make_async_remote_copy(
            src_ref=keys(member, core) if same else kother,
            dst_ref=keys(member, core),
            send_sem=sem,
            recv_sem=krecv_sem.at[member],
            device_id=dev(group, m, c),
        )

    def query_copy(r, c, same):
        return pltpu.make_async_remote_copy(
            src_ref=qrecv.at[0, core] if same else qother,
            dst_ref=qrecv.at[r, core],
            send_sem=near_sem.at[0],
            recv_sem=qrecv_sem.at[r],
            device_id=dev(1 - group if r else group, member, c),
        )

    query_copy(1, core, True).start()
    query_copy(1, other, False).start()

    def send_keys(d, carry):
        m = shifted(members - 1 - d)
        key_copy(m, core, True, ksend_sem.at[0]).start()
        key_copy(m, other, False, ksend_sem.at[0]).start()
        return carry

    send_keys(0, 0)
    query_copy(0, other, False).start()
    key_copy(member, other, False, near_sem.at[0]).start()
    if members > 2:
        each(members - 2, lambda d, carry: send_keys(d + 1, carry), 0)

    count = count_ref[0]

    def valid(positions):
        return (positions >= text_slots) | (positions < count)

    lane = lax.broadcasted_iota(jnp.int32, (1, width), 1)
    in_tail = lane >= 2 * head
    spot = jnp.where(in_tail, lane - 2 * head, lane)
    half = jnp.where(in_tail, tail, head)
    far = spot >= half
    spot = jnp.where(far, spot - half, spot) + jnp.where(in_tail, head, 0)
    row_place = jnp.where(far, chip_of(1 - group, member), chip) * pair_rows + spot
    row_weight = jnp.where(valid(row_place), 2.0 * weight, 0.0)

    def place_queries(r):
        for which in (0, 1):
            joined = jnp.concatenate([qrecv[r, c, which].astype(F32) for c in (0, 1)], axis=0)
            joined = joined.astype(BF16)
            qcat[which, r * head:(r + 1) * head] = joined[:head]
            if tail:
                at = 2 * head + r * tail
                qcat[which, at:at + tail] = joined[head:]

    def fill_bias(d, carry):
        place = chip_of(group, sender(d)) * pair_rows
        place += lax.broadcasted_iota(jnp.int32, (pair_rows, 128), 0)
        bias_ref[d] = jnp.where(valid(place), 0.0, MASKED).reshape(groups, 8, 128)
        return carry

    each(members, fill_bias, 0)

    def powers(d, m, which, lanes):
        span = lanes.stop - lanes.start
        scores = lax.dot_general(
            krecv[m, which, 0:pair_rows], qcat[which, lanes], (((1,), (1,)), ((), ())),
            preferred_element_type=F32,
        ).reshape(groups, 8, span)
        bias = bias_ref[d]
        scores = jnp.concatenate([
            scores[:, :, i:min(i + 128, span)] + bias[:, :, :min(128, span - i)]
            for i in range(0, span, 128)
        ], axis=2)
        top = jnp.max(scores, axis=0)
        return top, jnp.exp2((scores - top[None]) * power_scale)

    def score_chunk(d, m, lanes):
        m_s, s_pow = powers(d, m, 0, lanes)
        m_e, e_pow = powers(d, m, 1, lanes)
        s_buf[d, :, :, lanes] = s_pow
        e_buf[d, :, :, lanes] = e_pow
        for i, value in enumerate((
            m_e, jnp.sum(e_pow, axis=0), m_s, jnp.sum(s_pow, axis=0),
            jnp.sum(e_pow * e_pow, axis=0), jnp.sum(e_pow * s_pow, axis=0),
        )):
            stats_ref[i, d, :, lanes] = value

    early, late, full = slice(0, head), slice(head, width), slice(0, width)
    wait(qrecv.at[0, 0], qrecv_sem.at[0])
    wait(kother, krecv_sem.at[member])
    place_queries(0)
    ahead = 2 if members == 4 else 1
    for d in range(ahead):
        m = shifted(d) if d else member
        if d:
            wait(chips_keys(m), krecv_sem.at[m])
        if head:
            score_chunk(d, m, early)
    wait(qrecv.at[1], qrecv_sem.at[1])
    place_queries(1)
    for d in range(ahead):
        score_chunk(d, shifted(d) if d else member, late)

    def far_scores(d, carry):
        d = members - 1 - d
        m = sender(d)
        wait(chips_keys(m), krecv_sem.at[m])
        score_chunk(d, m, full)
        return carry

    each(members - ahead, far_scores, 0)

    def fold(op, value):
        return op(op(value, axis=0), axis=0, keepdims=True)

    tops_e, tops_s = stats_ref[0], stats_ref[2]
    m_e, m_s = fold(jnp.max, tops_e), fold(jnp.max, tops_s)
    f_e = jnp.exp2((tops_e - m_e) * power_scale)
    f_s = jnp.exp2((tops_s - m_s) * power_scale)
    stats = (
        m_e, fold(jnp.sum, stats_ref[1] * f_e),
        m_s, fold(jnp.sum, stats_ref[3] * f_s),
        fold(jnp.sum, stats_ref[4] * (f_e * f_e)),
        fold(jnp.sum, stats_ref[5] * (f_e * f_s)),
    )
    packed = jnp.concatenate(stats + (jnp.zeros((2, width), F32),), axis=0)
    st_send[:, :head] = packed[:, head:2 * head]
    st_send[:, head:2 * head] = packed[:, :head]
    if tail:
        st_send[:, 2 * head:] = jnp.concatenate(
            [packed[:, 2 * head + tail:], packed[:, 2 * head:2 * head + tail]], axis=1
        )
    stat_copy = pltpu.make_async_remote_copy(
        src_ref=st_send, dst_ref=st_recv, send_sem=st_sems.at[0], recv_sem=st_sems.at[1],
        device_id=dev(1 - group, member, core),
    )
    stat_copy.start()

    def turn_keys(d, carry):
        m = sender(d)
        kturn[d] = krecv[m, 1, 0:pair_rows].astype(F32).T.astype(BF16)
        return carry

    each(members, turn_keys, 0)

    stat_copy.wait_recv()
    m_e1, l_e1, m_s1, l_s1, sq1, cr1 = stats
    m_e2, l_e2, m_s2, l_s2, sq2, cr2 = (st_recv[i:i + 1] for i in range(6))
    m_e, m_s = jnp.maximum(m_e1, m_e2), jnp.maximum(m_s1, m_s2)
    fe1, fe2 = jnp.exp2((m_e1 - m_e) * power_scale), jnp.exp2((m_e2 - m_e) * power_scale)
    fs1, fs2 = jnp.exp2((m_s1 - m_s) * power_scale), jnp.exp2((m_s2 - m_s) * power_scale)
    inv_e = 1.0 / (l_e1 * fe1 + l_e2 * fe2)
    inv_s = 1.0 / (l_s1 * fs1 + l_s2 * fs2)
    sq = sq1 * fe1 * fe1 + sq2 * fe2 * fe2
    cr = cr1 * fe1 * fs1 + cr2 * fe2 * fs2
    stats_ref[1] = f_e * (fe1 * inv_e)
    stats_ref[3] = f_s * (fs1 * inv_s)
    delta = row_weight * (sq * inv_e * inv_e - cr * inv_e * inv_s)

    def kg_copy(m, c, sem):
        return pltpu.make_async_remote_copy(
            src_ref=kg_send.at[m, c], dst_ref=kg_recv.at[member, core],
            send_sem=sem, recv_sem=kgrecv_sem.at[member],
            device_id=dev(group, m, c),
        )

    def qg_copy(r, c):
        return pltpu.make_async_remote_copy(
            src_ref=qg_send.at[r, c], dst_ref=qg_recv.at[r, core],
            send_sem=gnear_sem.at[0], recv_sem=qgrecv_sem.at[r],
            device_id=dev(1 - group if r else group, member, c),
        )

    q_edit = qcat[1]

    def grad_chunk(d):
        prob_e = e_buf[d] * stats_ref[1, d][None]
        prob_s = s_buf[d] * stats_ref[3, d][None]
        grad = prob_e * (row_weight[None] * (prob_e - prob_s) - delta[None])
        grad = grad.reshape(pair_rows, width).astype(BF16)
        grad_buf[d] = grad
        return jnp.dot(grad, q_edit, preferred_element_type=F32) * scale

    def far_grad(i, carry):
        d = (2, 3, 1)[i] if members == 4 else members - 1 - i
        m = sender(d)
        k_part = grad_chunk(d)
        for c in (0, 1):
            kg_send[m, c] = k_part[c * rows:(c + 1) * rows].astype(BF16)
        for c in (core, other):
            kg_copy(m, c, kgsend_sem.at[0]).start()
        return carry

    each(members - 1, far_grad, 0)
    k_part = grad_chunk(0)
    for c in (0, 1):
        kg_own[c] = k_part[c * rows:(c + 1) * rows]
        kg_send[member, c] = k_part[c * rows:(c + 1) * rows].astype(BF16)

    q_total = each(
        members,
        lambda d, q: q + jnp.dot(kturn[d], grad_buf[d], preferred_element_type=F32),
        jnp.zeros((HEAD_DIM, width), F32),
    )
    q_rows = q_total.T * scale
    for r in (1, 0):
        joined = [q_rows[r * head:(r + 1) * head]]
        if tail:
            at = 2 * head + r * tail
            joined.append(q_rows[at:at + tail])
        joined = jnp.concatenate(joined, axis=0)
        for c in (0, 1):
            part = joined[c * rows:(c + 1) * rows]
            if not r:
                qg_own[c] = part
            qg_send[r, c] = part.astype(BF16)
        if r:
            qg_copy(1, core).start()
            qg_copy(1, other).start()
    qg_copy(0, other).start()
    kg_copy(member, other, gnear_sem.at[0]).start()

    def put(ref, mine, theirs):
        ref[:, own_cols] = mine
        ref[:, other_cols] = theirs

    wait(kg_recv.at[member, 0], kgrecv_sem.at[member])

    def add_far(d, sums):
        mine, theirs = sums
        m = shifted(d + 1)
        wait(kg_recv.at[m], kgrecv_sem.at[m])
        return mine + kg_recv[m, core].astype(F32), theirs + kg_recv[m, other].astype(F32)

    sums = each(members - 1, add_far, (kg_own[core], kg_recv[member, other].astype(F32)))
    put(kg_ref, *sums)

    wait(qg_recv.at[0, 0], qgrecv_sem.at[0])
    wait(qg_recv.at[1], qgrecv_sem.at[1])
    put(
        qg_ref,
        qg_own[core] + qg_recv[1, core].astype(F32),
        qg_recv[0, other].astype(F32) + qg_recv[1, other].astype(F32),
    )

    wait(chips_keys(slice(0, members - 1)), ksend_sem.at[0])
    wait(qrecv, near_sem.at[0])
    stat_copy.wait_send()
    wait(kg_send.at[0:members - 1], kgsend_sem.at[0])
    wait(qg_send, gnear_sem.at[0])


def line_kernel(
    chips,
    count_hbm, qs_hbm, ks_hbm, qe_hbm, ke_hbm,
    qg_ref, kg_ref,
    count_ref, krecv, kother, qrecv, qother, qcat, kturn, bias_ref, grad_buf, e_buf, s_buf, stats_ref,
    st_send, st_recv,
    st_side, st_turn, kg_send, kg_recv, qg_send, qg_recv, qg_own, kg_own,
    load_sem, ksend_sem, near_sem, krecv_sem, qrecv_sem, st_sems, side_sems,
    kgsend_sem, gnear_sem, gfar_sem, kgrecv_sem, qgrecv_sem,
):
    members = chips // 2
    rows = kother.shape[1]
    pair_rows = 2 * rows
    head = pair_rows // 128 * 128
    tail = pair_rows - head
    width = qcat.shape[1]
    blocks = {0: 0, 1: width - head, 2: width - 2 * head}
    groups = pair_rows // 8
    all_rows = rows * chips * 2
    text_slots = min(512, all_rows // 4)
    scale = 1.0 / math.sqrt(HEAD_DIM)
    power_scale = scale * math.log2(math.e)
    weight = 4.0 * all_rows * math.sqrt(all_rows)
    me = lax.axis_index("ctx")
    chip, core = me // 2, me % 2
    other = 1 - core
    group, member = chip // members, chip % members
    inner = (group + member // 2) % 2 == 1
    outer = (group + member // 2) % 2 == 0
    target = (2 - group) * 2 + chip % 2

    def chip_of(g, m):
        return g * members + m

    def dev(g, m, c):
        return {"ctx": chip_of(g, m) * 2 + c}

    def shifted(d):
        if members % 2:
            return (member + d) % members
        return (member // 2 + d // 2) % (members // 2) * 2 + (member + d) % 2

    def sender(d):
        if members % 2:
            return (member + members - d) % members
        return (member // 2 + members - d // 2) % (members // 2) * 2 + (member + d) % 2

    def each(n, body, init):
        if n <= 8:
            for i in range(n):
                init = body(i, init)
            return init
        return lax.fori_loop(0, n, body, init)

    def wait(ref, sem):
        pltpu.make_async_copy(ref, ref, sem).wait()

    def keys(m, c):
        return krecv.at[m, :, pl.ds(pl.multiple_of(c * rows, 8), rows)]

    def chips_keys(m):
        return krecv.at[m, :, 0:pair_rows]

    own_head = (core + group) % 2
    own_cols = pl.ds(pl.multiple_of(own_head * HEAD_DIM, HEAD_DIM), HEAD_DIM)
    other_cols = pl.ds(pl.multiple_of((1 - own_head) * HEAD_DIM, HEAD_DIM), HEAD_DIM)
    loads = []
    for i, (src, dst_own, dst_other) in enumerate((
        (qs_hbm, qrecv.at[0, core, 0], qother.at[0]),
        (qe_hbm, qrecv.at[0, core, 1], qother.at[1]),
        (ks_hbm, keys(member, core).at[0], kother.at[0]),
        (ke_hbm, keys(member, core).at[1], kother.at[1]),
    )):
        loads.append(pltpu.make_async_copy(src.at[:, own_cols], dst_own, load_sem.at[0]))
        loads.append(pltpu.make_async_copy(src.at[:, other_cols], dst_other, load_sem.at[0]))
    count_load = pltpu.make_async_copy(count_hbm, count_ref, load_sem.at[1])
    for load in loads:
        load.start()
    count_load.start()

    barrier = pltpu.get_barrier_semaphore()

    for c in (0, 1):
        pl.semaphore_signal(barrier, inc=1, device_id=dev(1 - group, member, c))

    @pl.when(inner)
    def _():
        for c in (0, 1):
            pl.semaphore_signal(barrier, inc=1, device_id={"ctx": target * 2 + c})

    for d in (3, 2, 1):
        for c in (0, 1):
            pl.semaphore_signal(barrier, inc=1, device_id=dev(group, shifted(d), c))
    pl.semaphore_signal(barrier, inc=1, device_id=dev(group, member, other))
    qcat[...] = jnp.zeros_like(qcat)
    pl.semaphore_wait(barrier, jnp.where(inner, 2 * members + 3, 2 * members + 1))
    wait(chips_keys(slice(0, 2)), load_sem.at[0])
    count_load.wait()

    def key_copy(m, c, same, sem):
        return pltpu.make_async_remote_copy(
            src_ref=keys(member, core) if same else kother,
            dst_ref=keys(member, core),
            send_sem=sem,
            recv_sem=krecv_sem.at[member],
            device_id=dev(group, m, c),
        )

    far_slot = jnp.where(inner, 1, 2)

    def query_copy(far, c, same):
        slot = far_slot if far else 0
        return pltpu.make_async_remote_copy(
            src_ref=qrecv.at[0, core] if same else qother,
            dst_ref=qrecv.at[slot, core],
            send_sem=near_sem.at[0],
            recv_sem=qrecv_sem.at[slot],
            device_id={"ctx": target * 2 + c} if far else dev(group, member, c),
        )

    def send_keys(d):
        key_copy(shifted(d), core, True, ksend_sem.at[0]).start()
        key_copy(shifted(d), other, False, ksend_sem.at[0]).start()

    query_copy(1, other, True).start()
    query_copy(1, core, False).start()
    query_copy(0, other, False).start()
    key_copy(member, other, False, near_sem.at[0]).start()
    send_keys(3)
    send_keys(2)
    send_keys(1)

    count = count_ref[0]

    def valid(positions):
        return (positions >= text_slots) | (positions < count)

    lane = lax.broadcasted_iota(jnp.int32, (1, width), 1)
    own_lane = lane < head
    row_place = chip * pair_rows + lane
    live = own_lane
    for slot, owner in ((0, chip), (1, target), (2, chip_of(1 - group, member))):
        there = lane >= head + slot * tail
        there = there & (lane < head + (slot + 1) * tail)
        row_place = jnp.where(there, owner * pair_rows + lane - slot * tail, row_place)
        if slot:
            at = blocks[slot]
            ahead = (lane >= at) & (lane < at + head)
            row_place = jnp.where(ahead, owner * pair_rows + lane - at, row_place)
            there = (there | ahead) & inner
        live = live | there
    row_weight = jnp.where(live & valid(row_place), 2.0 * weight, 0.0)

    @pl.when(outer)
    def _():
        for buf in (e_buf, s_buf):
            buf[:, :, :, width - 2 * head:] = jnp.zeros((members, groups, 8, 2 * head), F32)

    def place_queries(slot):
        for which in (0, 1):
            joined = jnp.concatenate([qrecv[slot, c, which].astype(F32) for c in (0, 1)], axis=0)
            joined = joined.astype(BF16)
            qcat[which, blocks[slot]:blocks[slot] + head] = joined[:head]
            if tail:
                at = head + slot * tail
                qcat[which, at:at + tail] = joined[head:]

    def fill_bias(d, carry):
        place = chip_of(group, sender(d)) * pair_rows
        place += lax.broadcasted_iota(jnp.int32, (pair_rows, 128), 0)
        bias_ref[d] = jnp.where(valid(place), 0.0, MASKED).reshape(groups, 8, 128)
        return carry

    each(members, fill_bias, 0)

    def powers(d, m, which, lanes):
        span = lanes.stop - lanes.start
        scores = lax.dot_general(
            krecv[m, which, 0:pair_rows], qcat[which, lanes], (((1,), (1,)), ((), ())),
            preferred_element_type=F32,
        ).reshape(groups, 8, span)
        bias = bias_ref[d]
        scores = jnp.concatenate([
            scores[:, :, i:min(i + 128, span)] + bias[:, :, :min(128, span - i)]
            for i in range(0, span, 128)
        ], axis=2)
        top = jnp.max(scores, axis=0)
        return top, jnp.exp2((scores - top[None]) * power_scale)

    def score_chunk(d, m, lanes):
        m_s, s_pow = powers(d, m, 0, lanes)
        m_e, e_pow = powers(d, m, 1, lanes)
        s_buf[d, :, :, lanes] = s_pow
        e_buf[d, :, :, lanes] = e_pow
        for i, value in enumerate((
            m_e, jnp.sum(e_pow, axis=0), m_s, jnp.sum(s_pow, axis=0),
            jnp.sum(e_pow * e_pow, axis=0), jnp.sum(e_pow * s_pow, axis=0),
        )):
            stats_ref[i, d, :, lanes] = value

    own, late = slice(0, head), slice(head, width - head)
    side, full, both = slice(width - head, width), slice(0, width), slice(0, width - 2 * head)

    def keys_from(d):
        m = sender(d)
        wait(chips_keys(m), krecv_sem.at[m])
        return m

    wait(qrecv.at[0, 0], qrecv_sem.at[0])
    wait(kother, krecv_sem.at[member])
    place_queries(0)

    @pl.when(outer)
    def _():
        score_chunk(0, member, both)
        for d in (1, 3, 2):
            score_chunk(d, keys_from(d), both)

    @pl.when(inner)
    def _():
        for slot in (1, 2):
            wait(qrecv.at[slot], qrecv_sem.at[slot])
        for slot in (1, 2):
            place_queries(slot)
        score_chunk(0, member, full)
        score_chunk(1, keys_from(1), full)
        for d in (3, 2):
            keys_from(d)
        for d in (3, 2):
            score_chunk(d, sender(d), full)

    def fold(op, value):
        return op(op(value, axis=0), axis=0, keepdims=True)

    tops_e, tops_s = stats_ref[0], stats_ref[2]
    m_e, m_s = fold(jnp.max, tops_e), fold(jnp.max, tops_s)
    f_e = jnp.exp2((tops_e - m_e) * power_scale)
    f_s = jnp.exp2((tops_s - m_s) * power_scale)
    stats = (
        m_e, fold(jnp.sum, stats_ref[1] * f_e),
        m_s, fold(jnp.sum, stats_ref[3] * f_s),
        fold(jnp.sum, stats_ref[4] * (f_e * f_e)),
        fold(jnp.sum, stats_ref[5] * (f_e * f_s)),
    )
    packed = jnp.concatenate(stats + (jnp.zeros((2, width), F32),), axis=0)
    span = width - 3 * head
    tails = packed[:, head:head + span]
    st_send[:, :head] = jnp.where(inner, packed[:, blocks[2]:blocks[2] + head], packed[:, :head])
    st_send[:, head:] = jnp.where(
        inner, pltpu.roll(tails, span - 2 * tail, 1), pltpu.roll(tails, 2 * tail, 1)
    )
    stat_copy = pltpu.make_async_remote_copy(
        src_ref=st_send, dst_ref=st_recv, send_sem=st_sems.at[0], recv_sem=st_sems.at[1],
        device_id=dev(1 - group, member, other),
    )
    side_copy = pltpu.make_async_remote_copy(
        src_ref=st_side, dst_ref=st_turn, send_sem=side_sems.at[0], recv_sem=side_sems.at[1],
        device_id={"ctx": target * 2 + other},
    )

    @pl.when(inner)
    def _():
        st_side[:, :head] = packed[:, blocks[1]:]
        st_side[:, head:2 * head] = packed[:, :head]
        tail_lane = lax.broadcasted_iota(jnp.int32, (8, span), 1)
        st_side[:, 2 * head:] = jnp.where(
            tail_lane < tail, pltpu.roll(tails, span - tail, 1), pltpu.roll(tails, tail, 1)
        )
        side_copy.start()

    stat_copy.start()

    def turn_keys(d, carry):
        m = sender(d)
        kturn[d] = krecv[m, 1, 0:pair_rows].astype(F32).T.astype(BF16)
        return carry

    each(members, turn_keys, 0)

    @pl.when(inner)
    def _():
        side_copy.wait_recv()

    stat_copy.wait_recv()
    there, turned = st_recv[...], st_turn[...]
    tail_lane = lax.broadcasted_iota(jnp.int32, (8, span), 1)
    second = jnp.concatenate([
        jnp.where(inner, turned[:, :head], there[:, :head]),
        jnp.where(inner & (tail_lane < 2 * tail), turned[:, 2 * head:], there[:, head:]),
        there[:, :head],
        turned[:, head:2 * head],
    ], axis=1)
    m_e1, l_e1, m_s1, l_s1, sq1, cr1 = stats
    m_e2, l_e2, m_s2, l_s2, sq2, cr2 = (second[i:i + 1] for i in range(6))
    m_e, m_s = jnp.maximum(m_e1, m_e2), jnp.maximum(m_s1, m_s2)
    fe1, fe2 = jnp.exp2((m_e1 - m_e) * power_scale), jnp.exp2((m_e2 - m_e) * power_scale)
    fs1, fs2 = jnp.exp2((m_s1 - m_s) * power_scale), jnp.exp2((m_s2 - m_s) * power_scale)
    inv_e = 1.0 / (l_e1 * fe1 + l_e2 * fe2)
    inv_s = 1.0 / (l_s1 * fs1 + l_s2 * fs2)
    sq = sq1 * fe1 * fe1 + sq2 * fe2 * fe2
    cr = cr1 * fe1 * fs1 + cr2 * fe2 * fs2
    stats_ref[1] = jnp.where(live, f_e * (fe1 * inv_e), 0.0)
    stats_ref[3] = jnp.where(live, f_s * (fs1 * inv_s), 0.0)
    delta = jnp.where(live, row_weight * (sq * inv_e * inv_e - cr * inv_e * inv_s), 0.0)

    def kg_copy(m, c, sem):
        return pltpu.make_async_remote_copy(
            src_ref=kg_send.at[m, c], dst_ref=kg_recv.at[member, core],
            send_sem=sem, recv_sem=kgrecv_sem.at[member],
            device_id=dev(group, m, c),
        )

    def qg_copy(slot, c):
        return pltpu.make_async_remote_copy(
            src_ref=qg_send.at[slot, c], dst_ref=qg_recv.at[1 if slot else 0, core],
            send_sem=gfar_sem.at[0] if slot else gnear_sem.at[0],
            recv_sem=qgrecv_sem.at[1 if slot else 0],
            device_id=(dev(group, member, c), {"ctx": target * 2 + c}, dev(1 - group, member, c))[slot],
        )

    q_edit = qcat[1]

    def grad_chunk(d):
        prob_e = e_buf[d] * stats_ref[1, d][None]
        prob_s = s_buf[d] * stats_ref[3, d][None]
        grad = prob_e * (row_weight[None] * (prob_e - prob_s) - delta[None])
        grad = grad.reshape(pair_rows, width).astype(BF16)
        grad_buf[d] = grad
        return jnp.dot(grad, q_edit, preferred_element_type=F32) * scale

    def far_grad(i, carry):
        d = (2, 3, 1)[i] if members == 4 else members - 1 - i
        m = sender(d)
        k_part = grad_chunk(d)
        for c in (0, 1):
            kg_send[m, c] = k_part[c * rows:(c + 1) * rows].astype(BF16)
        for c in (core, other):
            kg_copy(m, c, kgsend_sem.at[0]).start()
        return carry

    each(members - 1, far_grad, 0)
    k_part = grad_chunk(0)
    for c in (0, 1):
        kg_own[c] = k_part[c * rows:(c + 1) * rows]
        kg_send[member, c] = k_part[c * rows:(c + 1) * rows].astype(BF16)

    q_total = each(
        members,
        lambda d, q: q + jnp.dot(kturn[d], grad_buf[d], preferred_element_type=F32),
        jnp.zeros((HEAD_DIM, width), F32),
    )
    q_rows = q_total.T * scale
    for slot in (2, 1, 0):
        joined = [q_rows[blocks[slot]:blocks[slot] + head]]
        if tail:
            at = head + slot * tail
            joined.append(q_rows[at:at + tail])
        joined = jnp.concatenate(joined, axis=0)
        for c in (0, 1):
            part = joined[c * rows:(c + 1) * rows]
            if not slot:
                qg_own[c] = part
            qg_send[slot, c] = part.astype(BF16)

    @pl.when(inner)
    def _():
        for slot in (2, 1):
            qg_copy(slot, core).start()
            qg_copy(slot, other).start()

    qg_copy(0, other).start()
    kg_copy(member, other, gnear_sem.at[0]).start()

    def put(ref, mine, theirs):
        ref[:, own_cols] = mine
        ref[:, other_cols] = theirs

    wait(kg_recv.at[member, 0], kgrecv_sem.at[member])

    def add_far(d, sums):
        mine, theirs = sums
        m = shifted(d + 1)
        wait(kg_recv.at[m], kgrecv_sem.at[m])
        return mine + kg_recv[m, core].astype(F32), theirs + kg_recv[m, other].astype(F32)

    sums = each(members - 1, add_far, (kg_own[core], kg_recv[member, other].astype(F32)))
    put(kg_ref, *sums)

    wait(qg_recv.at[0, 0], qgrecv_sem.at[0])
    wait(qg_recv.at[1], qgrecv_sem.at[1])
    put(
        qg_ref,
        qg_own[core] + qg_recv[1, other].astype(F32),
        qg_recv[0, other].astype(F32) + qg_recv[1, core].astype(F32),
    )

    wait(chips_keys(slice(0, members - 1)), ksend_sem.at[0])
    wait(qrecv.at[0:2], near_sem.at[0])
    stat_copy.wait_send()
    wait(kg_send.at[0:members - 1], kgsend_sem.at[0])
    wait(qg_send.at[0], gnear_sem.at[0])

    @pl.when(inner)
    def _():
        wait(qg_send.at[1:3], gfar_sem.at[0])
        side_copy.wait_send()


def put_out(qg_vmem, kg_vmem, qg_hbm, kg_hbm, sems):
    copies = (
        pltpu.make_async_copy(qg_vmem, qg_hbm, sems.at[0]),
        pltpu.make_async_copy(kg_vmem, kg_hbm, sems.at[1]),
    )
    for copy in copies:
        copy.start()
    for copy in copies:
        copy.wait()


def solution(mesh):
    chips = mesh.shape["ctx"] // 2
    members = chips // 2

    def local(query_source, key_source, query_edit, key_edit, text_count):
        rows, full = query_source.shape
        width = 4 * rows
        groups = 2 * rows // 8
        dma = pltpu.SemaphoreType.DMA
        vmem = pltpu.VMEM
        in_line = chips == 8
        if in_line:
            pair = 2 * rows
            head = pair // 128 * 128
            width = 3 * head + -(-3 * (pair - head) // 128) * 128
        slots = 3 if in_line else 2
        stat = vmem((8, width - 2 * head if in_line else width), F32)
        side = [vmem((8, width - head), F32)] * 2 if in_line else []
        grads = pl.pallas_call(
            functools.partial(line_kernel if in_line else kernel, chips),
            out_shape=(
                pltpu.VMEM((rows, full), F32),
                pltpu.VMEM((rows, full), F32),
            ),
            in_specs=[pl.BlockSpec(memory_space=pltpu.HBM)] * 5,
            out_specs=(pl.BlockSpec(memory_space=pltpu.VMEM),) * 2,
            scratch_shapes=[
                pltpu.SMEM((1,), jnp.int32),
                vmem((members, 2, 2 * rows + 8, HEAD_DIM), BF16),
                vmem((2, rows, HEAD_DIM), BF16),
                vmem((slots, 2, 2, rows, HEAD_DIM), BF16),
                vmem((2, rows, HEAD_DIM), BF16),
                vmem((2, width, HEAD_DIM), BF16),
                vmem((members, HEAD_DIM, 2 * rows), BF16),
                vmem((members, groups, 8, 128), F32),
                vmem((members, 2 * rows, width), BF16),
                vmem((members, groups, 8, width), F32),
                vmem((members, groups, 8, width), F32),
                vmem((6, members, 8, width), F32),
                stat,
                stat,
                *side,
                vmem((members, 2, rows, HEAD_DIM), BF16),
                vmem((members, 2, rows, HEAD_DIM), BF16),
                vmem((slots, 2, rows, HEAD_DIM), BF16),
                vmem((2, 2, rows, HEAD_DIM), BF16),
                vmem((2, rows, HEAD_DIM), F32),
                vmem((2, rows, HEAD_DIM), F32),
                dma((2,)),
                dma((1,)),
                dma((1,)),
                dma((members,)),
                dma((slots,)),
                dma((2,)),
                *([dma((2,))] if in_line else []),
                dma((1,)),
                dma((1,)),
                *([dma((1,))] if in_line else []),
                dma((members,)),
                dma((2,)),
            ],
            compiler_params=pltpu.CompilerParams(collective_id=0, has_side_effects=True),
        )(text_count, query_source, key_source, query_edit, key_edit)
        return pl.pallas_call(
            put_out,
            out_shape=(pltpu.HBM((rows, full), F32),) * 2,
            in_specs=[pl.BlockSpec(memory_space=pltpu.VMEM)] * 2,
            out_specs=(pl.BlockSpec(memory_space=pltpu.HBM),) * 2,
            scratch_shapes=[dma((2,))],
        )(*(pltpu.with_memory_space_constraint(g, pltpu.VMEM) for g in grads))

    spec = P(("req", "ctx"), None)
    return jax.shard_map(
        local, mesh=mesh, in_specs=(spec,) * 4 + (P("req"),), out_specs=(spec, spec), check_vma=False
    )
```

```python
import functools
import math

import jax
import jax.numpy as jnp
from jax import lax
from jax.experimental import pallas as pl
from jax.experimental.pallas import tpu as pltpu
from jax.sharding import PartitionSpec as P

HEAD_DIM = 128
MASKED = -1e30
F32 = jnp.float32
BF16 = jnp.bfloat16


def kernel(
    chips,
    count_hbm, qs_hbm, ks_hbm, qe_hbm, ke_hbm,
    qg_ref, kg_ref,
    count_ref, krecv, kother, qrecv, qother, qcat, kturn, bias_ref, grad_buf, e_buf, s_buf, stats_ref,
    st_send, st_recv,
    kg_send, kg_recv, qg_send, qg_recv, qg_own, kg_own,
    load_sem, ksend_sem, near_sem, krecv_sem, qrecv_sem, st_sems,
    kgsend_sem, gnear_sem, kgrecv_sem, qgrecv_sem,
):
    members = chips // 2
    rows = kother.shape[1]
    pair_rows = 2 * rows
    width = 2 * pair_rows
    head = pair_rows // 128 * 128
    tail = pair_rows - head
    groups = pair_rows // 8
    all_rows = rows * chips * 2
    text_slots = min(512, all_rows // 4)
    scale = 1.0 / math.sqrt(HEAD_DIM)
    power_scale = scale * math.log2(math.e)
    weight = 4.0 * all_rows * math.sqrt(all_rows)
    me = lax.axis_index("ctx")
    chip, core = me // 2, me % 2
    other = 1 - core
    group, member = chip // members, chip % members

    def chip_of(g, m):
        return g * members + m

    def dev(g, m, c):
        return {"ctx": chip_of(g, m) * 2 + c}

    def shifted(d):
        if members % 2:
            return (member + d) % members
        return (member // 2 + d // 2) % (members // 2) * 2 + (member + d) % 2

    def sender(d):
        if members % 2:
            return (member + members - d) % members
        return (member // 2 + members - d // 2) % (members // 2) * 2 + (member + d) % 2

    def each(n, body, init):
        if n <= 8:
            for i in range(n):
                init = body(i, init)
            return init
        return lax.fori_loop(0, n, body, init)

    def wait(ref, sem):
        pltpu.make_async_copy(ref, ref, sem).wait()

    def keys(m, c):
        return krecv.at[m, :, pl.ds(pl.multiple_of(c * rows, 8), rows)]

    def chips_keys(m):
        return krecv.at[m, :, 0:pair_rows]

    own_cols = pl.ds(pl.multiple_of(core * HEAD_DIM, HEAD_DIM), HEAD_DIM)
    other_cols = pl.ds(pl.multiple_of(other * HEAD_DIM, HEAD_DIM), HEAD_DIM)
    loads = []
    for i, (src, dst_own, dst_other) in enumerate((
        (qs_hbm, qrecv.at[0, core, 0], qother.at[0]),
        (qe_hbm, qrecv.at[0, core, 1], qother.at[1]),
        (ks_hbm, keys(member, core).at[0], kother.at[0]),
        (ke_hbm, keys(member, core).at[1], kother.at[1]),
    )):
        loads.append(pltpu.make_async_copy(src.at[:, own_cols], dst_own, load_sem.at[0]))
        loads.append(pltpu.make_async_copy(src.at[:, other_cols], dst_other, load_sem.at[0]))
    count_load = pltpu.make_async_copy(count_hbm, count_ref, load_sem.at[1])
    for load in loads:
        load.start()
    count_load.start()

    barrier = pltpu.get_barrier_semaphore()

    def greet(d, carry):
        for c in (0, 1):
            pl.semaphore_signal(barrier, inc=1, device_id=dev(group, shifted(d + 1), c))
        return carry

    for c in (0, 1):
        pl.semaphore_signal(barrier, inc=1, device_id=dev(1 - group, member, c))
    pl.semaphore_signal(barrier, inc=1, device_id=dev(group, member, other))
    each(members - 1, greet, 0)
    pl.semaphore_wait(barrier, 2 * members + 1)
    wait(chips_keys(slice(0, 2)), load_sem.at[0])
    count_load.wait()

    def key_copy(m, c, same, sem):
        return pltpu.make_async_remote_copy(
            src_ref=keys(member, core) if same else kother,
            dst_ref=keys(member, core),
            send_sem=sem,
            recv_sem=krecv_sem.at[member],
            device_id=dev(group, m, c),
        )

    def query_copy(r, c, same):
        return pltpu.make_async_remote_copy(
            src_ref=qrecv.at[0, core] if same else qother,
            dst_ref=qrecv.at[r, core],
            send_sem=near_sem.at[0],
            recv_sem=qrecv_sem.at[r],
            device_id=dev(1 - group if r else group, member, c),
        )

    query_copy(1, core, True).start()
    query_copy(1, other, False).start()

    def send_keys(d, carry):
        m = shifted(members - 1 - d)
        key_copy(m, core, True, ksend_sem.at[0]).start()
        key_copy(m, other, False, ksend_sem.at[0]).start()
        return carry

    send_keys(0, 0)
    query_copy(0, other, False).start()
    key_copy(member, other, False, near_sem.at[0]).start()
    if members > 2:
        each(members - 2, lambda d, carry: send_keys(d + 1, carry), 0)

    count = count_ref[0]

    def valid(positions):
        return (positions >= text_slots) | (positions < count)

    lane = lax.broadcasted_iota(jnp.int32, (1, width), 1)
    in_tail = lane >= 2 * head
    spot = jnp.where(in_tail, lane - 2 * head, lane)
    half = jnp.where(in_tail, tail, head)
    far = spot >= half
    spot = jnp.where(far, spot - half, spot) + jnp.where(in_tail, head, 0)
    row_place = jnp.where(far, chip_of(1 - group, member), chip) * pair_rows + spot
    row_weight = jnp.where(valid(row_place), 2.0 * weight, 0.0)

    def place_queries(r):
        for which in (0, 1):
            joined = jnp.concatenate([qrecv[r, c, which].astype(F32) for c in (0, 1)], axis=0)
            joined = joined.astype(BF16)
            qcat[which, r * head:(r + 1) * head] = joined[:head]
            if tail:
                at = 2 * head + r * tail
                qcat[which, at:at + tail] = joined[head:]

    def fill_bias(d, carry):
        place = chip_of(group, sender(d)) * pair_rows
        place += lax.broadcasted_iota(jnp.int32, (pair_rows, 128), 0)
        bias_ref[d] = jnp.where(valid(place), 0.0, MASKED).reshape(groups, 8, 128)
        return carry

    each(members, fill_bias, 0)

    def powers(d, m, which, lanes):
        span = lanes.stop - lanes.start
        scores = lax.dot_general(
            krecv[m, which, 0:pair_rows], qcat[which, lanes], (((1,), (1,)), ((), ())),
            preferred_element_type=F32,
        ).reshape(groups, 8, span)
        bias = bias_ref[d]
        scores = jnp.concatenate([
            scores[:, :, i:min(i + 128, span)] + bias[:, :, :min(128, span - i)]
            for i in range(0, span, 128)
        ], axis=2)
        top = jnp.max(scores, axis=0)
        return top, jnp.exp2((scores - top[None]) * power_scale)

    def score_chunk(d, m, lanes):
        m_s, s_pow = powers(d, m, 0, lanes)
        m_e, e_pow = powers(d, m, 1, lanes)
        s_buf[d, :, :, lanes] = s_pow
        e_buf[d, :, :, lanes] = e_pow
        for i, value in enumerate((
            m_e, jnp.sum(e_pow, axis=0), m_s, jnp.sum(s_pow, axis=0),
            jnp.sum(e_pow * e_pow, axis=0), jnp.sum(e_pow * s_pow, axis=0),
        )):
            stats_ref[i, d, :, lanes] = value

    early, late, full = slice(0, head), slice(head, width), slice(0, width)
    wait(qrecv.at[0, 0], qrecv_sem.at[0])
    wait(kother, krecv_sem.at[member])
    place_queries(0)
    ahead = 2 if members == 4 else 1
    for d in range(ahead):
        m = shifted(d) if d else member
        if d:
            wait(chips_keys(m), krecv_sem.at[m])
        if head:
            score_chunk(d, m, early)
    wait(qrecv.at[1], qrecv_sem.at[1])
    place_queries(1)
    for d in range(ahead):
        score_chunk(d, shifted(d) if d else member, late)

    def far_scores(d, carry):
        d = members - 1 - d
        m = sender(d)
        wait(chips_keys(m), krecv_sem.at[m])
        score_chunk(d, m, full)
        return carry

    each(members - ahead, far_scores, 0)

    def fold(op, value):
        return op(op(value, axis=0), axis=0, keepdims=True)

    tops_e, tops_s = stats_ref[0], stats_ref[2]
    m_e, m_s = fold(jnp.max, tops_e), fold(jnp.max, tops_s)
    f_e = jnp.exp2((tops_e - m_e) * power_scale)
    f_s = jnp.exp2((tops_s - m_s) * power_scale)
    stats = (
        m_e, fold(jnp.sum, stats_ref[1] * f_e),
        m_s, fold(jnp.sum, stats_ref[3] * f_s),
        fold(jnp.sum, stats_ref[4] * (f_e * f_e)),
        fold(jnp.sum, stats_ref[5] * (f_e * f_s)),
    )
    packed = jnp.concatenate(stats + (jnp.zeros((2, width), F32),), axis=0)
    st_send[:, :head] = packed[:, head:2 * head]
    st_send[:, head:2 * head] = packed[:, :head]
    if tail:
        st_send[:, 2 * head:] = jnp.concatenate(
            [packed[:, 2 * head + tail:], packed[:, 2 * head:2 * head + tail]], axis=1
        )
    stat_copy = pltpu.make_async_remote_copy(
        src_ref=st_send, dst_ref=st_recv, send_sem=st_sems.at[0], recv_sem=st_sems.at[1],
        device_id=dev(1 - group, member, core),
    )
    stat_copy.start()

    def turn_keys(d, carry):
        m = sender(d)
        kturn[d] = krecv[m, 1, 0:pair_rows].astype(F32).T.astype(BF16)
        return carry

    each(members, turn_keys, 0)

    stat_copy.wait_recv()
    m_e1, l_e1, m_s1, l_s1, sq1, cr1 = stats
    m_e2, l_e2, m_s2, l_s2, sq2, cr2 = (st_recv[i:i + 1] for i in range(6))
    m_e, m_s = jnp.maximum(m_e1, m_e2), jnp.maximum(m_s1, m_s2)
    fe1, fe2 = jnp.exp2((m_e1 - m_e) * power_scale), jnp.exp2((m_e2 - m_e) * power_scale)
    fs1, fs2 = jnp.exp2((m_s1 - m_s) * power_scale), jnp.exp2((m_s2 - m_s) * power_scale)
    inv_e = 1.0 / (l_e1 * fe1 + l_e2 * fe2)
    inv_s = 1.0 / (l_s1 * fs1 + l_s2 * fs2)
    sq = sq1 * fe1 * fe1 + sq2 * fe2 * fe2
    cr = cr1 * fe1 * fs1 + cr2 * fe2 * fs2
    stats_ref[1] = f_e * (fe1 * inv_e)
    stats_ref[3] = f_s * (fs1 * inv_s)
    delta = row_weight * (sq * inv_e * inv_e - cr * inv_e * inv_s)

    def kg_copy(m, c, sem):
        return pltpu.make_async_remote_copy(
            src_ref=kg_send.at[m, c], dst_ref=kg_recv.at[member, core],
            send_sem=sem, recv_sem=kgrecv_sem.at[member],
            device_id=dev(group, m, c),
        )

    def qg_copy(r, c):
        return pltpu.make_async_remote_copy(
            src_ref=qg_send.at[r, c], dst_ref=qg_recv.at[r, core],
            send_sem=gnear_sem.at[0], recv_sem=qgrecv_sem.at[r],
            device_id=dev(1 - group if r else group, member, c),
        )

    q_edit = qcat[1]

    def grad_chunk(d):
        prob_e = e_buf[d] * stats_ref[1, d][None]
        prob_s = s_buf[d] * stats_ref[3, d][None]
        grad = prob_e * (row_weight[None] * (prob_e - prob_s) - delta[None])
        grad = grad.reshape(pair_rows, width).astype(BF16)
        grad_buf[d] = grad
        return jnp.dot(grad, q_edit, preferred_element_type=F32) * scale

    def far_grad(i, carry):
        d = (2, 3, 1)[i] if members == 4 else members - 1 - i
        m = sender(d)
        k_part = grad_chunk(d)
        for c in (0, 1):
            kg_send[m, c] = k_part[c * rows:(c + 1) * rows].astype(BF16)
        for c in (core, other):
            kg_copy(m, c, kgsend_sem.at[0]).start()
        return carry

    each(members - 1, far_grad, 0)
    k_part = grad_chunk(0)
    for c in (0, 1):
        kg_own[c] = k_part[c * rows:(c + 1) * rows]
        kg_send[member, c] = k_part[c * rows:(c + 1) * rows].astype(BF16)

    q_total = each(
        members,
        lambda d, q: q + jnp.dot(kturn[d], grad_buf[d], preferred_element_type=F32),
        jnp.zeros((HEAD_DIM, width), F32),
    )
    q_rows = q_total.T * scale
    for r in (1, 0):
        joined = [q_rows[r * head:(r + 1) * head]]
        if tail:
            at = 2 * head + r * tail
            joined.append(q_rows[at:at + tail])
        joined = jnp.concatenate(joined, axis=0)
        for c in (0, 1):
            part = joined[c * rows:(c + 1) * rows]
            if not r:
                qg_own[c] = part
            qg_send[r, c] = part.astype(BF16)
        if r:
            qg_copy(1, core).start()
            qg_copy(1, other).start()
    qg_copy(0, other).start()
    kg_copy(member, other, gnear_sem.at[0]).start()

    def put(ref, mine, theirs):
        ref[:, own_cols] = mine
        ref[:, other_cols] = theirs

    wait(kg_recv.at[member, 0], kgrecv_sem.at[member])

    def add_far(d, sums):
        mine, theirs = sums
        m = shifted(d + 1)
        wait(kg_recv.at[m], kgrecv_sem.at[m])
        return mine + kg_recv[m, core].astype(F32), theirs + kg_recv[m, other].astype(F32)

    sums = each(members - 1, add_far, (kg_own[core], kg_recv[member, other].astype(F32)))
    put(kg_ref, *sums)

    wait(qg_recv.at[0, 0], qgrecv_sem.at[0])
    wait(qg_recv.at[1], qgrecv_sem.at[1])
    put(
        qg_ref,
        qg_own[core] + qg_recv[1, core].astype(F32),
        qg_recv[0, other].astype(F32) + qg_recv[1, other].astype(F32),
    )

    wait(chips_keys(slice(0, members - 1)), ksend_sem.at[0])
    wait(qrecv, near_sem.at[0])
    stat_copy.wait_send()
    wait(kg_send.at[0:members - 1], kgsend_sem.at[0])
    wait(qg_send, gnear_sem.at[0])


def line_kernel(
    chips,
    count_hbm, qs_hbm, ks_hbm, qe_hbm, ke_hbm,
    qg_ref, kg_ref,
    count_ref, krecv, kother, qrecv, qother, qcat, kturn, bias_ref, grad_buf, e_buf, s_buf, stats_ref,
    st_send, st_recv,
    st_side, st_turn, kg_send, kg_recv, qg_send, qg_recv, qg_own, kg_own,
    load_sem, ksend_sem, near_sem, krecv_sem, qrecv_sem, st_sems, side_sems,
    kgsend_sem, gnear_sem, gfar_sem, kgrecv_sem, qgrecv_sem,
):
    members = chips // 2
    rows = kother.shape[1]
    pair_rows = 2 * rows
    head = pair_rows // 128 * 128
    tail = pair_rows - head
    width = qcat.shape[1]
    blocks = {0: 0, 1: width - head, 2: width - 2 * head}
    groups = pair_rows // 8
    all_rows = rows * chips * 2
    text_slots = min(512, all_rows // 4)
    scale = 1.0 / math.sqrt(HEAD_DIM)
    power_scale = scale * math.log2(math.e)
    weight = 4.0 * all_rows * math.sqrt(all_rows)
    me = lax.axis_index("ctx")
    chip, core = me // 2, me % 2
    other = 1 - core
    group, member = chip // members, chip % members
    inner = (group + member // 2) % 2 == 1
    outer = (group + member // 2) % 2 == 0
    target = (2 - group) * 2 + chip % 2

    def chip_of(g, m):
        return g * members + m

    def dev(g, m, c):
        return {"ctx": chip_of(g, m) * 2 + c}

    def shifted(d):
        if members % 2:
            return (member + d) % members
        return (member // 2 + d // 2) % (members // 2) * 2 + (member + d) % 2

    def sender(d):
        if members % 2:
            return (member + members - d) % members
        return (member // 2 + members - d // 2) % (members // 2) * 2 + (member + d) % 2

    def each(n, body, init):
        if n <= 8:
            for i in range(n):
                init = body(i, init)
            return init
        return lax.fori_loop(0, n, body, init)

    def wait(ref, sem):
        pltpu.make_async_copy(ref, ref, sem).wait()

    def keys(m, c):
        return krecv.at[m, :, pl.ds(pl.multiple_of(c * rows, 8), rows)]

    def chips_keys(m):
        return krecv.at[m, :, 0:pair_rows]

    own_head = (core + group) % 2
    own_cols = pl.ds(pl.multiple_of(own_head * HEAD_DIM, HEAD_DIM), HEAD_DIM)
    other_cols = pl.ds(pl.multiple_of((1 - own_head) * HEAD_DIM, HEAD_DIM), HEAD_DIM)
    loads = []
    for i, (src, dst_own, dst_other) in enumerate((
        (qs_hbm, qrecv.at[0, core, 0], qother.at[0]),
        (qe_hbm, qrecv.at[0, core, 1], qother.at[1]),
        (ks_hbm, keys(member, core).at[0], kother.at[0]),
        (ke_hbm, keys(member, core).at[1], kother.at[1]),
    )):
        loads.append(pltpu.make_async_copy(src.at[:, own_cols], dst_own, load_sem.at[0]))
        loads.append(pltpu.make_async_copy(src.at[:, other_cols], dst_other, load_sem.at[0]))
    count_load = pltpu.make_async_copy(count_hbm, count_ref, load_sem.at[1])
    for load in loads:
        load.start()
    count_load.start()

    barrier = pltpu.get_barrier_semaphore()

    for c in (0, 1):
        pl.semaphore_signal(barrier, inc=1, device_id=dev(1 - group, member, c))

    @pl.when(inner)
    def _():
        for c in (0, 1):
            pl.semaphore_signal(barrier, inc=1, device_id={"ctx": target * 2 + c})

    for d in (3, 2, 1):
        for c in (0, 1):
            pl.semaphore_signal(barrier, inc=1, device_id=dev(group, shifted(d), c))
    pl.semaphore_signal(barrier, inc=1, device_id=dev(group, member, other))
    qcat[...] = jnp.zeros_like(qcat)
    pl.semaphore_wait(barrier, jnp.where(inner, 2 * members + 3, 2 * members + 1))
    wait(chips_keys(slice(0, 2)), load_sem.at[0])
    count_load.wait()

    def key_copy(m, c, same, sem):
        return pltpu.make_async_remote_copy(
            src_ref=keys(member, core) if same else kother,
            dst_ref=keys(member, core),
            send_sem=sem,
            recv_sem=krecv_sem.at[member],
            device_id=dev(group, m, c),
        )

    far_slot = jnp.where(inner, 1, 2)

    def query_copy(far, c, same):
        slot = far_slot if far else 0
        return pltpu.make_async_remote_copy(
            src_ref=qrecv.at[0, core] if same else qother,
            dst_ref=qrecv.at[slot, core],
            send_sem=near_sem.at[0],
            recv_sem=qrecv_sem.at[slot],
            device_id={"ctx": target * 2 + c} if far else dev(group, member, c),
        )

    def send_keys(d):
        key_copy(shifted(d), core, True, ksend_sem.at[0]).start()
        key_copy(shifted(d), other, False, ksend_sem.at[0]).start()

    query_copy(1, other, True).start()
    query_copy(1, core, False).start()
    query_copy(0, other, False).start()
    key_copy(member, other, False, near_sem.at[0]).start()
    send_keys(3)
    send_keys(2)
    send_keys(1)

    count = count_ref[0]

    def valid(positions):
        return (positions >= text_slots) | (positions < count)

    lane = lax.broadcasted_iota(jnp.int32, (1, width), 1)
    own_lane = lane < head
    row_place = chip * pair_rows + lane
    live = own_lane
    for slot, owner in ((0, chip), (1, target), (2, chip_of(1 - group, member))):
        there = lane >= head + slot * tail
        there = there & (lane < head + (slot + 1) * tail)
        row_place = jnp.where(there, owner * pair_rows + lane - slot * tail, row_place)
        if slot:
            at = blocks[slot]
            ahead = (lane >= at) & (lane < at + head)
            row_place = jnp.where(ahead, owner * pair_rows + lane - at, row_place)
            there = (there | ahead) & inner
        live = live | there
    row_weight = jnp.where(live & valid(row_place), 2.0 * weight, 0.0)

    @pl.when(outer)
    def _():
        for buf in (e_buf, s_buf):
            buf[:, :, :, width - 2 * head:] = jnp.zeros((members, groups, 8, 2 * head), F32)

    def place_queries(slot):
        for which in (0, 1):
            joined = jnp.concatenate([qrecv[slot, c, which].astype(F32) for c in (0, 1)], axis=0)
            joined = joined.astype(BF16)
            qcat[which, blocks[slot]:blocks[slot] + head] = joined[:head]
            if tail:
                at = head + slot * tail
                qcat[which, at:at + tail] = joined[head:]

    def fill_bias(d, carry):
        place = chip_of(group, sender(d)) * pair_rows
        place += lax.broadcasted_iota(jnp.int32, (pair_rows, 128), 0)
        bias_ref[d] = jnp.where(valid(place), 0.0, MASKED).reshape(groups, 8, 128)
        return carry

    each(members, fill_bias, 0)

    def powers(d, m, which, lanes):
        span = lanes.stop - lanes.start
        scores = lax.dot_general(
            krecv[m, which, 0:pair_rows], qcat[which, lanes], (((1,), (1,)), ((), ())),
            preferred_element_type=F32,
        ).reshape(groups, 8, span)
        bias = bias_ref[d]
        scores = jnp.concatenate([
            scores[:, :, i:min(i + 128, span)] + bias[:, :, :min(128, span - i)]
            for i in range(0, span, 128)
        ], axis=2)
        top = jnp.max(scores, axis=0)
        return top, jnp.exp2((scores - top[None]) * power_scale)

    def score_chunk(d, m, lanes):
        m_s, s_pow = powers(d, m, 0, lanes)
        m_e, e_pow = powers(d, m, 1, lanes)
        s_buf[d, :, :, lanes] = s_pow
        e_buf[d, :, :, lanes] = e_pow
        for i, value in enumerate((
            m_e, jnp.sum(e_pow, axis=0), m_s, jnp.sum(s_pow, axis=0),
            jnp.sum(e_pow * e_pow, axis=0), jnp.sum(e_pow * s_pow, axis=0),
        )):
            stats_ref[i, d, :, lanes] = value

    own, late = slice(0, head), slice(head, width - head)
    side, full, both = slice(width - head, width), slice(0, width), slice(0, width - 2 * head)

    def keys_from(d):
        m = sender(d)
        wait(chips_keys(m), krecv_sem.at[m])
        return m

    wait(qrecv.at[0, 0], qrecv_sem.at[0])
    wait(kother, krecv_sem.at[member])
    place_queries(0)

    @pl.when(outer)
    def _():
        score_chunk(0, member, both)
        for d in (1, 3, 2):
            score_chunk(d, keys_from(d), both)

    @pl.when(inner)
    def _():
        for slot in (1, 2):
            wait(qrecv.at[slot], qrecv_sem.at[slot])
        for slot in (1, 2):
            place_queries(slot)
        score_chunk(0, member, full)
        score_chunk(1, keys_from(1), full)
        for d in (3, 2):
            keys_from(d)
        for d in (3, 2):
            score_chunk(d, sender(d), full)

    def fold(op, value):
        return op(op(value, axis=0), axis=0, keepdims=True)

    tops_e, tops_s = stats_ref[0], stats_ref[2]
    m_e, m_s = fold(jnp.max, tops_e), fold(jnp.max, tops_s)
    f_e = jnp.exp2((tops_e - m_e) * power_scale)
    f_s = jnp.exp2((tops_s - m_s) * power_scale)
    stats = (
        m_e, fold(jnp.sum, stats_ref[1] * f_e),
        m_s, fold(jnp.sum, stats_ref[3] * f_s),
        fold(jnp.sum, stats_ref[4] * (f_e * f_e)),
        fold(jnp.sum, stats_ref[5] * (f_e * f_s)),
    )
    packed = jnp.concatenate(stats + (jnp.zeros((2, width), F32),), axis=0)
    span = width - 3 * head
    tails = packed[:, head:head + span]
    st_send[:, :head] = jnp.where(inner, packed[:, blocks[2]:blocks[2] + head], packed[:, :head])
    st_send[:, head:] = jnp.where(
        inner, pltpu.roll(tails, span - 2 * tail, 1), pltpu.roll(tails, 2 * tail, 1)
    )
    stat_copy = pltpu.make_async_remote_copy(
        src_ref=st_send, dst_ref=st_recv, send_sem=st_sems.at[0], recv_sem=st_sems.at[1],
        device_id=dev(1 - group, member, other),
    )
    side_copy = pltpu.make_async_remote_copy(
        src_ref=st_side, dst_ref=st_turn, send_sem=side_sems.at[0], recv_sem=side_sems.at[1],
        device_id={"ctx": target * 2 + other},
    )

    @pl.when(inner)
    def _():
        st_side[:, :head] = packed[:, blocks[1]:]
        st_side[:, head:2 * head] = packed[:, :head]
        tail_lane = lax.broadcasted_iota(jnp.int32, (8, span), 1)
        st_side[:, 2 * head:] = jnp.where(
            tail_lane < tail, pltpu.roll(tails, span - tail, 1), pltpu.roll(tails, tail, 1)
        )
        side_copy.start()

    stat_copy.start()

    def turn_keys(d, carry):
        m = sender(d)
        kturn[d] = krecv[m, 1, 0:pair_rows].astype(F32).T.astype(BF16)
        return carry

    each(members, turn_keys, 0)

    @pl.when(inner)
    def _():
        side_copy.wait_recv()

    stat_copy.wait_recv()
    there, turned = st_recv[...], st_turn[...]
    tail_lane = lax.broadcasted_iota(jnp.int32, (8, span), 1)
    second = jnp.concatenate([
        jnp.where(inner, turned[:, :head], there[:, :head]),
        jnp.where(inner & (tail_lane < 2 * tail), turned[:, 2 * head:], there[:, head:]),
        there[:, :head],
        turned[:, head:2 * head],
    ], axis=1)
    m_e1, l_e1, m_s1, l_s1, sq1, cr1 = stats
    m_e2, l_e2, m_s2, l_s2, sq2, cr2 = (second[i:i + 1] for i in range(6))
    m_e, m_s = jnp.maximum(m_e1, m_e2), jnp.maximum(m_s1, m_s2)
    fe1, fe2 = jnp.exp2((m_e1 - m_e) * power_scale), jnp.exp2((m_e2 - m_e) * power_scale)
    fs1, fs2 = jnp.exp2((m_s1 - m_s) * power_scale), jnp.exp2((m_s2 - m_s) * power_scale)
    inv_e = 1.0 / (l_e1 * fe1 + l_e2 * fe2)
    inv_s = 1.0 / (l_s1 * fs1 + l_s2 * fs2)
    sq = sq1 * fe1 * fe1 + sq2 * fe2 * fe2
    cr = cr1 * fe1 * fs1 + cr2 * fe2 * fs2
    stats_ref[1] = jnp.where(live, f_e * (fe1 * inv_e), 0.0)
    stats_ref[3] = jnp.where(live, f_s * (fs1 * inv_s), 0.0)
    delta = jnp.where(live, row_weight * (sq * inv_e * inv_e - cr * inv_e * inv_s), 0.0)

    def kg_copy(m, c, sem):
        return pltpu.make_async_remote_copy(
            src_ref=kg_send.at[m, c], dst_ref=kg_recv.at[member, core],
            send_sem=sem, recv_sem=kgrecv_sem.at[member],
            device_id=dev(group, m, c),
        )

    def qg_copy(slot, c):
        return pltpu.make_async_remote_copy(
            src_ref=qg_send.at[slot, c], dst_ref=qg_recv.at[1 if slot else 0, core],
            send_sem=gfar_sem.at[0] if slot else gnear_sem.at[0],
            recv_sem=qgrecv_sem.at[1 if slot else 0],
            device_id=(dev(group, member, c), {"ctx": target * 2 + c}, dev(1 - group, member, c))[slot],
        )

    q_edit = qcat[1]

    def grad_chunk(d):
        prob_e = e_buf[d] * stats_ref[1, d][None]
        prob_s = s_buf[d] * stats_ref[3, d][None]
        grad = prob_e * (row_weight[None] * (prob_e - prob_s) - delta[None])
        grad = grad.reshape(pair_rows, width).astype(BF16)
        grad_buf[d] = grad
        return jnp.dot(grad, q_edit, preferred_element_type=F32) * scale

    def far_grad(i, carry):
        d = (2, 3, 1)[i] if members == 4 else members - 1 - i
        m = sender(d)
        k_part = grad_chunk(d)
        for c in (0, 1):
            kg_send[m, c] = k_part[c * rows:(c + 1) * rows].astype(BF16)
        for c in (0, 1):
            kg_copy(m, c, kgsend_sem.at[0]).start()
        return carry

    each(members - 1, far_grad, 0)
    k_part = grad_chunk(0)
    for c in (0, 1):
        kg_own[c] = k_part[c * rows:(c + 1) * rows]
        kg_send[member, c] = k_part[c * rows:(c + 1) * rows].astype(BF16)

    q_total = each(
        members,
        lambda d, q: q + jnp.dot(kturn[d], grad_buf[d], preferred_element_type=F32),
        jnp.zeros((HEAD_DIM, width), F32),
    )
    q_rows = q_total.T * scale
    for slot in (2, 1, 0):
        joined = [q_rows[blocks[slot]:blocks[slot] + head]]
        if tail:
            at = head + slot * tail
            joined.append(q_rows[at:at + tail])
        joined = jnp.concatenate(joined, axis=0)
        for c in (0, 1):
            part = joined[c * rows:(c + 1) * rows]
            if not slot:
                qg_own[c] = part
            qg_send[slot, c] = part.astype(BF16)

    @pl.when(inner)
    def _():
        for slot in (2, 1):
            for c in (0, 1):
                qg_copy(slot, c).start()

    qg_copy(0, other).start()
    kg_copy(member, other, gnear_sem.at[0]).start()

    def put(ref, mine, theirs):
        ref[:, own_cols] = mine
        ref[:, other_cols] = theirs

    wait(kg_recv.at[member, 0], kgrecv_sem.at[member])

    def add_far(d, sums):
        mine, theirs = sums
        m = shifted(d + 1)
        wait(kg_recv.at[m], kgrecv_sem.at[m])
        return mine + kg_recv[m, core].astype(F32), theirs + kg_recv[m, other].astype(F32)

    sums = each(members - 1, add_far, (kg_own[core], kg_recv[member, other].astype(F32)))
    put(kg_ref, *sums)

    wait(qg_recv.at[0, 0], qgrecv_sem.at[0])
    wait(qg_recv.at[1], qgrecv_sem.at[1])
    put(
        qg_ref,
        qg_own[core] + qg_recv[1, other].astype(F32),
        qg_recv[0, other].astype(F32) + qg_recv[1, core].astype(F32),
    )

    wait(chips_keys(slice(0, members - 1)), ksend_sem.at[0])
    wait(qrecv.at[0:2], near_sem.at[0])
    stat_copy.wait_send()
    wait(kg_send.at[0:members - 1], kgsend_sem.at[0])
    wait(qg_send.at[0], gnear_sem.at[0])

    @pl.when(inner)
    def _():
        wait(qg_send.at[1:3], gfar_sem.at[0])
        side_copy.wait_send()


def put_out(qg_vmem, kg_vmem, qg_hbm, kg_hbm, sems):
    copies = (
        pltpu.make_async_copy(qg_vmem, qg_hbm, sems.at[0]),
        pltpu.make_async_copy(kg_vmem, kg_hbm, sems.at[1]),
    )
    for copy in copies:
        copy.start()
    for copy in copies:
        copy.wait()


def solution(mesh):
    chips = mesh.shape["ctx"] // 2
    members = chips // 2

    def local(query_source, key_source, query_edit, key_edit, text_count):
        rows, full = query_source.shape
        width = 4 * rows
        groups = 2 * rows // 8
        dma = pltpu.SemaphoreType.DMA
        vmem = pltpu.VMEM
        in_line = chips == 8
        if in_line:
            pair = 2 * rows
            head = pair // 128 * 128
            width = 3 * head + -(-3 * (pair - head) // 128) * 128
        slots = 3 if in_line else 2
        stat = vmem((8, width - 2 * head if in_line else width), F32)
        side = [vmem((8, width - head), F32)] * 2 if in_line else []
        grads = pl.pallas_call(
            functools.partial(line_kernel if in_line else kernel, chips),
            out_shape=(
                pltpu.VMEM((rows, full), F32),
                pltpu.VMEM((rows, full), F32),
            ),
            in_specs=[pl.BlockSpec(memory_space=pltpu.HBM)] * 5,
            out_specs=(pl.BlockSpec(memory_space=pltpu.VMEM),) * 2,
            scratch_shapes=[
                pltpu.SMEM((1,), jnp.int32),
                vmem((members, 2, 2 * rows + 8, HEAD_DIM), BF16),
                vmem((2, rows, HEAD_DIM), BF16),
                vmem((slots, 2, 2, rows, HEAD_DIM), BF16),
                vmem((2, rows, HEAD_DIM), BF16),
                vmem((2, width, HEAD_DIM), BF16),
                vmem((members, HEAD_DIM, 2 * rows), BF16),
                vmem((members, groups, 8, 128), F32),
                vmem((members, 2 * rows, width), BF16),
                vmem((members, groups, 8, width), F32),
                vmem((members, groups, 8, width), F32),
                vmem((6, members, 8, width), F32),
                stat,
                stat,
                *side,
                vmem((members, 2, rows, HEAD_DIM), BF16),
                vmem((members, 2, rows, HEAD_DIM), BF16),
                vmem((slots, 2, rows, HEAD_DIM), BF16),
                vmem((2, 2, rows, HEAD_DIM), BF16),
                vmem((2, rows, HEAD_DIM), F32),
                vmem((2, rows, HEAD_DIM), F32),
                dma((2,)),
                dma((1,)),
                dma((1,)),
                dma((members,)),
                dma((slots,)),
                dma((2,)),
                *([dma((2,))] if in_line else []),
                dma((1,)),
                dma((1,)),
                *([dma((1,))] if in_line else []),
                dma((members,)),
                dma((2,)),
            ],
            compiler_params=pltpu.CompilerParams(collective_id=0, has_side_effects=True),
        )(text_count, query_source, key_source, query_edit, key_edit)
        return pl.pallas_call(
            put_out,
            out_shape=(pltpu.HBM((rows, full), F32),) * 2,
            in_specs=[pl.BlockSpec(memory_space=pltpu.VMEM)] * 2,
            out_specs=(pl.BlockSpec(memory_space=pltpu.HBM),) * 2,
            scratch_shapes=[dma((2,))],
        )(*(pltpu.with_memory_space_constraint(g, pltpu.VMEM) for g in grads))

    spec = P(("req", "ctx"), None)
    return jax.shard_map(
        local, mesh=mesh, in_specs=(spec,) * 4 + (P("req"),), out_specs=(spec, spec), check_vma=False
    )
```

```python
import functools
import math

import jax
import jax.numpy as jnp
from jax import lax
from jax.experimental import pallas as pl
from jax.experimental.pallas import tpu as pltpu
from jax.sharding import PartitionSpec as P

HEAD_DIM = 128
MASKED = -1e30
F32 = jnp.float32
BF16 = jnp.bfloat16


def kernel(
    chips,
    count_hbm, qs_hbm, ks_hbm, qe_hbm, ke_hbm,
    qg_ref, kg_ref,
    count_ref, krecv, kother, qrecv, qother, qcat, kturn, bias_ref, grad_buf, e_buf, s_buf, stats_ref,
    st_send, st_recv,
    kg_send, kg_recv, qg_send, qg_recv, qg_own, kg_own,
    load_sem, ksend_sem, near_sem, krecv_sem, qrecv_sem, st_sems,
    kgsend_sem, gnear_sem, kgrecv_sem, qgrecv_sem,
):
    members = chips // 2
    rows = kother.shape[1]
    pair_rows = 2 * rows
    width = 2 * pair_rows
    head = pair_rows // 128 * 128
    tail = pair_rows - head
    groups = pair_rows // 8
    all_rows = rows * chips * 2
    text_slots = min(512, all_rows // 4)
    scale = 1.0 / math.sqrt(HEAD_DIM)
    power_scale = scale * math.log2(math.e)
    weight = 4.0 * all_rows * math.sqrt(all_rows)
    me = lax.axis_index("ctx")
    chip, core = me // 2, me % 2
    other = 1 - core
    group, member = chip // members, chip % members

    def chip_of(g, m):
        return g * members + m

    def dev(g, m, c):
        return {"ctx": chip_of(g, m) * 2 + c}

    def shifted(d):
        if members % 2:
            return (member + d) % members
        return (member // 2 + d // 2) % (members // 2) * 2 + (member + d) % 2

    def sender(d):
        if members % 2:
            return (member + members - d) % members
        return (member // 2 + members - d // 2) % (members // 2) * 2 + (member + d) % 2

    def each(n, body, init):
        if n <= 8:
            for i in range(n):
                init = body(i, init)
            return init
        return lax.fori_loop(0, n, body, init)

    def wait(ref, sem):
        pltpu.make_async_copy(ref, ref, sem).wait()

    def keys(m, c):
        return krecv.at[m, :, pl.ds(pl.multiple_of(c * rows, 8), rows)]

    def chips_keys(m):
        return krecv.at[m, :, 0:pair_rows]

    own_cols = pl.ds(pl.multiple_of(core * HEAD_DIM, HEAD_DIM), HEAD_DIM)
    other_cols = pl.ds(pl.multiple_of(other * HEAD_DIM, HEAD_DIM), HEAD_DIM)
    loads = []
    for i, (src, dst_own, dst_other) in enumerate((
        (qs_hbm, qrecv.at[0, core, 0], qother.at[0]),
        (qe_hbm, qrecv.at[0, core, 1], qother.at[1]),
        (ks_hbm, keys(member, core).at[0], kother.at[0]),
        (ke_hbm, keys(member, core).at[1], kother.at[1]),
    )):
        loads.append(pltpu.make_async_copy(src.at[:, own_cols], dst_own, load_sem.at[0]))
        loads.append(pltpu.make_async_copy(src.at[:, other_cols], dst_other, load_sem.at[0]))
    count_load = pltpu.make_async_copy(count_hbm, count_ref, load_sem.at[1])
    for load in loads:
        load.start()
    count_load.start()

    barrier = pltpu.get_barrier_semaphore()

    def greet(d, carry):
        for c in (0, 1):
            pl.semaphore_signal(barrier, inc=1, device_id=dev(group, shifted(d + 1), c))
        return carry

    for c in (0, 1):
        pl.semaphore_signal(barrier, inc=1, device_id=dev(1 - group, member, c))
    pl.semaphore_signal(barrier, inc=1, device_id=dev(group, member, other))
    each(members - 1, greet, 0)
    pl.semaphore_wait(barrier, 2 * members + 1)
    wait(chips_keys(slice(0, 2)), load_sem.at[0])
    count_load.wait()

    def key_copy(m, c, same, sem):
        return pltpu.make_async_remote_copy(
            src_ref=keys(member, core) if same else kother,
            dst_ref=keys(member, core),
            send_sem=sem,
            recv_sem=krecv_sem.at[member],
            device_id=dev(group, m, c),
        )

    def query_copy(r, c, same):
        return pltpu.make_async_remote_copy(
            src_ref=qrecv.at[0, core] if same else qother,
            dst_ref=qrecv.at[r, core],
            send_sem=near_sem.at[0],
            recv_sem=qrecv_sem.at[r],
            device_id=dev(1 - group if r else group, member, c),
        )

    query_copy(1, core, True).start()
    query_copy(1, other, False).start()

    def send_keys(d, carry):
        m = shifted(members - 1 - d)
        key_copy(m, core, True, ksend_sem.at[0]).start()
        key_copy(m, other, False, ksend_sem.at[0]).start()
        return carry

    send_keys(0, 0)
    query_copy(0, other, False).start()
    key_copy(member, other, False, near_sem.at[0]).start()
    if members > 2:
        each(members - 2, lambda d, carry: send_keys(d + 1, carry), 0)

    count = count_ref[0]

    def valid(positions):
        return (positions >= text_slots) | (positions < count)

    lane = lax.broadcasted_iota(jnp.int32, (1, width), 1)
    in_tail = lane >= 2 * head
    spot = jnp.where(in_tail, lane - 2 * head, lane)
    half = jnp.where(in_tail, tail, head)
    far = spot >= half
    spot = jnp.where(far, spot - half, spot) + jnp.where(in_tail, head, 0)
    row_place = jnp.where(far, chip_of(1 - group, member), chip) * pair_rows + spot
    row_weight = jnp.where(valid(row_place), 2.0 * weight, 0.0)

    def place_queries(r):
        for which in (0, 1):
            joined = jnp.concatenate([qrecv[r, c, which].astype(F32) for c in (0, 1)], axis=0)
            joined = joined.astype(BF16)
            qcat[which, r * head:(r + 1) * head] = joined[:head]
            if tail:
                at = 2 * head + r * tail
                qcat[which, at:at + tail] = joined[head:]

    def fill_bias(d, carry):
        place = chip_of(group, sender(d)) * pair_rows
        place += lax.broadcasted_iota(jnp.int32, (pair_rows, 128), 0)
        bias_ref[d] = jnp.where(valid(place), 0.0, MASKED).reshape(groups, 8, 128)
        return carry

    each(members, fill_bias, 0)

    def powers(d, m, which, lanes):
        span = lanes.stop - lanes.start
        scores = lax.dot_general(
            krecv[m, which, 0:pair_rows], qcat[which, lanes], (((1,), (1,)), ((), ())),
            preferred_element_type=F32,
        ).reshape(groups, 8, span)
        bias = bias_ref[d]
        scores = jnp.concatenate([
            scores[:, :, i:min(i + 128, span)] + bias[:, :, :min(128, span - i)]
            for i in range(0, span, 128)
        ], axis=2)
        top = jnp.max(scores, axis=0)
        return top, jnp.exp2((scores - top[None]) * power_scale)

    def score_chunk(d, m, lanes):
        m_s, s_pow = powers(d, m, 0, lanes)
        m_e, e_pow = powers(d, m, 1, lanes)
        s_buf[d, :, :, lanes] = s_pow
        e_buf[d, :, :, lanes] = e_pow
        for i, value in enumerate((
            m_e, jnp.sum(e_pow, axis=0), m_s, jnp.sum(s_pow, axis=0),
            jnp.sum(e_pow * e_pow, axis=0), jnp.sum(e_pow * s_pow, axis=0),
        )):
            stats_ref[i, d, :, lanes] = value

    early, late, full = slice(0, head), slice(head, width), slice(0, width)
    wait(qrecv.at[0, 0], qrecv_sem.at[0])
    wait(kother, krecv_sem.at[member])
    place_queries(0)
    ahead = 2 if members == 4 else 1
    for d in range(ahead):
        m = shifted(d) if d else member
        if d:
            wait(chips_keys(m), krecv_sem.at[m])
        if head:
            score_chunk(d, m, early)
    wait(qrecv.at[1], qrecv_sem.at[1])
    place_queries(1)
    for d in range(ahead):
        score_chunk(d, shifted(d) if d else member, late)

    def far_scores(d, carry):
        d = members - 1 - d
        m = sender(d)
        wait(chips_keys(m), krecv_sem.at[m])
        score_chunk(d, m, full)
        return carry

    each(members - ahead, far_scores, 0)

    def fold(op, value):
        return op(op(value, axis=0), axis=0, keepdims=True)

    tops_e, tops_s = stats_ref[0], stats_ref[2]
    m_e, m_s = fold(jnp.max, tops_e), fold(jnp.max, tops_s)
    f_e = jnp.exp2((tops_e - m_e) * power_scale)
    f_s = jnp.exp2((tops_s - m_s) * power_scale)
    stats = (
        m_e, fold(jnp.sum, stats_ref[1] * f_e),
        m_s, fold(jnp.sum, stats_ref[3] * f_s),
        fold(jnp.sum, stats_ref[4] * (f_e * f_e)),
        fold(jnp.sum, stats_ref[5] * (f_e * f_s)),
    )
    packed = jnp.concatenate(stats + (jnp.zeros((2, width), F32),), axis=0)
    st_send[:, :head] = packed[:, head:2 * head]
    st_send[:, head:2 * head] = packed[:, :head]
    if tail:
        st_send[:, 2 * head:] = jnp.concatenate(
            [packed[:, 2 * head + tail:], packed[:, 2 * head:2 * head + tail]], axis=1
        )
    stat_copy = pltpu.make_async_remote_copy(
        src_ref=st_send, dst_ref=st_recv, send_sem=st_sems.at[0], recv_sem=st_sems.at[1],
        device_id=dev(1 - group, member, core),
    )
    stat_copy.start()

    def turn_keys(d, carry):
        m = sender(d)
        kturn[d] = krecv[m, 1, 0:pair_rows].astype(F32).T.astype(BF16)
        return carry

    each(members, turn_keys, 0)

    stat_copy.wait_recv()
    m_e1, l_e1, m_s1, l_s1, sq1, cr1 = stats
    m_e2, l_e2, m_s2, l_s2, sq2, cr2 = (st_recv[i:i + 1] for i in range(6))
    m_e, m_s = jnp.maximum(m_e1, m_e2), jnp.maximum(m_s1, m_s2)
    fe1, fe2 = jnp.exp2((m_e1 - m_e) * power_scale), jnp.exp2((m_e2 - m_e) * power_scale)
    fs1, fs2 = jnp.exp2((m_s1 - m_s) * power_scale), jnp.exp2((m_s2 - m_s) * power_scale)
    inv_e = 1.0 / (l_e1 * fe1 + l_e2 * fe2)
    inv_s = 1.0 / (l_s1 * fs1 + l_s2 * fs2)
    sq = sq1 * fe1 * fe1 + sq2 * fe2 * fe2
    cr = cr1 * fe1 * fs1 + cr2 * fe2 * fs2
    stats_ref[1] = f_e * (fe1 * inv_e)
    stats_ref[3] = f_s * (fs1 * inv_s)
    delta = row_weight * (sq * inv_e * inv_e - cr * inv_e * inv_s)

    def kg_copy(m, c, sem):
        return pltpu.make_async_remote_copy(
            src_ref=kg_send.at[m, c], dst_ref=kg_recv.at[member, core],
            send_sem=sem, recv_sem=kgrecv_sem.at[member],
            device_id=dev(group, m, c),
        )

    def qg_copy(r, c):
        return pltpu.make_async_remote_copy(
            src_ref=qg_send.at[r, c], dst_ref=qg_recv.at[r, core],
            send_sem=gnear_sem.at[0], recv_sem=qgrecv_sem.at[r],
            device_id=dev(1 - group if r else group, member, c),
        )

    q_edit = qcat[1]

    def grad_chunk(d):
        prob_e = e_buf[d] * stats_ref[1, d][None]
        prob_s = s_buf[d] * stats_ref[3, d][None]
        grad = prob_e * (row_weight[None] * (prob_e - prob_s) - delta[None])
        grad = grad.reshape(pair_rows, width).astype(BF16)
        grad_buf[d] = grad
        return jnp.dot(grad, q_edit, preferred_element_type=F32) * scale

    def far_grad(i, carry):
        d = (2, 3, 1)[i] if members == 4 else members - 1 - i
        m = sender(d)
        k_part = grad_chunk(d)
        for c in (0, 1):
            kg_send[m, c] = k_part[c * rows:(c + 1) * rows].astype(BF16)
        for c in (core, other):
            kg_copy(m, c, kgsend_sem.at[0]).start()
        return carry

    each(members - 1, far_grad, 0)
    k_part = grad_chunk(0)
    for c in (0, 1):
        kg_own[c] = k_part[c * rows:(c + 1) * rows]
        kg_send[member, c] = k_part[c * rows:(c + 1) * rows].astype(BF16)

    q_total = each(
        members,
        lambda d, q: q + jnp.dot(kturn[d], grad_buf[d], preferred_element_type=F32),
        jnp.zeros((HEAD_DIM, width), F32),
    )
    q_rows = q_total.T * scale
    for r in (1, 0):
        joined = [q_rows[r * head:(r + 1) * head]]
        if tail:
            at = 2 * head + r * tail
            joined.append(q_rows[at:at + tail])
        joined = jnp.concatenate(joined, axis=0)
        for c in (0, 1):
            part = joined[c * rows:(c + 1) * rows]
            if not r:
                qg_own[c] = part
            qg_send[r, c] = part.astype(BF16)
        if r:
            qg_copy(1, core).start()
            qg_copy(1, other).start()
    qg_copy(0, other).start()
    kg_copy(member, other, gnear_sem.at[0]).start()

    def put(ref, mine, theirs):
        ref[:, own_cols] = mine
        ref[:, other_cols] = theirs

    wait(kg_recv.at[member, 0], kgrecv_sem.at[member])

    def add_far(d, sums):
        mine, theirs = sums
        m = shifted(d + 1)
        wait(kg_recv.at[m], kgrecv_sem.at[m])
        return mine + kg_recv[m, core].astype(F32), theirs + kg_recv[m, other].astype(F32)

    sums = each(members - 1, add_far, (kg_own[core], kg_recv[member, other].astype(F32)))
    put(kg_ref, *sums)

    wait(qg_recv.at[0, 0], qgrecv_sem.at[0])
    wait(qg_recv.at[1], qgrecv_sem.at[1])
    put(
        qg_ref,
        qg_own[core] + qg_recv[1, core].astype(F32),
        qg_recv[0, other].astype(F32) + qg_recv[1, other].astype(F32),
    )

    wait(chips_keys(slice(0, members - 1)), ksend_sem.at[0])
    wait(qrecv, near_sem.at[0])
    stat_copy.wait_send()
    wait(kg_send.at[0:members - 1], kgsend_sem.at[0])
    wait(qg_send, gnear_sem.at[0])


def line_kernel(
    chips,
    count_hbm, qs_hbm, ks_hbm, qe_hbm, ke_hbm,
    qg_ref, kg_ref,
    count_ref, krecv, kother, qrecv, qother, qcat, kturn, bias_ref, grad_buf, e_buf, s_buf, stats_ref,
    st_send, st_recv,
    st_side, st_turn, kg_send, kg_recv, qg_send, qg_recv, qg_own, kg_own,
    load_sem, ksend_sem, near_sem, krecv_sem, qrecv_sem, st_sems, side_sems,
    kgsend_sem, gnear_sem, gfar_sem, kgrecv_sem, qgrecv_sem,
):
    members = chips // 2
    rows = kother.shape[1]
    pair_rows = 2 * rows
    head = pair_rows // 128 * 128
    tail = pair_rows - head
    width = qcat.shape[1]
    blocks = {0: 0, 1: width - head, 2: width - 2 * head}
    groups = pair_rows // 8
    all_rows = rows * chips * 2
    text_slots = min(512, all_rows // 4)
    scale = 1.0 / math.sqrt(HEAD_DIM)
    power_scale = scale * math.log2(math.e)
    weight = 4.0 * all_rows * math.sqrt(all_rows)
    me = lax.axis_index("ctx")
    chip, core = me // 2, me % 2
    other = 1 - core
    group, member = chip // members, chip % members
    inner = (group + member // 2) % 2 == 1
    outer = (group + member // 2) % 2 == 0
    target = (2 - group) * 2 + chip % 2

    def chip_of(g, m):
        return g * members + m

    def dev(g, m, c):
        return {"ctx": chip_of(g, m) * 2 + c}

    def shifted(d):
        if members % 2:
            return (member + d) % members
        return (member // 2 + d // 2) % (members // 2) * 2 + (member + d) % 2

    def sender(d):
        if members % 2:
            return (member + members - d) % members
        return (member // 2 + members - d // 2) % (members // 2) * 2 + (member + d) % 2

    def each(n, body, init):
        if n <= 8:
            for i in range(n):
                init = body(i, init)
            return init
        return lax.fori_loop(0, n, body, init)

    def wait(ref, sem):
        pltpu.make_async_copy(ref, ref, sem).wait()

    def keys(m, c):
        return krecv.at[m, :, pl.ds(pl.multiple_of(c * rows, 8), rows)]

    def chips_keys(m):
        return krecv.at[m, :, 0:pair_rows]

    own_head = (core + group) % 2
    own_cols = pl.ds(pl.multiple_of(own_head * HEAD_DIM, HEAD_DIM), HEAD_DIM)
    other_cols = pl.ds(pl.multiple_of((1 - own_head) * HEAD_DIM, HEAD_DIM), HEAD_DIM)
    loads = []
    for i, (src, dst_own, dst_other) in enumerate((
        (qs_hbm, qrecv.at[0, core, 0], qother.at[0]),
        (qe_hbm, qrecv.at[0, core, 1], qother.at[1]),
        (ks_hbm, keys(member, core).at[0], kother.at[0]),
        (ke_hbm, keys(member, core).at[1], kother.at[1]),
    )):
        loads.append(pltpu.make_async_copy(src.at[:, own_cols], dst_own, load_sem.at[0]))
        loads.append(pltpu.make_async_copy(src.at[:, other_cols], dst_other, load_sem.at[0]))
    count_load = pltpu.make_async_copy(count_hbm, count_ref, load_sem.at[1])
    for load in loads:
        load.start()
    count_load.start()

    barrier = pltpu.get_barrier_semaphore()

    for c in (0, 1):
        pl.semaphore_signal(barrier, inc=1, device_id=dev(1 - group, member, c))

    @pl.when(inner)
    def _():
        for c in (0, 1):
            pl.semaphore_signal(barrier, inc=1, device_id={"ctx": target * 2 + c})

    for d in (3, 2, 1):
        for c in (0, 1):
            pl.semaphore_signal(barrier, inc=1, device_id=dev(group, shifted(d), c))
    pl.semaphore_signal(barrier, inc=1, device_id=dev(group, member, other))
    qcat[...] = jnp.zeros_like(qcat)
    pl.semaphore_wait(barrier, jnp.where(inner, 2 * members + 3, 2 * members + 1))
    wait(chips_keys(slice(0, 2)), load_sem.at[0])
    count_load.wait()

    def key_copy(m, c, same, sem):
        return pltpu.make_async_remote_copy(
            src_ref=keys(member, core) if same else kother,
            dst_ref=keys(member, core),
            send_sem=sem,
            recv_sem=krecv_sem.at[member],
            device_id=dev(group, m, c),
        )

    far_slot = jnp.where(inner, 1, 2)

    def query_copy(far, c, same):
        slot = far_slot if far else 0
        return pltpu.make_async_remote_copy(
            src_ref=qrecv.at[0, core] if same else qother,
            dst_ref=qrecv.at[slot, core],
            send_sem=near_sem.at[0],
            recv_sem=qrecv_sem.at[slot],
            device_id={"ctx": target * 2 + c} if far else dev(group, member, c),
        )

    def send_keys(d):
        key_copy(shifted(d), core, True, ksend_sem.at[0]).start()
        key_copy(shifted(d), other, False, ksend_sem.at[0]).start()

    query_copy(1, other, True).start()
    query_copy(1, core, False).start()
    query_copy(0, other, False).start()
    key_copy(member, other, False, near_sem.at[0]).start()
    send_keys(3)
    send_keys(2)
    send_keys(1)

    count = count_ref[0]

    def valid(positions):
        return (positions >= text_slots) | (positions < count)

    lane = lax.broadcasted_iota(jnp.int32, (1, width), 1)
    own_lane = lane < head
    row_place = chip * pair_rows + lane
    live = own_lane
    for slot, owner in ((0, chip), (1, target), (2, chip_of(1 - group, member))):
        there = lane >= head + slot * tail
        there = there & (lane < head + (slot + 1) * tail)
        row_place = jnp.where(there, owner * pair_rows + lane - slot * tail, row_place)
        if slot:
            at = blocks[slot]
            ahead = (lane >= at) & (lane < at + head)
            row_place = jnp.where(ahead, owner * pair_rows + lane - at, row_place)
            there = (there | ahead) & inner
        live = live | there
    row_weight = jnp.where(live & valid(row_place), 2.0 * weight, 0.0)

    @pl.when(outer)
    def _():
        for buf in (e_buf, s_buf):
            buf[:, :, :, width - 2 * head:] = jnp.zeros((members, groups, 8, 2 * head), F32)

    def place_queries(slot):
        for which in (0, 1):
            joined = jnp.concatenate([qrecv[slot, c, which].astype(F32) for c in (0, 1)], axis=0)
            joined = joined.astype(BF16)
            qcat[which, blocks[slot]:blocks[slot] + head] = joined[:head]
            if tail:
                at = head + slot * tail
                qcat[which, at:at + tail] = joined[head:]

    def fill_bias(d, carry):
        place = chip_of(group, sender(d)) * pair_rows
        place += lax.broadcasted_iota(jnp.int32, (pair_rows, 128), 0)
        bias_ref[d] = jnp.where(valid(place), 0.0, MASKED).reshape(groups, 8, 128)
        return carry

    each(members, fill_bias, 0)

    def powers(d, m, which, lanes):
        span = lanes.stop - lanes.start
        scores = lax.dot_general(
            krecv[m, which, 0:pair_rows], qcat[which, lanes], (((1,), (1,)), ((), ())),
            preferred_element_type=F32,
        ).reshape(groups, 8, span)
        bias = bias_ref[d]
        scores = jnp.concatenate([
            scores[:, :, i:min(i + 128, span)] + bias[:, :, :min(128, span - i)]
            for i in range(0, span, 128)
        ], axis=2)
        top = jnp.max(scores, axis=0)
        return top, jnp.exp2((scores - top[None]) * power_scale)

    def score_chunk(d, m, lanes):
        m_s, s_pow = powers(d, m, 0, lanes)
        m_e, e_pow = powers(d, m, 1, lanes)
        s_buf[d, :, :, lanes] = s_pow
        e_buf[d, :, :, lanes] = e_pow
        for i, value in enumerate((
            m_e, jnp.sum(e_pow, axis=0), m_s, jnp.sum(s_pow, axis=0),
            jnp.sum(e_pow * e_pow, axis=0), jnp.sum(e_pow * s_pow, axis=0),
        )):
            stats_ref[i, d, :, lanes] = value

    own, late = slice(0, head), slice(head, width - head)
    side, full, both = slice(width - head, width), slice(0, width), slice(0, width - 2 * head)

    def keys_from(d):
        m = sender(d)
        wait(chips_keys(m), krecv_sem.at[m])
        return m

    wait(qrecv.at[0, 0], qrecv_sem.at[0])
    wait(kother, krecv_sem.at[member])
    place_queries(0)

    @pl.when(outer)
    def _():
        score_chunk(0, member, both)
        for d in (1, 3, 2):
            score_chunk(d, keys_from(d), both)

    @pl.when(inner)
    def _():
        for slot in (1, 2):
            wait(qrecv.at[slot], qrecv_sem.at[slot])
        for slot in (1, 2):
            place_queries(slot)
        score_chunk(0, member, full)
        for d in (1, 2, 3):
            keys_from(d)
        for d in (1, 2, 3):
            score_chunk(d, sender(d), full)

    def fold(op, value):
        return op(op(value, axis=0), axis=0, keepdims=True)

    tops_e, tops_s = stats_ref[0], stats_ref[2]
    m_e, m_s = fold(jnp.max, tops_e), fold(jnp.max, tops_s)
    f_e = jnp.exp2((tops_e - m_e) * power_scale)
    f_s = jnp.exp2((tops_s - m_s) * power_scale)
    stats = (
        m_e, fold(jnp.sum, stats_ref[1] * f_e),
        m_s, fold(jnp.sum, stats_ref[3] * f_s),
        fold(jnp.sum, stats_ref[4] * (f_e * f_e)),
        fold(jnp.sum, stats_ref[5] * (f_e * f_s)),
    )
    packed = jnp.concatenate(stats + (jnp.zeros((2, width), F32),), axis=0)
    span = width - 3 * head
    tails = packed[:, head:head + span]
    st_send[:, :head] = jnp.where(inner, packed[:, blocks[2]:blocks[2] + head], packed[:, :head])
    st_send[:, head:] = jnp.where(
        inner, pltpu.roll(tails, span - 2 * tail, 1), pltpu.roll(tails, 2 * tail, 1)
    )
    stat_copy = pltpu.make_async_remote_copy(
        src_ref=st_send, dst_ref=st_recv, send_sem=st_sems.at[0], recv_sem=st_sems.at[1],
        device_id=dev(1 - group, member, other),
    )
    side_copy = pltpu.make_async_remote_copy(
        src_ref=st_side, dst_ref=st_turn, send_sem=side_sems.at[0], recv_sem=side_sems.at[1],
        device_id={"ctx": target * 2 + other},
    )

    @pl.when(inner)
    def _():
        st_side[:, :head] = packed[:, blocks[1]:]
        st_side[:, head:2 * head] = packed[:, :head]
        tail_lane = lax.broadcasted_iota(jnp.int32, (8, span), 1)
        st_side[:, 2 * head:] = jnp.where(
            tail_lane < tail, pltpu.roll(tails, span - tail, 1), pltpu.roll(tails, tail, 1)
        )
        side_copy.start()

    stat_copy.start()

    def turn_keys(d, carry):
        m = sender(d)
        kturn[d] = krecv[m, 1, 0:pair_rows].astype(F32).T.astype(BF16)
        return carry

    each(members, turn_keys, 0)

    @pl.when(inner)
    def _():
        side_copy.wait_recv()

    stat_copy.wait_recv()
    there, turned = st_recv[...], st_turn[...]
    tail_lane = lax.broadcasted_iota(jnp.int32, (8, span), 1)
    second = jnp.concatenate([
        jnp.where(inner, turned[:, :head], there[:, :head]),
        jnp.where(inner & (tail_lane < 2 * tail), turned[:, 2 * head:], there[:, head:]),
        there[:, :head],
        turned[:, head:2 * head],
    ], axis=1)
    m_e1, l_e1, m_s1, l_s1, sq1, cr1 = stats
    m_e2, l_e2, m_s2, l_s2, sq2, cr2 = (second[i:i + 1] for i in range(6))
    m_e, m_s = jnp.maximum(m_e1, m_e2), jnp.maximum(m_s1, m_s2)
    fe1, fe2 = jnp.exp2((m_e1 - m_e) * power_scale), jnp.exp2((m_e2 - m_e) * power_scale)
    fs1, fs2 = jnp.exp2((m_s1 - m_s) * power_scale), jnp.exp2((m_s2 - m_s) * power_scale)
    inv_e = 1.0 / (l_e1 * fe1 + l_e2 * fe2)
    inv_s = 1.0 / (l_s1 * fs1 + l_s2 * fs2)
    sq = sq1 * fe1 * fe1 + sq2 * fe2 * fe2
    cr = cr1 * fe1 * fs1 + cr2 * fe2 * fs2
    stats_ref[1] = jnp.where(live, f_e * (fe1 * inv_e), 0.0)
    stats_ref[3] = jnp.where(live, f_s * (fs1 * inv_s), 0.0)
    delta = jnp.where(live, row_weight * (sq * inv_e * inv_e - cr * inv_e * inv_s), 0.0)

    def kg_copy(m, c, sem):
        return pltpu.make_async_remote_copy(
            src_ref=kg_send.at[m, c], dst_ref=kg_recv.at[member, core],
            send_sem=sem, recv_sem=kgrecv_sem.at[member],
            device_id=dev(group, m, c),
        )

    def qg_copy(slot, c):
        return pltpu.make_async_remote_copy(
            src_ref=qg_send.at[slot, c], dst_ref=qg_recv.at[1 if slot else 0, core],
            send_sem=gfar_sem.at[0] if slot else gnear_sem.at[0],
            recv_sem=qgrecv_sem.at[1 if slot else 0],
            device_id=(dev(group, member, c), {"ctx": target * 2 + c}, dev(1 - group, member, c))[slot],
        )

    q_edit = qcat[1]

    def grad_chunk(d):
        prob_e = e_buf[d] * stats_ref[1, d][None]
        prob_s = s_buf[d] * stats_ref[3, d][None]
        grad = prob_e * (row_weight[None] * (prob_e - prob_s) - delta[None])
        grad = grad.reshape(pair_rows, width).astype(BF16)
        grad_buf[d] = grad
        return jnp.dot(grad, q_edit, preferred_element_type=F32) * scale

    def far_grad(i, carry):
        d = (2, 3, 1)[i] if members == 4 else members - 1 - i
        m = sender(d)
        k_part = grad_chunk(d)
        for c in (0, 1):
            kg_send[m, c] = k_part[c * rows:(c + 1) * rows].astype(BF16)
        for c in (0, 1):
            kg_copy(m, c, kgsend_sem.at[0]).start()
        return carry

    each(members - 1, far_grad, 0)
    k_part = grad_chunk(0)
    for c in (0, 1):
        kg_own[c] = k_part[c * rows:(c + 1) * rows]
        kg_send[member, c] = k_part[c * rows:(c + 1) * rows].astype(BF16)

    q_total = each(
        members,
        lambda d, q: q + jnp.dot(kturn[d], grad_buf[d], preferred_element_type=F32),
        jnp.zeros((HEAD_DIM, width), F32),
    )
    q_rows = q_total.T * scale
    for slot in (2, 1, 0):
        joined = [q_rows[blocks[slot]:blocks[slot] + head]]
        if tail:
            at = head + slot * tail
            joined.append(q_rows[at:at + tail])
        joined = jnp.concatenate(joined, axis=0)
        for c in (0, 1):
            part = joined[c * rows:(c + 1) * rows]
            if not slot:
                qg_own[c] = part
            qg_send[slot, c] = part.astype(BF16)

    @pl.when(inner)
    def _():
        for slot in (2, 1):
            for c in (0, 1):
                qg_copy(slot, c).start()

    qg_copy(0, other).start()
    kg_copy(member, other, gnear_sem.at[0]).start()

    def put(ref, mine, theirs):
        ref[:, own_cols] = mine
        ref[:, other_cols] = theirs

    wait(kg_recv.at[member, 0], kgrecv_sem.at[member])

    def add_far(d, sums):
        mine, theirs = sums
        m = shifted(d + 1)
        wait(kg_recv.at[m], kgrecv_sem.at[m])
        return mine + kg_recv[m, core].astype(F32), theirs + kg_recv[m, other].astype(F32)

    sums = each(members - 1, add_far, (kg_own[core], kg_recv[member, other].astype(F32)))
    put(kg_ref, *sums)

    wait(qg_recv.at[0, 0], qgrecv_sem.at[0])
    wait(qg_recv.at[1], qgrecv_sem.at[1])
    put(
        qg_ref,
        qg_own[core] + qg_recv[1, other].astype(F32),
        qg_recv[0, other].astype(F32) + qg_recv[1, core].astype(F32),
    )

    wait(chips_keys(slice(0, members - 1)), ksend_sem.at[0])
    wait(qrecv.at[0:2], near_sem.at[0])
    stat_copy.wait_send()
    wait(kg_send.at[0:members - 1], kgsend_sem.at[0])
    wait(qg_send.at[0], gnear_sem.at[0])

    @pl.when(inner)
    def _():
        wait(qg_send.at[1:3], gfar_sem.at[0])
        side_copy.wait_send()


def put_out(qg_vmem, kg_vmem, qg_hbm, kg_hbm, sems):
    copies = (
        pltpu.make_async_copy(qg_vmem, qg_hbm, sems.at[0]),
        pltpu.make_async_copy(kg_vmem, kg_hbm, sems.at[1]),
    )
    for copy in copies:
        copy.start()
    for copy in copies:
        copy.wait()


def solution(mesh):
    chips = mesh.shape["ctx"] // 2
    members = chips // 2

    def local(query_source, key_source, query_edit, key_edit, text_count):
        rows, full = query_source.shape
        width = 4 * rows
        groups = 2 * rows // 8
        dma = pltpu.SemaphoreType.DMA
        vmem = pltpu.VMEM
        in_line = chips == 8
        if in_line:
            pair = 2 * rows
            head = pair // 128 * 128
            width = 3 * head + -(-3 * (pair - head) // 128) * 128
        slots = 3 if in_line else 2
        stat = vmem((8, width - 2 * head if in_line else width), F32)
        side = [vmem((8, width - head), F32)] * 2 if in_line else []
        grads = pl.pallas_call(
            functools.partial(line_kernel if in_line else kernel, chips),
            out_shape=(
                pltpu.VMEM((rows, full), F32),
                pltpu.VMEM((rows, full), F32),
            ),
            in_specs=[pl.BlockSpec(memory_space=pltpu.HBM)] * 5,
            out_specs=(pl.BlockSpec(memory_space=pltpu.VMEM),) * 2,
            scratch_shapes=[
                pltpu.SMEM((1,), jnp.int32),
                vmem((members, 2, 2 * rows + 8, HEAD_DIM), BF16),
                vmem((2, rows, HEAD_DIM), BF16),
                vmem((slots, 2, 2, rows, HEAD_DIM), BF16),
                vmem((2, rows, HEAD_DIM), BF16),
                vmem((2, width, HEAD_DIM), BF16),
                vmem((members, HEAD_DIM, 2 * rows), BF16),
                vmem((members, groups, 8, 128), F32),
                vmem((members, 2 * rows, width), BF16),
                vmem((members, groups, 8, width), F32),
                vmem((members, groups, 8, width), F32),
                vmem((6, members, 8, width), F32),
                stat,
                stat,
                *side,
                vmem((members, 2, rows, HEAD_DIM), BF16),
                vmem((members, 2, rows, HEAD_DIM), BF16),
                vmem((slots, 2, rows, HEAD_DIM), BF16),
                vmem((2, 2, rows, HEAD_DIM), BF16),
                vmem((2, rows, HEAD_DIM), F32),
                vmem((2, rows, HEAD_DIM), F32),
                dma((2,)),
                dma((1,)),
                dma((1,)),
                dma((members,)),
                dma((slots,)),
                dma((2,)),
                *([dma((2,))] if in_line else []),
                dma((1,)),
                dma((1,)),
                *([dma((1,))] if in_line else []),
                dma((members,)),
                dma((2,)),
            ],
            compiler_params=pltpu.CompilerParams(collective_id=0, has_side_effects=True),
        )(text_count, query_source, key_source, query_edit, key_edit)
        return pl.pallas_call(
            put_out,
            out_shape=(pltpu.HBM((rows, full), F32),) * 2,
            in_specs=[pl.BlockSpec(memory_space=pltpu.VMEM)] * 2,
            out_specs=(pl.BlockSpec(memory_space=pltpu.HBM),) * 2,
            scratch_shapes=[dma((2,))],
        )(*(pltpu.with_memory_space_constraint(g, pltpu.VMEM) for g in grads))

    spec = P(("req", "ctx"), None)
    return jax.shard_map(
        local, mesh=mesh, in_specs=(spec,) * 4 + (P("req"),), out_specs=(spec, spec), check_vma=False
    )
```
